32 devices in a mesh: row: 8 (over z, y), col: 4 (over x, core).
Axes of the slice: x: 2, y: 2, z: 4, core: 2. Of those that a mesh axis runs over, the one named last changes fastest.
Arguments:
- stack_embedding: bfloat16 [64, 160, 256], P('row', 'col'), may hold values from -6 to 6
- pair_representation: bfloat16 [160, 160, 128], P('row', 'col'), may hold values from -8 to 8
- mixing_entry_coefficients: bfloat16 [256, 1024], replicated, may hold values from -0.375 to 0.375
- mixing_final_coefficients: bfloat16 [256, 256], replicated, may hold values from -1 to 1
- pair_bias_matrix: bfloat16 [128, 8], replicated, may hold values from -4 to 4
- tensor_side_coefficients: bfloat16 [256, 64], replicated, may hold values from -0.375 to 0.375
- outer_output_weight: bfloat16 [1024, 128], replicated, may hold values from -1 to 1
- triangle_projection_weight: bfloat16 [128, 640], replicated, may hold values from -0.5 to 0.5
- triangle_output_weight: bfloat16 [128, 128], replicated, may hold values from -0.5 to 0.5
Outputs:
- stack_embedding_updated: bfloat16 [64, 160, 256], P('row', 'col')
- pair_state_next: bfloat16 [160, 160, 128], P('row', 'col')
The draws below stay inside these ranges and needn't reach their ends.
All inputs are finite; a program needn't handle non-finite values.
Results may differ from the reference program's by a relative error of at most 0.015.
Values may be sent and summed in bfloat16 or wider, within the bound.
No kernel may reach another device: no remote copies, remote signals or barrier semaphores. Data moves between devices by JAX's collectives and lax.ppermute only.
A program may use at most 128 MiB of HBM per device.

```python
import jax
import jax.numpy as jnp
from jax import lax

STACK_FEATURES = 256
C_Z = 128
FOCUS_GROUPS = 8
PRODUCT_FACTORS = 32
FEATURE_WIDTH = 32
CHAIN_TOTAL = 64
POSITION_TOTAL = 160
ROWS_DEV = 20


def bias_table(draw_key):
    table_key = jax.random.fold_in(draw_key, 101)
    return jnp.clip(jax.random.normal(table_key, (C_Z, FOCUS_GROUPS), jnp.float32) * (2.0 * C_Z ** (-0.5)), -4.0, 4.0)


def draw_pair_bias_matrix(draw_key, part):
    return bias_table(draw_key).astype(jnp.bfloat16)


def draw_pair_representation(draw_key, part):
    noise_key = jax.random.fold_in(draw_key, 202)
    field = jax.random.normal(noise_key, (POSITION_TOTAL, POSITION_TOTAL, C_Z), jnp.float32)
    return jnp.clip(field, -8.0, 8.0).astype(jnp.bfloat16)


def block_scale(key, dims, split, smallest, high):
    factor_of, own = 1.0, jax.random.fold_in(key, 6)
    for dim, parts in split:
        steps = jnp.exp(jax.random.uniform(jax.random.fold_in(own, dim), (parts,), jnp.float32, smallest / len(split), high / len(split)))
        factor_of = factor_of * jnp.repeat(steps, dims[dim] // parts).reshape([-1 if axis == dim else 1 for axis in range(len(dims))])
    return factor_of


def gaussian(key, shape, deviation, bound, pieces=(), held_as=jnp.bfloat16):
    result = jax.random.normal(key, shape, jnp.float32) * deviation
    if len(pieces) > 0:
        result = block_scale(key, shape, pieces, -0.22, 0.18) * result
    return jnp.clip(result, min=-bound, max=bound).astype(held_as)


def setup_inputs(seed: int = 0) -> dict:
    key_list = jax.random.split(jax.random.key(seed), 10)
    stack_embedding = gaussian(key_list[0], (CHAIN_TOTAL, POSITION_TOTAL, STACK_FEATURES), 1.0, 6.0, ((0, 8), (1, 4)))
    pair_representation = draw_pair_representation(jax.random.fold_in(key_list[9], 71), 0)
    mixing_entry_coefficients = gaussian(key_list[2], (STACK_FEATURES, 4 * STACK_FEATURES), STACK_FEATURES ** -0.5, 0.375)
    mixing_final_coefficients = gaussian(key_list[3], (STACK_FEATURES, STACK_FEATURES), (STACK_FEATURES // 8) ** -0.5, 1.0)
    pair_bias_matrix = draw_pair_bias_matrix(jax.random.fold_in(key_list[9], 71), 0)
    tensor_side_coefficients = gaussian(key_list[5], (STACK_FEATURES, 2 * PRODUCT_FACTORS), STACK_FEATURES ** -0.5, 0.375)
    outer_output_weight = gaussian(key_list[6], (PRODUCT_FACTORS * PRODUCT_FACTORS, C_Z), PRODUCT_FACTORS ** -0.5, 1.0)
    triangle_projection_weight = gaussian(key_list[7], (C_Z, 5 * C_Z), C_Z ** -0.5, 0.5)
    triangle_output_weight = gaussian(key_list[8], (C_Z, C_Z), C_Z ** -0.5, 0.5)
    return dict(stack_embedding=stack_embedding, pair_representation=pair_representation, mixing_entry_coefficients=mixing_entry_coefficients, mixing_final_coefficients=mixing_final_coefficients, pair_bias_matrix=pair_bias_matrix, tensor_side_coefficients=tensor_side_coefficients, outer_output_weight=outer_output_weight, triangle_projection_weight=triangle_projection_weight, triangle_output_weight=triangle_output_weight)


epsilon = 1e-05

def standardize_features(inputs):
    inputs = inputs.astype(jnp.float32)
    center = inputs - lax.optimization_barrier(jnp.mean(inputs, axis=-1, keepdims=True))
    spread = lax.optimization_barrier(jnp.mean(center * center, axis=-1, keepdims=True))
    return center * lax.rsqrt(spread + epsilon)

def reference(stack_embedding, pair_representation, mixing_entry_coefficients, mixing_final_coefficients, pair_bias_matrix, tensor_side_coefficients, outer_output_weight, triangle_projection_weight, triangle_output_weight):
    stack_standardized = standardize_features(stack_embedding).astype(jnp.bfloat16).reshape(-1, STACK_FEATURES)
    mapped_lines = jnp.dot(stack_standardized, mixing_entry_coefficients, preferred_element_type=jnp.float32)
    stack_probe_vectors = (mapped_lines[:, :STACK_FEATURES] * FEATURE_WIDTH ** (-0.5)).astype(jnp.bfloat16).reshape(CHAIN_TOTAL, POSITION_TOTAL, FOCUS_GROUPS, FEATURE_WIDTH)
    stack_lookup_vectors = mapped_lines[:, STACK_FEATURES:2 * STACK_FEATURES].astype(jnp.bfloat16).reshape(CHAIN_TOTAL, POSITION_TOTAL, FOCUS_GROUPS, FEATURE_WIDTH)
    stack_content_vectors = mapped_lines[:, 2 * STACK_FEATURES:3 * STACK_FEATURES].astype(jnp.bfloat16).reshape(CHAIN_TOTAL, POSITION_TOTAL, FOCUS_GROUPS, FEATURE_WIDTH)
    sigmoid_factors = jax.nn.sigmoid(mapped_lines[:, 3 * STACK_FEATURES:]).reshape(CHAIN_TOTAL, POSITION_TOTAL, STACK_FEATURES)
    pair_normed = standardize_features(pair_representation).astype(jnp.bfloat16)
    pair_bias = jnp.einsum('ijc,ch->hij', pair_normed.astype(jnp.float32), pair_bias_matrix.astype(jnp.float32))
    pair_bias = lax.optimization_barrier(pair_bias.astype(jnp.bfloat16)).astype(jnp.float32)

    def lone_chain_lines(sequence_items):
        seq_query, seq_keys, seq_values = sequence_items
        scores = jnp.einsum('ihd,jhd->hij', seq_query.astype(jnp.float32), seq_keys.astype(jnp.float32)) + pair_bias
        row_peak = lax.optimization_barrier(jnp.max(scores, axis=-1, keepdims=True))
        exponent = jnp.exp(scores - row_peak)
        row_total = lax.optimization_barrier(jnp.sum(exponent, axis=-1))
        probs = lax.optimization_barrier(exponent.astype(jnp.bfloat16)).astype(jnp.float32)
        blended = jnp.einsum('hij,jhd->ihd', probs, seq_values.astype(jnp.float32))
        return blended / jnp.transpose(row_total)[..., None]
    weighted_mixture = lax.map(lone_chain_lines, (stack_probe_vectors, stack_lookup_vectors, stack_content_vectors)).reshape(CHAIN_TOTAL, POSITION_TOTAL, STACK_FEATURES)
    scaled_mixture = (sigmoid_factors * weighted_mixture).astype(jnp.bfloat16)
    stack_increment = jnp.dot(scaled_mixture.reshape(-1, STACK_FEATURES), mixing_final_coefficients, preferred_element_type=jnp.float32).reshape(CHAIN_TOTAL, POSITION_TOTAL, STACK_FEATURES)
    stack_embedding_updated = (stack_embedding.astype(jnp.float32) + stack_increment).astype(jnp.bfloat16)
    tensor_standardized = standardize_features(stack_embedding_updated).astype(jnp.bfloat16).reshape(-1, STACK_FEATURES)
    sides = jnp.dot(tensor_standardized, tensor_side_coefficients, preferred_element_type=jnp.float32).astype(jnp.bfloat16)
    sides = sides.reshape(CHAIN_TOTAL, POSITION_TOTAL, 2 * PRODUCT_FACTORS)
    left_side = sides[..., :PRODUCT_FACTORS]
    right_side = sides[..., PRODUCT_FACTORS:]
    left_blocks = jnp.transpose(left_side.reshape(CHAIN_TOTAL, POSITION_TOTAL // ROWS_DEV, ROWS_DEV, PRODUCT_FACTORS), (1, 0, 2, 3))

    def outer_block(left_block):
        products = jnp.einsum('sic,sjd->ijcd', left_block.astype(jnp.float32), right_side.astype(jnp.float32))
        averaged = (products * (1.0 / CHAIN_TOTAL)).astype(jnp.bfloat16)
        return jnp.dot(averaged.reshape(-1, PRODUCT_FACTORS * PRODUCT_FACTORS), outer_output_weight, preferred_element_type=jnp.float32).reshape(ROWS_DEV, POSITION_TOTAL, C_Z)
    outer_update = lax.map(outer_block, left_blocks).reshape(POSITION_TOTAL, POSITION_TOTAL, C_Z)
    pair_mid = (pair_representation.astype(jnp.float32) + outer_update).astype(jnp.bfloat16)
    tri_normed = standardize_features(pair_mid).astype(jnp.bfloat16).reshape(-1, C_Z)

    def project(block_index):
        columns = triangle_projection_weight[:, block_index * C_Z:(block_index + 1) * C_Z]
        return jnp.dot(tri_normed, columns, preferred_element_type=jnp.float32).reshape(POSITION_TOTAL, POSITION_TOTAL, C_Z)
    left_edge = (jax.nn.sigmoid(project(1)) * project(0)).astype(jnp.bfloat16)
    right_edge = (jax.nn.sigmoid(project(3)) * project(2)).astype(jnp.bfloat16)
    out_gate = jax.nn.sigmoid(project(4))
    summed = jnp.einsum('ikc,jkc->ijc', left_edge.astype(jnp.float32), right_edge.astype(jnp.float32))
    tri_ln = standardize_features(summed).astype(jnp.bfloat16)
    tri_update = jnp.dot(tri_ln.reshape(-1, C_Z), triangle_output_weight, preferred_element_type=jnp.float32).reshape(POSITION_TOTAL, POSITION_TOTAL, C_Z)
    pair_state_next = (pair_mid.astype(jnp.float32) + out_gate * tri_update).astype(jnp.bfloat16)
    return (stack_embedding_updated, pair_state_next)
```

```python
import functools

import jax
import jax.numpy as jnp
import numpy as np
from jax import lax
from jax.experimental import pallas as pl
from jax.experimental.pallas import tpu as pltpu
from jax.sharding import PartitionSpec as P

epsilon = 1e-05
LANES = 128
SUBLANES = 8
F32 = jnp.float32
BF16 = jnp.bfloat16
ALL = ("row", "col")
NT = (((1,), (1,)), ((), ()))
VMEM = pl.BlockSpec(memory_space=pltpu.VMEM)
SMEM = pl.BlockSpec(memory_space=pltpu.SMEM)


def standardize_features(inputs, axis=-1):
    inputs = inputs.astype(jnp.float32)
    center = inputs - jnp.mean(inputs, axis=axis, keepdims=True)
    spread = jnp.mean(center * center, axis=axis, keepdims=True)
    return center * lax.rsqrt(spread + epsilon)


def dot(a, b):
    return jnp.dot(a, b, preferred_element_type=F32)


def dot_nt(a, b):
    return lax.dot_general(a, b, NT, preferred_element_type=F32)


def lane_iota(rows):
    return lax.broadcasted_iota(jnp.int32, (rows, LANES), 1)


def call(body, out_shape, scratch, in_specs, name):
    return pl.pallas_call(
        body,
        out_shape=out_shape,
        in_specs=in_specs,
        out_specs=jax.tree.map(lambda _: VMEM, out_shape),
        scratch_shapes=scratch,
        name=name,
        compiler_params=pltpu.CompilerParams(vmem_limit_bytes=40 * 1024 * 1024),
    )


class Plan:
    def __init__(self, n_row, n_col, x, pair, heads, outer, channels_out):
        self.n_row, self.n_col, self.n = n_row, n_col, n_row * n_col
        self.seqs, self.res, self.feat = x
        self.rows, self.cols, self.width = pair
        self.heads, self.outer = heads, outer
        self.hd = self.feat // heads
        self.total = self.res * n_col
        self.ok = False
        if self.seqs % n_col or self.width != LANES or heads != SUBLANES or self.cols != self.res:
            return
        if self.rows * n_row != self.total or self.feat % LANES:
            return
        self.own = self.seqs // n_col
        self.seq_total = self.own * self.n
        self.i_main = LANES // heads
        self.i_rem = self.rows - self.i_main
        if not 0 < self.i_rem or LANES % (self.i_rem * heads) or self.cols % SUBLANES:
            return
        self.rem = self.i_rem * heads
        self.fold = LANES // self.rem
        if n_row % self.fold:
            return
        self.groups = self.cols // SUBLANES
        self.rem_rows = -(-self.groups // self.fold)
        self.bias_rows = self.cols + SUBLANES * self.rem_rows
        if LANES % outer:
            return
        self.pack = LANES // outer
        if self.rows % self.pack or self.cols % self.pack:
            return
        self.lk, self.rk = self.rows // self.pack, self.cols // self.pack
        used = (self.lk + self.rk) * self.own
        self.side_rows = -(-used // 16) * 16
        self.cpad = -(-self.cols // 16) * 16
        if self.width % self.n:
            return
        self.ch = self.width // self.n
        if 2 * self.ch != SUBLANES or n_row % n_col:
            return
        self.q = LANES // self.cols
        self.ig = -(-self.rows // self.q)
        self.ipad = self.ig * self.q
        self.per = n_row // n_col
        self.jslot = self.per * self.ipad
        if self.per * self.rows != self.cols or self.q * self.jslot > LANES:
            return
        self.m = n_row * self.ig
        self.edge_rows = self.ig * SUBLANES
        self.back_rows = -(-self.ig * self.ch // 16) * 16
        self.ok = True

    def j_base(self, c):
        return (c // self.q) * LANES + (c % self.q) * self.jslot


def bias_kernel(p, pair_ref, w_ref, out_ref):
    normed = standardize_features(pair_ref[...])
    heads = p.heads
    spread = (lax.broadcasted_iota(jnp.int32, (heads, LANES), 1) % heads
              == lax.broadcasted_iota(jnp.int32, (heads, LANES), 0))
    tiled = dot(w_ref[...], jnp.where(spread, 1.0, 0.0).astype(BF16))
    slot = lane_iota(p.width) // heads
    main = jnp.zeros((p.cols, LANES), F32)
    rem = jnp.zeros((p.cols, LANES), F32)
    for i in range(p.rows):
        block = normed[i * p.cols:(i + 1) * p.cols].astype(BF16)
        if i < p.i_main:
            main += dot(block, jnp.where(slot == i, tiled, 0.0).astype(BF16))
        else:
            rem += dot(block, jnp.where(slot % p.i_rem == i - p.i_main, tiled, 0.0).astype(BF16))
    piece = [main]
    at = lane_iota(SUBLANES) // p.rem
    for k in range(p.rem_rows):
        folded = jnp.zeros((SUBLANES, LANES), F32)
        for f in range(p.fold):
            g = k * p.fold + f
            if g < p.groups:
                folded = jnp.where(at == f, rem[g * SUBLANES:(g + 1) * SUBLANES], folded)
        piece.append(folded)
    piece = jnp.concatenate(piece, axis=0).astype(BF16)
    for d in range(p.n):
        out_ref[d] = piece


def project_kernel(p, col_ref, *refs):
    x_refs = refs[:p.n_col]
    w_ref, q_ref, k_ref, v_ref, gate_ref, x_out, hold = refs[p.n_col:]
    me = col_ref[0]
    for shift in range(p.n_col):
        hold[lax.rem(me + (p.n_col - shift), p.n_col)] = x_refs[shift][...].astype(F32)
    f = p.feat
    for s in range(p.own):
        x = jnp.concatenate([hold[c, s] for c in range(p.n_col)], axis=0)
        x_out[s] = x
        lines = dot(standardize_features(x).astype(BF16), w_ref[...])
        q_ref[s] = (lines[:, :f] * p.hd ** (-0.5)).astype(BF16)
        k_ref[s] = lines[:, f:2 * f].astype(BF16)
        v_ref[s] = lines[:, 2 * f:3 * f].astype(BF16)
        gate_ref[s] = jax.nn.sigmoid(lines[:, 3 * f:])


def attend_kernel(p, q_ref, k_ref, v_ref, gate_ref, x_ref, bias_ref, sel_ref, wf_ref, wl_ref, wr_ref,
                  emb_ref, side_ref, bias, l4, r4, lint, rint, send):
    h, t, f = p.heads, p.total, p.feat
    main = p.n_row * LANES
    for r in range(p.n_row):
        for c in range(p.n_col):
            bias[c * p.cols:(c + 1) * p.cols, r * LANES:(r + 1) * LANES] = (
                bias_ref[r * p.n_col + c, 0:p.cols].astype(F32))
    at = lane_iota(SUBLANES) // p.rem
    for c in range(p.n_col):
        for b in range(p.n_row // p.fold):
            tails = [bias_ref[(b * p.fold + u) * p.n_col + c, p.cols:p.bias_rows].astype(F32)
                     for u in range(p.fold)]
            for g in range(p.groups):
                k, part = g // p.fold, g % p.fold
                block = jnp.zeros((SUBLANES, LANES), F32)
                for u in range(p.fold):
                    piece = tails[u][k * SUBLANES:(k + 1) * SUBLANES]
                    turn = ((u - part) * p.rem) % LANES
                    if turn:
                        piece = pltpu.roll(piece, turn, axis=1)
                    block = jnp.where(at == u, piece, block)
                bias[c * p.cols + g * SUBLANES:c * p.cols + (g + 1) * SUBLANES,
                     main + b * LANES:main + (b + 1) * LANES] = block
    head_of = (lax.broadcasted_iota(jnp.int32, (h, f), 1) // p.hd
               == lax.broadcasted_iota(jnp.int32, (h, f), 0))
    head_mask = jnp.where(head_of, 1.0, 0.0)
    wide = t * h
    own_head = (lax.broadcasted_iota(jnp.int32, (f, wide), 0) // p.hd
                == lax.broadcasted_iota(jnp.int32, (f, wide), 1) % h)
    lane = lane_iota(t // p.pack) // p.outer
    for s in range(p.own):
        q = q_ref[s].astype(F32)
        spread = jnp.broadcast_to(q[:, None, :], (t, h, f)) * head_mask[None]
        parts = [spread[r * p.rows:r * p.rows + p.i_main] for r in range(p.n_row)]
        parts += [spread[r * p.rows + p.i_main:(r + 1) * p.rows] for r in range(p.n_row)]
        spread = jnp.concatenate(parts, axis=0).reshape(wide, f).astype(BF16)
        scores = dot_nt(k_ref[s], spread) + bias[...]
        peak = jnp.max(scores, axis=0, keepdims=True)
        weights = jnp.exp(scores - peak)
        total = jnp.sum(weights, axis=0, keepdims=True)
        v_t = jnp.transpose(v_ref[s].astype(F32)).astype(BF16)
        mixed = dot(v_t, weights.astype(BF16)) * (1.0 / total)
        mixed = jnp.where(own_head, mixed, 0.0).astype(BF16)
        attended = dot_nt(sel_ref[...], mixed)
        gated = (gate_ref[s] * attended).astype(BF16)
        new = (x_ref[s] + dot(gated, wf_ref[...])).astype(BF16).astype(F32)
        for c in range(p.n_col):
            emb_ref[c, s] = new[c * p.res:(c + 1) * p.res].astype(BF16)
        normed = standardize_features(new).astype(BF16)
        for w_ref, four, woven in ((wl_ref, l4, lint), (wr_ref, r4, rint)):
            four[...] = dot(normed, w_ref[...])
            packed = four[pl.ds(0, t // p.pack, stride=p.pack), :]
            for a in range(1, p.pack):
                packed = jnp.where(lane == a, four[pl.ds(a, t // p.pack, stride=p.pack), :], packed)
            woven[pl.ds(s, t // p.pack, stride=p.own), :] = packed
    nr, nl = p.rk * p.own, p.lk * p.own
    for r in range(p.n_row):
        for c in range(p.n_col):
            d = r * p.n_col + c
            send[d, 0:nr] = rint[c * nr:(c + 1) * nr]
            send[d, nr:nr + nl] = lint[r * nl:(r + 1) * nl]
            if nr + nl < p.side_rows:
                send[d, nr + nl:p.side_rows] = jnp.zeros((p.side_rows - nr - nl, LANES), F32)
    side_ref[...] = send[...].astype(BF16)


def outer_kernel(p, recv_ref, pair_ref, wbd_ref, wv_ref, wg_ref, mid_ref, edge_ref,
                 flat, rt, lhs, mid):
    flat[...] = recv_ref[...].reshape(p.n * p.side_rows, LANES).astype(F32)

    def chunk(k):
        return jnp.concatenate(
            [flat[pl.ds(k * p.own + s, p.n, stride=p.side_rows), :] for s in range(p.own)], axis=0)

    left = jnp.concatenate([chunk(p.rk + k) for k in range(p.lk)], axis=1).astype(BF16)
    for k in range(p.rk):
        rt[k * LANES:(k + 1) * LANES, :] = jnp.transpose(chunk(k))
    right = jnp.concatenate(
        [rt[pl.ds(d, p.cols, stride=p.outer), :] for d in range(p.outer)], axis=0).astype(BF16)
    products = dot(right, left) * (1.0 / p.seq_total)
    for d in range(p.outer):
        for g in range(p.lk):
            lhs[g * p.cpad:g * p.cpad + p.cols, d * LANES:(d + 1) * LANES] = products[
                d * p.cols:(d + 1) * p.cols, g * LANES:(g + 1) * LANES].astype(BF16)
            if p.cpad > p.cols:
                lhs[g * p.cpad + p.cols:(g + 1) * p.cpad, d * LANES:(d + 1) * LANES] = jnp.zeros(
                    (p.cpad - p.cols, LANES), BF16)
    update = dot(lhs[...], wbd_ref[...])
    for i in range(p.rows):
        g, a = i // p.pack, i % p.pack
        fresh = (pair_ref[i].astype(F32)
                 + update[g * p.cpad:g * p.cpad + p.cols, a * p.width:(a + 1) * p.width]).astype(BF16)
        mid_ref[i] = fresh
        mid[i * p.cols:(i + 1) * p.cols, :] = fresh.astype(F32)
    tail = mid.shape[0] - p.rows * p.cols
    mid[p.rows * p.cols:, :] = jnp.zeros((tail, LANES), F32)
    step = p.q * p.cols
    for k in range(p.ig):
        normed = standardize_features(mid[k * step:k * step + LANES, :]).astype(BF16)
        value = dot_nt(wv_ref[...], normed)
        gate = jax.nn.sigmoid(dot_nt(wg_ref[...], normed))
        edge_ref[:, k * SUBLANES:(k + 1) * SUBLANES, :] = (gate * value).reshape(
            p.n, SUBLANES, LANES).astype(BF16)


def gate_kernel(p, mid_ref, w_ref, out_ref):
    normed = standardize_features(mid_ref[...]).reshape(p.rows * p.cols, p.width).astype(BF16)
    out_ref[...] = jax.nn.sigmoid(dot(normed, w_ref[...]))


def triangle_kernel(p, recv_ref, out_ref, flat, ls, rs, os, sb):
    for r in range(p.n_row):
        for c in range(p.n_col):
            flat[c, r * p.edge_rows:(r + 1) * p.edge_rows, :] = recv_ref[r * p.n_col + c].astype(F32)
    lane = lane_iota(p.m)
    blocks = p.per * p.ig
    rs[...] = jnp.zeros_like(rs)
    for ch in range(p.ch):
        for c in range(p.n_col):
            left = flat[c, pl.ds(ch, p.m, stride=SUBLANES), :]
            right = flat[c, pl.ds(p.ch + ch, p.m, stride=SUBLANES), :]
            for a in range(p.q):
                turn = (-a * p.cols) % LANES
                lt = pltpu.roll(left, turn, axis=1) if turn else left
                rt = pltpu.roll(right, turn, axis=1) if turn else right
                ls[ch, c, pl.ds(a, p.m, stride=p.q), :] = jnp.where(lane < p.cols, lt, 0.0)
                for first in range(0, p.n_col, p.q):
                    many = min(p.q, p.n_col - first) * blocks
                    rs[ch, c, pl.ds(p.j_base(first) + a, many, stride=p.q), :] = rt[
                        first * blocks:first * blocks + many]
    for ch in range(p.ch):
        lfull = jnp.concatenate([ls[ch, c] for c in range(p.n_col)], axis=1).astype(BF16)
        rfull = jnp.concatenate([rs[ch, c] for c in range(p.n_col)], axis=1).astype(BF16)
        summed = dot_nt(lfull, rfull)
        for b in range(summed.shape[1] // LANES):
            os[ch, b] = summed[:, b * LANES:(b + 1) * LANES]
        rows = [[os[ch, b, pl.ds(a, p.m, stride=p.q), :] for a in range(p.q)]
                for b in range(summed.shape[1] // LANES)]
        for c in range(p.n_col):
            b, part = c // p.q, c % p.q
            packed = None
            for a in range(p.q):
                turn = ((a - part) * p.jslot) % LANES
                piece = pltpu.roll(rows[b][a], turn, axis=1) if turn else rows[b][a]
                packed = piece if packed is None else jnp.where(lane // p.jslot == a, piece, packed)
            sb[c, pl.ds(ch, p.m, stride=p.ch), :] = packed
    used = p.ig * p.ch
    for r in range(p.n_row):
        for c in range(p.n_col):
            d = r * p.n_col + c
            out_ref[d, 0:used] = sb[c, r * used:(r + 1) * used, :].astype(BF16)
            if used < p.back_rows:
                out_ref[d, used:p.back_rows] = jnp.zeros((p.back_rows - used, LANES), BF16)


def final_kernel(p, recv_ref, mid_ref, gate_ref, w_ref, out_ref, flat, hold, update):
    flat[...] = recv_ref[...].reshape(p.n * p.back_rows, LANES).astype(F32)
    for k in range(p.ig):
        summed = jnp.concatenate(
            [flat[pl.ds(k * p.ch + ch, p.n, stride=p.back_rows), :] for ch in range(p.ch)], axis=0)
        normed = jnp.transpose(standardize_features(summed, axis=0)).astype(BF16)
        hold[...] = dot(normed, w_ref[...])
        for a in range(p.q):
            i = k * p.q + a
            if i < p.rows:
                for u in range(p.per):
                    update[i * p.cols + u * p.rows:i * p.cols + (u + 1) * p.rows, :] = hold[
                        a * p.jslot + u * p.ipad:a * p.jslot + u * p.ipad + p.rows, :]
    fresh = mid_ref[...].astype(F32).reshape(p.rows * p.cols, p.width) + gate_ref[...] * update[...]
    out_ref[...] = fresh.reshape(p.rows, p.cols, p.width).astype(BF16)


def fast(p, x, pair, w_in, w_out, w_bias, w_side, w_outer, w_tri, w_last):
    col = lax.axis_index("col")
    n, ch, width = p.n, p.ch, p.width
    sds = jax.ShapeDtypeStruct

    left_w, right_w = w_side[:, :p.outer], w_side[:, p.outer:]
    left_w, right_w = jnp.tile(left_w, (1, p.pack)), jnp.tile(right_w, (1, p.pack))
    by_d = jnp.transpose(w_outer.reshape(p.outer, p.outer, width), (1, 0, 2))
    eye = jnp.eye(p.pack, dtype=bool)
    w_bd = jnp.where(eye[None, :, None, :, None], by_d[:, None, :, None, :], jnp.zeros((), BF16)).reshape(
        p.outer * LANES, p.pack * width)
    blocks = jnp.transpose(w_tri.reshape(width, 5, width), (1, 2, 0)).reshape(5, n, ch, width)
    value_w = jnp.concatenate([blocks[0], blocks[2]], axis=1).reshape(n * 2 * ch, width)
    gate_w = jnp.concatenate([blocks[1], blocks[3]], axis=1).reshape(n * 2 * ch, width)
    own_gate_w = w_tri[:, 4 * width:]
    last_w = jnp.transpose(w_last.reshape(n, ch, width), (1, 0, 2)).reshape(width, width)
    spot = np.arange(p.total).reshape(p.n_row, p.rows)
    order = np.concatenate([spot[:, :p.i_main].reshape(-1), spot[:, p.i_main:].reshape(-1)])
    sel = jnp.asarray((np.arange(p.total)[:, None] == np.repeat(order, p.heads)[None]), BF16)

    piece = call(functools.partial(bias_kernel, p), sds((n, p.bias_rows, LANES), BF16), [], [VMEM] * 2, "bias")(
        pair.reshape(p.rows * p.cols, width), w_bias)
    bias = lax.all_to_all(piece, ALL, 0, 0, tiled=True)
    chunks = x.reshape(p.n_col, p.own, p.res, p.feat)
    parts = []
    for shift in range(p.n_col):
        part = lax.dynamic_index_in_dim(chunks, lax.rem(col + shift, p.n_col), 0, keepdims=False)
        if shift:
            part = lax.ppermute(part, "col", [(c, (c + shift) % p.n_col) for c in range(p.n_col)])
        parts.append(part)
    seq = (p.own, p.total, p.feat)
    q, k, v, gate, whole = call(
        functools.partial(project_kernel, p),
        (sds(seq, BF16), sds(seq, BF16), sds(seq, BF16), sds(seq, F32), sds(seq, F32)),
        [pltpu.VMEM((p.n_col, p.own, p.res, p.feat), F32)],
        [SMEM] + [VMEM] * (p.n_col + 1), "project")(col.reshape(1), *parts, w_in)
    emb, sides = call(
        functools.partial(attend_kernel, p),
        (sds((p.n_col, p.own, p.res, p.feat), BF16), sds((n, p.side_rows, LANES), BF16)),
        [pltpu.VMEM((p.total, p.total * p.heads), F32)]
        + [pltpu.VMEM((p.total, LANES), F32)] * 2
        + [pltpu.VMEM((p.total // p.pack * p.own, LANES), F32)] * 2
        + [pltpu.VMEM((n, p.side_rows, LANES), F32)],
        [VMEM] * 10, "attend")(q, k, v, gate, whole, bias, sel, w_out, left_w, right_w)

    sides = lax.all_to_all(sides, ALL, 0, 0, tiled=True)
    mid, edges = call(
        functools.partial(outer_kernel, p),
        (sds((p.rows, p.cols, width), BF16), sds((n, p.edge_rows, LANES), BF16)),
        [pltpu.VMEM((n * p.side_rows, LANES), F32),
         pltpu.VMEM((p.rk * LANES, p.seq_total), F32),
         pltpu.VMEM((p.lk * p.cpad, p.outer * LANES), BF16),
         pltpu.VMEM(((p.ig - 1) * p.q * p.cols + LANES, LANES), F32)],
        [VMEM] * 5, "outer")(sides, pair, w_bd, value_w, gate_w)

    edges = lax.all_to_all(edges, ALL, 0, 0, tiled=True)
    out_gate = call(functools.partial(gate_kernel, p), sds((p.rows * p.cols, width), F32), [], [VMEM] * 2, "gate")(
        mid, own_gate_w)
    n_lane = p.j_base(p.n_col - 1) // LANES + 1
    back = call(
        functools.partial(triangle_kernel, p), sds((n, p.back_rows, LANES), BF16),
        [pltpu.VMEM((p.n_col, p.n_row * p.edge_rows, LANES), F32),
         pltpu.VMEM((ch, p.n_col, p.m * p.q, LANES), F32),
         pltpu.VMEM((ch, p.n_col, n_lane * LANES, LANES), F32),
         pltpu.VMEM((ch, n_lane, p.m * p.q, LANES), F32),
         pltpu.VMEM((p.n_col, p.m * ch, LANES), F32)],
        [VMEM], "triangle")(edges)

    home = jnp.zeros((p.n_col, p.own, p.res, p.feat), BF16)
    for shift in range(p.n_col):
        part = lax.dynamic_index_in_dim(emb, lax.rem(col + shift, p.n_col), 0, keepdims=False)
        if shift:
            part = lax.ppermute(part, "col", [(c, (c + shift) % p.n_col) for c in range(p.n_col)])
        home = lax.dynamic_update_index_in_dim(home, part, lax.rem(col + p.n_col - shift, p.n_col), 0)

    back = lax.all_to_all(back, ALL, 0, 0, tiled=True)
    state = call(
        functools.partial(final_kernel, p), sds((p.rows, p.cols, width), BF16),
        [pltpu.VMEM((n * p.back_rows, LANES), F32), pltpu.VMEM((LANES, LANES), F32),
         pltpu.VMEM((p.rows * p.cols, LANES), F32)],
        [VMEM] * 4, "final")(back, mid, out_gate, last_w)
    return home.reshape(x.shape), state


def general(
    stack_embedding,
    pair_representation,
    mixing_entry_coefficients,
    mixing_final_coefficients,
    pair_bias_matrix,
    tensor_side_coefficients,
    outer_output_weight,
    triangle_projection_weight,
    triangle_output_weight,
):
    sequences_per_device, residues_per_device, alignment_channels = stack_embedding.shape
    rows_dev = pair_representation.shape[0]
    pair_width = pair_representation.shape[2]
    number_heads = pair_bias_matrix.shape[1]
    head_channels = alignment_channels // number_heads
    outer_width = tensor_side_coefficients.shape[1] // 2
    row_count = lax.axis_size("row")
    seq_total = sequences_per_device * row_count
    row_index = lax.axis_index("row")
    normalized_input = (
        standardize_features(stack_embedding).astype(jnp.bfloat16).reshape(-1, alignment_channels)
    )
    mapped_lines = jnp.dot(
        normalized_input, mixing_entry_coefficients, preferred_element_type=jnp.float32
    )
    stack_probe_vectors = (
        (mapped_lines[:, :alignment_channels] * head_channels ** (-0.5))
        .astype(jnp.bfloat16)
        .reshape(sequences_per_device, residues_per_device, number_heads, head_channels)
    )
    stack_lookup_vectors = (
        mapped_lines[:, alignment_channels : 2 * alignment_channels]
        .astype(jnp.bfloat16)
        .reshape(sequences_per_device, residues_per_device, alignment_channels)
    )
    stack_content_vectors = (
        mapped_lines[:, 2 * alignment_channels : 3 * alignment_channels]
        .astype(jnp.bfloat16)
        .reshape(sequences_per_device, residues_per_device, alignment_channels)
    )
    sigmoid_factors = jax.nn.sigmoid(mapped_lines[:, 3 * alignment_channels :]).reshape(
        sequences_per_device, residues_per_device, alignment_channels
    )
    pair_normed = standardize_features(pair_representation).astype(jnp.bfloat16)
    bias_local = jnp.einsum(
        "ijc,ch->hij", pair_normed, pair_bias_matrix, preferred_element_type=jnp.float32
    ).astype(jnp.bfloat16)
    bias_all = lax.all_gather(bias_local, "row", axis=1, tiled=True)
    bias_query = lax.all_to_all(bias_all, "col", split_axis=1, concat_axis=2, tiled=True)
    best_score = jnp.full(
        (sequences_per_device, number_heads, residues_per_device), -1e30, jnp.float32
    )
    received_keys = lax.all_gather(stack_lookup_vectors, "col", axis=1, tiled=True)
    received_values = lax.all_gather(stack_content_vectors, "col", axis=1, tiled=True)
    key_count = received_keys.shape[1]
    received_keys = received_keys.reshape(
        sequences_per_device, key_count, number_heads, head_channels
    )
    received_values = received_values.reshape(
        sequences_per_device, key_count, number_heads, head_channels
    )
    bias_piece = bias_query.astype(jnp.float32)
    scores = (
        jnp.einsum(
            "yeca,yica->ycei",
            stack_probe_vectors,
            received_keys,
            preferred_element_type=jnp.float32,
        )
        + bias_piece[None]
    )
    next_best = jnp.maximum(best_score, jnp.max(scores, axis=-1))
    weights = jnp.exp(scores - next_best[..., None])
    next_sum = jnp.sum(weights, axis=-1)
    update = jnp.einsum(
        "shqk,skhd->sqhd",
        weights.astype(jnp.bfloat16),
        received_values,
        preferred_element_type=jnp.float32,
    )
    weighted_mixture = (update / jnp.transpose(next_sum, (0, 2, 1))[..., None]).reshape(
        sequences_per_device, residues_per_device, alignment_channels
    )
    scaled_mixture = (sigmoid_factors * weighted_mixture).astype(jnp.bfloat16)
    stack_increment = jnp.dot(
        scaled_mixture.reshape(-1, alignment_channels),
        mixing_final_coefficients,
        preferred_element_type=jnp.float32,
    ).reshape(sequences_per_device, residues_per_device, alignment_channels)
    stack_embedding_updated = (stack_embedding.astype(jnp.float32) + stack_increment).astype(
        jnp.bfloat16
    )
    tensor_standardized = (
        standardize_features(stack_embedding_updated)
        .astype(jnp.bfloat16)
        .reshape(-1, alignment_channels)
    )
    sides = jnp.dot(
        tensor_standardized, tensor_side_coefficients, preferred_element_type=jnp.float32
    ).astype(jnp.bfloat16)
    sides = sides.reshape(sequences_per_device, residues_per_device, 2 * outer_width)
    left_side = sides[..., :outer_width]
    right_side = sides[..., outer_width:]
    left_wide = lax.all_gather(left_side, "col", axis=1, tiled=True)
    left_every, right_all = (
        lax.all_gather(left_wide, "row", axis=0, tiled=True),
        lax.all_gather(right_side, "row", axis=0, tiled=True),
    )
    left_all = lax.dynamic_slice_in_dim(left_every, row_index * rows_dev, rows_dev, 1)
    products = jnp.einsum("sic,sjd->ijcd", left_all, right_all, preferred_element_type=jnp.float32)
    averaged = (products * (1.0 / seq_total)).astype(jnp.bfloat16)
    outer_update = jnp.dot(
        averaged.reshape(-1, outer_width * outer_width),
        outer_output_weight,
        preferred_element_type=jnp.float32,
    )
    pair_mid = (
        pair_representation.astype(jnp.float32)
        + outer_update.reshape(rows_dev, residues_per_device, pair_width)
    ).astype(jnp.bfloat16)
    tri_normed = standardize_features(pair_mid).astype(jnp.bfloat16).reshape(-1, pair_width)
    tri_parts = jnp.dot(
        tri_normed, triangle_projection_weight, preferred_element_type=jnp.float32
    ).reshape(rows_dev, residues_per_device, 5 * pair_width)
    left_edge = (
        jax.nn.sigmoid(tri_parts[..., pair_width : 2 * pair_width]) * tri_parts[..., :pair_width]
    ).astype(jnp.bfloat16)
    right_edge = (
        jax.nn.sigmoid(tri_parts[..., 3 * pair_width : 4 * pair_width])
        * tri_parts[..., 2 * pair_width : 3 * pair_width]
    ).astype(jnp.bfloat16)
    out_gate = jax.nn.sigmoid(tri_parts[..., 4 * pair_width :])
    right_rows = lax.all_gather(right_edge, "row", axis=0, tiled=True)
    right_query = lax.all_to_all(right_rows, "col", split_axis=0, concat_axis=1, tiled=True)
    arrived = lax.all_gather(left_edge, "col", axis=1, tiled=True)
    summed = jnp.einsum("ikc,jkc->ijc", arrived, right_query, preferred_element_type=jnp.float32)
    tri_ln = standardize_features(summed).astype(jnp.bfloat16)
    tri_update = jnp.dot(
        tri_ln.reshape(-1, pair_width), triangle_output_weight, preferred_element_type=jnp.float32
    ).reshape(rows_dev, residues_per_device, pair_width)
    pair_state_next = (pair_mid.astype(jnp.float32) + out_gate * tri_update).astype(jnp.bfloat16)
    return (stack_embedding_updated, pair_state_next)


def shards(x, pair, w_in, w_out, w_bias, w_side, w_outer, w_tri, w_last):
    p = Plan(lax.axis_size("row"), lax.axis_size("col"), x.shape, pair.shape, w_bias.shape[1],
             w_side.shape[1] // 2, w_last.shape[1])
    path = functools.partial(fast, p) if p.ok else general
    return path(x, pair, w_in, w_out, w_bias, w_side, w_outer, w_tri, w_last)


def solution(mesh):
    return jax.shard_map(
        shards,
        mesh=mesh,
        in_specs=(P("row", "col", None), P("row", "col", None), P(), P(), P(), P(), P(), P(), P()),
        out_specs=(P("row", "col", None), P("row", "col", None)),
        check_vma=False,
    )
```

```python
import functools

import jax
import jax.numpy as jnp
import numpy as np
from jax import lax
from jax.experimental import pallas as pl
from jax.experimental.pallas import tpu as pltpu
from jax.sharding import PartitionSpec as P

epsilon = 1e-05
LANES = 128
SUBLANES = 8
F32 = jnp.float32
BF16 = jnp.bfloat16
ALL = ("row", "col")
NT = (((1,), (1,)), ((), ()))
VMEM = pl.BlockSpec(memory_space=pltpu.VMEM)
SMEM = pl.BlockSpec(memory_space=pltpu.SMEM)


def standardize_features(inputs, axis=-1):
    inputs = inputs.astype(jnp.float32)
    center = inputs - jnp.mean(inputs, axis=axis, keepdims=True)
    spread = jnp.mean(center * center, axis=axis, keepdims=True)
    return center * lax.rsqrt(spread + epsilon)


def dot(a, b):
    return jnp.dot(a, b, preferred_element_type=F32)


def dot_nt(a, b):
    return lax.dot_general(a, b, NT, preferred_element_type=F32)


def lane_iota(rows):
    return lax.broadcasted_iota(jnp.int32, (rows, LANES), 1)


def call(body, out_shape, scratch, in_specs, name):
    return pl.pallas_call(
        body,
        out_shape=out_shape,
        in_specs=in_specs,
        out_specs=jax.tree.map(lambda _: VMEM, out_shape),
        scratch_shapes=scratch,
        name=name,
        cost_estimate=pl.CostEstimate(flops=400_000_000, bytes_accessed=4_000_000, transcendentals=0),
        compiler_params=pltpu.CompilerParams(vmem_limit_bytes=24 * 1024 * 1024),
    )


class Plan:
    def __init__(self, n_row, n_col, x, pair, heads, outer, channels_out):
        self.n_row, self.n_col, self.n = n_row, n_col, n_row * n_col
        self.seqs, self.res, self.feat = x
        self.rows, self.cols, self.width = pair
        self.heads, self.outer = heads, outer
        self.hd = self.feat // heads
        self.total = self.res * n_col
        self.ok = False
        if self.seqs % n_col or self.width != LANES or heads != SUBLANES or self.cols != self.res:
            return
        if self.rows * n_row != self.total or self.feat % LANES:
            return
        self.own = self.seqs // n_col
        self.seq_total = self.own * self.n
        self.i_main = LANES // heads
        self.i_rem = self.rows - self.i_main
        if not 0 < self.i_rem or LANES % (self.i_rem * heads) or self.cols % SUBLANES:
            return
        self.rem = self.i_rem * heads
        self.fold = LANES // self.rem
        if n_row % self.fold:
            return
        self.groups = self.cols // SUBLANES
        self.rem_rows = -(-self.groups // self.fold)
        self.bias_rows = self.cols + SUBLANES * self.rem_rows
        if LANES % outer or outer % (LANES // outer):
            return
        self.pack = LANES // outer
        if self.rows % self.pack or self.cols % self.pack:
            return
        self.lk, self.rk = self.rows // self.pack, self.cols // self.pack
        used = (self.lk + self.rk) * self.own
        self.side_rows = -(-used // 16) * 16
        self.cpad = -(-self.cols // 16) * 16
        if self.width % self.n:
            return
        self.ch = self.width // self.n
        if 2 * self.ch != SUBLANES or n_row % n_col:
            return
        self.q = LANES // self.cols
        self.ig = -(-self.rows // self.q)
        self.ipad = self.ig * self.q
        self.per = n_row // n_col
        self.jslot = self.per * self.ipad
        if self.per * self.rows != self.cols or self.q * self.jslot > LANES:
            return
        self.m = n_row * self.ig
        self.edge_rows = self.ig * SUBLANES
        self.back_rows = -(-self.ig * self.ch // 16) * 16
        self.ok = True

    def j_base(self, c):
        return (c // self.q) * LANES + (c % self.q) * self.jslot


def bias_kernel(p, pair_ref, w_ref, out_ref):
    normed = standardize_features(pair_ref[...])
    heads = p.heads
    spread = (lax.broadcasted_iota(jnp.int32, (heads, LANES), 1) % heads
              == lax.broadcasted_iota(jnp.int32, (heads, LANES), 0))
    tiled = lax.dot_general(w_ref[...], jnp.where(spread, 1.0, 0.0).astype(BF16), (((0,), (0,)), ((), ())),
                            preferred_element_type=F32)
    slot = lane_iota(p.width) // heads
    main = jnp.zeros((p.cols, LANES), F32)
    rem = jnp.zeros((p.cols, LANES), F32)
    for i in range(p.rows):
        block = normed[i * p.cols:(i + 1) * p.cols].astype(BF16)
        if i < p.i_main:
            main += dot(block, jnp.where(slot == i, tiled, 0.0).astype(BF16))
        else:
            rem += dot(block, jnp.where(slot % p.i_rem == i - p.i_main, tiled, 0.0).astype(BF16))
    piece = [main]
    at = lane_iota(SUBLANES) // p.rem
    for k in range(p.rem_rows):
        folded = jnp.zeros((SUBLANES, LANES), F32)
        for f in range(p.fold):
            g = k * p.fold + f
            if g < p.groups:
                folded = jnp.where(at == f, rem[g * SUBLANES:(g + 1) * SUBLANES], folded)
        piece.append(folded)
    piece = jnp.concatenate(piece, axis=0).astype(BF16)
    for d in range(p.n):
        out_ref[d] = piece


def project_kernel(p, col_ref, *refs):
    x_refs = refs[:p.n_col]
    w_ref, q_ref, k_ref, v_ref, gate_ref, x_out, hold = refs[p.n_col:]
    me = col_ref[0]
    for shift in range(p.n_col):
        hold[lax.rem(me + (p.n_col - shift), p.n_col)] = x_refs[shift][...].astype(F32)
    f = p.feat
    for s in range(p.own):
        x = jnp.concatenate([hold[c, s] for c in range(p.n_col)], axis=0)
        x_out[s] = x
        lines = dot(standardize_features(x).astype(BF16), w_ref[...])
        q_ref[s] = (lines[:, :f] * p.hd ** (-0.5)).astype(BF16)
        k_ref[s] = lines[:, f:2 * f].astype(BF16)
        v_ref[s] = lines[:, 2 * f:3 * f].astype(BF16)
        gate_ref[s] = jax.nn.sigmoid(lines[:, 3 * f:])


def attend_kernel(p, q_ref, k_ref, v_ref, gate_ref, x_ref, bias_ref, sel_ref, wf_ref, wl_ref, wr_ref,
                  emb_ref, side_ref, bias, l4, r4, lint, rint, send):
    h, t, f = p.heads, p.total, p.feat
    main = p.n_row * LANES
    for r in range(p.n_row):
        for c in range(p.n_col):
            bias[c * p.cols:(c + 1) * p.cols, r * LANES:(r + 1) * LANES] = (
                bias_ref[r * p.n_col + c, 0:p.cols].astype(F32))
    at = lane_iota(SUBLANES) // p.rem
    for c in range(p.n_col):
        for b in range(p.n_row // p.fold):
            tails = [bias_ref[(b * p.fold + u) * p.n_col + c, p.cols:p.bias_rows].astype(F32)
                     for u in range(p.fold)]
            for g in range(p.groups):
                k, part = g // p.fold, g % p.fold
                block = jnp.zeros((SUBLANES, LANES), F32)
                for u in range(p.fold):
                    piece = tails[u][k * SUBLANES:(k + 1) * SUBLANES]
                    turn = ((u - part) * p.rem) % LANES
                    if turn:
                        piece = pltpu.roll(piece, turn, axis=1)
                    block = jnp.where(at == u, piece, block)
                bias[c * p.cols + g * SUBLANES:c * p.cols + (g + 1) * SUBLANES,
                     main + b * LANES:main + (b + 1) * LANES] = block
    head_of = (lax.broadcasted_iota(jnp.int32, (h, f), 1) // p.hd
               == lax.broadcasted_iota(jnp.int32, (h, f), 0))
    head_mask = jnp.where(head_of, 1.0, 0.0)
    wide = t * h
    own_head = (lax.broadcasted_iota(jnp.int32, (f, wide), 0) // p.hd
                == lax.broadcasted_iota(jnp.int32, (f, wide), 1) % h)
    lane = lane_iota(t // p.pack) // p.outer
    for s in range(p.own):
        q = q_ref[s].astype(F32)
        spread = jnp.broadcast_to(q[:, None, :], (t, h, f)) * head_mask[None]
        parts = [spread[r * p.rows:r * p.rows + p.i_main] for r in range(p.n_row)]
        parts += [spread[r * p.rows + p.i_main:(r + 1) * p.rows] for r in range(p.n_row)]
        spread = jnp.concatenate(parts, axis=0).reshape(wide, f).astype(BF16)
        scores = dot_nt(k_ref[s], spread) + bias[...]
        peak = jnp.max(scores, axis=0, keepdims=True)
        weights = jnp.exp(scores - peak)
        total = jnp.sum(weights, axis=0, keepdims=True)
        v_t = jnp.transpose(v_ref[s].astype(F32)).astype(BF16)
        mixed = dot(v_t, weights.astype(BF16)) * (1.0 / total)
        mixed = jnp.where(own_head, mixed, 0.0).astype(BF16)
        attended = dot_nt(sel_ref[...], mixed)
        gated = (gate_ref[s] * attended).astype(BF16)
        new = (x_ref[s] + dot(gated, wf_ref[...])).astype(BF16).astype(F32)
        for c in range(p.n_col):
            emb_ref[c, s] = new[c * p.res:(c + 1) * p.res].astype(BF16)
        normed = standardize_features(new).astype(BF16)
        for w_ref, four, woven in ((wl_ref, l4, lint), (wr_ref, r4, rint)):
            four[...] = dot(normed, w_ref[...])
            packed = four[pl.ds(0, t // p.pack, stride=p.pack), :]
            for a in range(1, p.pack):
                packed = jnp.where(lane == a, four[pl.ds(a, t // p.pack, stride=p.pack), :], packed)
            woven[pl.ds(s, t // p.pack, stride=p.own), :] = packed
    nr, nl = p.rk * p.own, p.lk * p.own
    for r in range(p.n_row):
        for c in range(p.n_col):
            d = r * p.n_col + c
            send[d, 0:nr] = rint[c * nr:(c + 1) * nr]
            send[d, nr:nr + nl] = lint[r * nl:(r + 1) * nl]
            if nr + nl < p.side_rows:
                send[d, nr + nl:p.side_rows] = jnp.zeros((p.side_rows - nr - nl, LANES), F32)
    side_ref[...] = send[...].astype(BF16)


def outer_kernel(p, recv_ref, pair_ref, w_ref, wv_ref, wg_ref, mid_ref, edge_ref,
                 flat, rt, lhs, mid):
    flat[...] = recv_ref[...].reshape(p.n * p.side_rows, LANES).astype(F32)

    def chunk(k):
        return jnp.concatenate(
            [flat[pl.ds(k * p.own + s, p.n, stride=p.side_rows), :] for s in range(p.own)], axis=0)

    for k in range(p.rk):
        rt[k * LANES:(k + 1) * LANES, :] = jnp.transpose(chunk(k))
    right = []
    for first in range(0, p.outer, p.pack):
        right.append(jnp.concatenate(
            [rt[pl.ds(first + d, p.cols, stride=p.outer), :] for d in range(p.pack)], axis=1))
    right = jnp.concatenate(right, axis=0).astype(BF16)
    at = lane_iota(p.seq_total) // p.outer
    left = []
    for g in range(p.lk):
        base = chunk(p.rk + g)
        turned = [base] + [pltpu.roll(base, t * p.outer, axis=1) for t in range(1, p.pack)]
        for a in range(p.pack):
            left.append(jnp.concatenate(
                [jnp.where(at == d, turned[(d - a) % p.pack], 0.0) for d in range(p.pack)], axis=0).astype(BF16))
    products = dot(right, jnp.concatenate(left, axis=1)) * (1.0 / p.seq_total)
    for i in range(p.rows):
        for g in range(p.outer // p.pack):
            lhs[i * p.cpad:i * p.cpad + p.cols, g * LANES:(g + 1) * LANES] = products[
                g * p.cols:(g + 1) * p.cols, i * LANES:(i + 1) * LANES].astype(BF16)
        if p.cpad > p.cols:
            lhs[i * p.cpad + p.cols:(i + 1) * p.cpad, :] = jnp.zeros((p.cpad - p.cols, lhs.shape[1]), BF16)
    update = dot(lhs[...], w_ref[...])
    for i in range(p.rows):
        fresh = (pair_ref[i].astype(F32) + update[i * p.cpad:i * p.cpad + p.cols]).astype(BF16)
        mid_ref[i] = fresh
        mid[i * p.cols:(i + 1) * p.cols, :] = fresh.astype(F32)
    tail = mid.shape[0] - p.rows * p.cols
    mid[p.rows * p.cols:, :] = jnp.zeros((tail, LANES), F32)
    step = p.q * p.cols
    for k in range(p.ig):
        normed = standardize_features(mid[k * step:k * step + LANES, :]).astype(BF16)
        value = dot_nt(wv_ref[...], normed)
        gate = jax.nn.sigmoid(dot_nt(wg_ref[...], normed))
        edge_ref[:, k * SUBLANES:(k + 1) * SUBLANES, :] = (gate * value).reshape(
            p.n, SUBLANES, LANES).astype(BF16)


def gate_kernel(p, mid_ref, w_ref, out_ref):
    normed = standardize_features(mid_ref[...]).reshape(p.rows * p.cols, p.width).astype(BF16)
    out_ref[...] = jax.nn.sigmoid(dot(normed, w_ref[...]))


def triangle_kernel(p, recv_ref, out_ref, flat, ls, rs, os, sb):
    for r in range(p.n_row):
        for c in range(p.n_col):
            flat[c, r * p.edge_rows:(r + 1) * p.edge_rows, :] = recv_ref[r * p.n_col + c].astype(F32)
    lane = lane_iota(p.m)
    blocks = p.per * p.ig
    rs[...] = jnp.zeros_like(rs)
    for ch in range(p.ch):
        for c in range(p.n_col):
            left = flat[c, pl.ds(ch, p.m, stride=SUBLANES), :]
            right = flat[c, pl.ds(p.ch + ch, p.m, stride=SUBLANES), :]
            for a in range(p.q):
                turn = (-a * p.cols) % LANES
                lt = pltpu.roll(left, turn, axis=1) if turn else left
                rt = pltpu.roll(right, turn, axis=1) if turn else right
                ls[ch, c, pl.ds(a, p.m, stride=p.q), :] = jnp.where(lane < p.cols, lt, 0.0)
                for first in range(0, p.n_col, p.q):
                    many = min(p.q, p.n_col - first) * blocks
                    rs[ch, c, pl.ds(p.j_base(first) + a, many, stride=p.q), :] = rt[
                        first * blocks:first * blocks + many]
    for ch in range(p.ch):
        lfull = jnp.concatenate([ls[ch, c] for c in range(p.n_col)], axis=1).astype(BF16)
        rfull = jnp.concatenate([rs[ch, c] for c in range(p.n_col)], axis=1).astype(BF16)
        summed = dot_nt(lfull, rfull)
        for b in range(summed.shape[1] // LANES):
            os[ch, b] = summed[:, b * LANES:(b + 1) * LANES]
        rows = [[os[ch, b, pl.ds(a, p.m, stride=p.q), :] for a in range(p.q)]
                for b in range(summed.shape[1] // LANES)]
        for c in range(p.n_col):
            b, part = c // p.q, c % p.q
            packed = None
            for a in range(p.q):
                turn = ((a - part) * p.jslot) % LANES
                piece = pltpu.roll(rows[b][a], turn, axis=1) if turn else rows[b][a]
                packed = piece if packed is None else jnp.where(lane // p.jslot == a, piece, packed)
            sb[c, pl.ds(ch, p.m, stride=p.ch), :] = packed
    used = p.ig * p.ch
    for r in range(p.n_row):
        for c in range(p.n_col):
            d = r * p.n_col + c
            out_ref[d, 0:used] = sb[c, r * used:(r + 1) * used, :].astype(BF16)
            if used < p.back_rows:
                out_ref[d, used:p.back_rows] = jnp.zeros((p.back_rows - used, LANES), BF16)


def final_kernel(p, recv_ref, mid_ref, gate_ref, w_ref, out_ref, flat, hold, update):
    flat[...] = recv_ref[...].reshape(p.n * p.back_rows, LANES).astype(F32)
    for k in range(p.ig):
        summed = jnp.concatenate(
            [flat[pl.ds(k * p.ch + ch, p.n, stride=p.back_rows), :] for ch in range(p.ch)], axis=0)
        normed = jnp.transpose(standardize_features(summed, axis=0)).astype(BF16)
        hold[...] = dot(normed, w_ref[...])
        for a in range(p.q):
            i = k * p.q + a
            if i < p.rows:
                for u in range(p.per):
                    update[i * p.cols + u * p.rows:i * p.cols + (u + 1) * p.rows, :] = hold[
                        a * p.jslot + u * p.ipad:a * p.jslot + u * p.ipad + p.rows, :]
    fresh = mid_ref[...].astype(F32).reshape(p.rows * p.cols, p.width) + gate_ref[...] * update[...]
    out_ref[...] = fresh.reshape(p.rows, p.cols, p.width).astype(BF16)


def fast(p, x, pair, w_in, w_out, w_bias, w_side, w_outer, w_tri, w_last):
    col = lax.axis_index("col")
    n, ch, width = p.n, p.ch, p.width
    sds = jax.ShapeDtypeStruct

    left_w, right_w = w_side[:, :p.outer], w_side[:, p.outer:]
    left_w, right_w = jnp.tile(left_w, (1, p.pack)), jnp.tile(right_w, (1, p.pack))
    by_d = jnp.transpose(w_outer.reshape(p.outer, p.outer, width), (1, 0, 2)).reshape(w_outer.shape)
    blocks = jnp.transpose(w_tri.reshape(width, 5, width), (1, 2, 0)).reshape(5, n, ch, width)
    value_w = jnp.concatenate([blocks[0], blocks[2]], axis=1).reshape(n * 2 * ch, width)
    gate_w = jnp.concatenate([blocks[1], blocks[3]], axis=1).reshape(n * 2 * ch, width)
    own_gate_w = w_tri[:, 4 * width:]
    last_w = jnp.transpose(w_last.reshape(n, ch, width), (1, 0, 2)).reshape(width, width)
    spot = np.arange(p.total).reshape(p.n_row, p.rows)
    order = np.concatenate([spot[:, :p.i_main].reshape(-1), spot[:, p.i_main:].reshape(-1)])
    sel = jnp.asarray((np.arange(p.total)[:, None] == np.repeat(order, p.heads)[None]), BF16)

    piece = call(functools.partial(bias_kernel, p), sds((n, p.bias_rows, LANES), BF16), [], [VMEM] * 2, "bias")(
        pair.reshape(p.rows * p.cols, width), w_bias.T)
    bias = lax.all_to_all(piece, ALL, 0, 0, tiled=True)
    chunks = x.reshape(p.n_col, p.own, p.res, p.feat)
    parts = []
    for shift in range(p.n_col):
        part = lax.dynamic_index_in_dim(chunks, lax.rem(col + shift, p.n_col), 0, keepdims=False)
        if shift:
            part = lax.ppermute(part, "col", [(c, (c + shift) % p.n_col) for c in range(p.n_col)])
        parts.append(part)
    seq = (p.own, p.total, p.feat)
    q, k, v, gate, whole = call(
        functools.partial(project_kernel, p),
        (sds(seq, BF16), sds(seq, BF16), sds(seq, BF16), sds(seq, F32), sds(seq, F32)),
        [pltpu.VMEM((p.n_col, p.own, p.res, p.feat), F32)],
        [SMEM] + [VMEM] * (p.n_col + 1), "project")(col.reshape(1), *parts, w_in)
    emb, sides = call(
        functools.partial(attend_kernel, p),
        (sds((p.n_col, p.own, p.res, p.feat), BF16), sds((n, p.side_rows, LANES), BF16)),
        [pltpu.VMEM((p.total, p.total * p.heads), F32)]
        + [pltpu.VMEM((p.total, LANES), F32)] * 2
        + [pltpu.VMEM((p.total // p.pack * p.own, LANES), F32)] * 2
        + [pltpu.VMEM((n, p.side_rows, LANES), F32)],
        [VMEM] * 10, "attend")(q, k, v, gate, whole, bias, sel, w_out, left_w, right_w)

    sides = lax.all_to_all(sides, ALL, 0, 0, tiled=True)
    mid, edges = call(
        functools.partial(outer_kernel, p),
        (sds((p.rows, p.cols, width), BF16), sds((n, p.edge_rows, LANES), BF16)),
        [pltpu.VMEM((n * p.side_rows, LANES), F32),
         pltpu.VMEM((p.rk * LANES, p.seq_total), F32),
         pltpu.VMEM((p.rows * p.cpad, p.outer * p.outer), BF16),
         pltpu.VMEM(((p.ig - 1) * p.q * p.cols + LANES, LANES), F32)],
        [VMEM] * 5, "outer")(sides, pair, by_d, value_w, gate_w)

    edges = lax.all_to_all(edges, ALL, 0, 0, tiled=True)
    out_gate = call(functools.partial(gate_kernel, p), sds((p.rows * p.cols, width), F32), [], [VMEM] * 2, "gate")(
        mid, own_gate_w)
    n_lane = p.j_base(p.n_col - 1) // LANES + 1
    back = call(
        functools.partial(triangle_kernel, p), sds((n, p.back_rows, LANES), BF16),
        [pltpu.VMEM((p.n_col, p.n_row * p.edge_rows, LANES), F32),
         pltpu.VMEM((ch, p.n_col, p.m * p.q, LANES), F32),
         pltpu.VMEM((ch, p.n_col, n_lane * LANES, LANES), F32),
         pltpu.VMEM((ch, n_lane, p.m * p.q, LANES), F32),
         pltpu.VMEM((p.n_col, p.m * ch, LANES), F32)],
        [VMEM], "triangle")(edges)

    home = jnp.zeros((p.n_col, p.own, p.res, p.feat), BF16)
    for shift in range(p.n_col):
        part = lax.dynamic_index_in_dim(emb, lax.rem(col + shift, p.n_col), 0, keepdims=False)
        if shift:
            part = lax.ppermute(part, "col", [(c, (c + shift) % p.n_col) for c in range(p.n_col)])
        home = lax.dynamic_update_index_in_dim(home, part, lax.rem(col + p.n_col - shift, p.n_col), 0)

    back = lax.all_to_all(back, ALL, 0, 0, tiled=True)
    state = call(
        functools.partial(final_kernel, p), sds((p.rows, p.cols, width), BF16),
        [pltpu.VMEM((n * p.back_rows, LANES), F32), pltpu.VMEM((LANES, LANES), F32),
         pltpu.VMEM((p.rows * p.cols, LANES), F32)],
        [VMEM] * 4, "final")(back, mid, out_gate, last_w)
    return home.reshape(x.shape), state


def general(
    stack_embedding,
    pair_representation,
    mixing_entry_coefficients,
    mixing_final_coefficients,
    pair_bias_matrix,
    tensor_side_coefficients,
    outer_output_weight,
    triangle_projection_weight,
    triangle_output_weight,
):
    sequences_per_device, residues_per_device, alignment_channels = stack_embedding.shape
    rows_dev = pair_representation.shape[0]
    pair_width = pair_representation.shape[2]
    number_heads = pair_bias_matrix.shape[1]
    head_channels = alignment_channels // number_heads
    outer_width = tensor_side_coefficients.shape[1] // 2
    row_count = lax.axis_size("row")
    seq_total = sequences_per_device * row_count
    row_index = lax.axis_index("row")
    normalized_input = (
        standardize_features(stack_embedding).astype(jnp.bfloat16).reshape(-1, alignment_channels)
    )
    mapped_lines = jnp.dot(
        normalized_input, mixing_entry_coefficients, preferred_element_type=jnp.float32
    )
    stack_probe_vectors = (
        (mapped_lines[:, :alignment_channels] * head_channels ** (-0.5))
        .astype(jnp.bfloat16)
        .reshape(sequences_per_device, residues_per_device, number_heads, head_channels)
    )
    stack_lookup_vectors = (
        mapped_lines[:, alignment_channels : 2 * alignment_channels]
        .astype(jnp.bfloat16)
        .reshape(sequences_per_device, residues_per_device, alignment_channels)
    )
    stack_content_vectors = (
        mapped_lines[:, 2 * alignment_channels : 3 * alignment_channels]
        .astype(jnp.bfloat16)
        .reshape(sequences_per_device, residues_per_device, alignment_channels)
    )
    sigmoid_factors = jax.nn.sigmoid(mapped_lines[:, 3 * alignment_channels :]).reshape(
        sequences_per_device, residues_per_device, alignment_channels
    )
    pair_normed = standardize_features(pair_representation).astype(jnp.bfloat16)
    bias_local = jnp.einsum(
        "ijc,ch->hij", pair_normed, pair_bias_matrix, preferred_element_type=jnp.float32
    ).astype(jnp.bfloat16)
    bias_all = lax.all_gather(bias_local, "row", axis=1, tiled=True)
    bias_query = lax.all_to_all(bias_all, "col", split_axis=1, concat_axis=2, tiled=True)
    best_score = jnp.full(
        (sequences_per_device, number_heads, residues_per_device), -1e30, jnp.float32
    )
    received_keys = lax.all_gather(stack_lookup_vectors, "col", axis=1, tiled=True)
    received_values = lax.all_gather(stack_content_vectors, "col", axis=1, tiled=True)
    key_count = received_keys.shape[1]
    received_keys = received_keys.reshape(
        sequences_per_device, key_count, number_heads, head_channels
    )
    received_values = received_values.reshape(
        sequences_per_device, key_count, number_heads, head_channels
    )
    bias_piece = bias_query.astype(jnp.float32)
    scores = (
        jnp.einsum(
            "yeca,yica->ycei",
            stack_probe_vectors,
            received_keys,
            preferred_element_type=jnp.float32,
        )
        + bias_piece[None]
    )
    next_best = jnp.maximum(best_score, jnp.max(scores, axis=-1))
    weights = jnp.exp(scores - next_best[..., None])
    next_sum = jnp.sum(weights, axis=-1)
    update = jnp.einsum(
        "shqk,skhd->sqhd",
        weights.astype(jnp.bfloat16),
        received_values,
        preferred_element_type=jnp.float32,
    )
    weighted_mixture = (update / jnp.transpose(next_sum, (0, 2, 1))[..., None]).reshape(
        sequences_per_device, residues_per_device, alignment_channels
    )
    scaled_mixture = (sigmoid_factors * weighted_mixture).astype(jnp.bfloat16)
    stack_increment = jnp.dot(
        scaled_mixture.reshape(-1, alignment_channels),
        mixing_final_coefficients,
        preferred_element_type=jnp.float32,
    ).reshape(sequences_per_device, residues_per_device, alignment_channels)
    stack_embedding_updated = (stack_embedding.astype(jnp.float32) + stack_increment).astype(
        jnp.bfloat16
    )
    tensor_standardized = (
        standardize_features(stack_embedding_updated)
        .astype(jnp.bfloat16)
        .reshape(-1, alignment_channels)
    )
    sides = jnp.dot(
        tensor_standardized, tensor_side_coefficients, preferred_element_type=jnp.float32
    ).astype(jnp.bfloat16)
    sides = sides.reshape(sequences_per_device, residues_per_device, 2 * outer_width)
    left_side = sides[..., :outer_width]
    right_side = sides[..., outer_width:]
    left_wide = lax.all_gather(left_side, "col", axis=1, tiled=True)
    left_every, right_all = (
        lax.all_gather(left_wide, "row", axis=0, tiled=True),
        lax.all_gather(right_side, "row", axis=0, tiled=True),
    )
    left_all = lax.dynamic_slice_in_dim(left_every, row_index * rows_dev, rows_dev, 1)
    products = jnp.einsum("sic,sjd->ijcd", left_all, right_all, preferred_element_type=jnp.float32)
    averaged = (products * (1.0 / seq_total)).astype(jnp.bfloat16)
    outer_update = jnp.dot(
        averaged.reshape(-1, outer_width * outer_width),
        outer_output_weight,
        preferred_element_type=jnp.float32,
    )
    pair_mid = (
        pair_representation.astype(jnp.float32)
        + outer_update.reshape(rows_dev, residues_per_device, pair_width)
    ).astype(jnp.bfloat16)
    tri_normed = standardize_features(pair_mid).astype(jnp.bfloat16).reshape(-1, pair_width)
    tri_parts = jnp.dot(
        tri_normed, triangle_projection_weight, preferred_element_type=jnp.float32
    ).reshape(rows_dev, residues_per_device, 5 * pair_width)
    left_edge = (
        jax.nn.sigmoid(tri_parts[..., pair_width : 2 * pair_width]) * tri_parts[..., :pair_width]
    ).astype(jnp.bfloat16)
    right_edge = (
        jax.nn.sigmoid(tri_parts[..., 3 * pair_width : 4 * pair_width])
        * tri_parts[..., 2 * pair_width : 3 * pair_width]
    ).astype(jnp.bfloat16)
    out_gate = jax.nn.sigmoid(tri_parts[..., 4 * pair_width :])
    right_rows = lax.all_gather(right_edge, "row", axis=0, tiled=True)
    right_query = lax.all_to_all(right_rows, "col", split_axis=0, concat_axis=1, tiled=True)
    arrived = lax.all_gather(left_edge, "col", axis=1, tiled=True)
    summed = jnp.einsum("ikc,jkc->ijc", arrived, right_query, preferred_element_type=jnp.float32)
    tri_ln = standardize_features(summed).astype(jnp.bfloat16)
    tri_update = jnp.dot(
        tri_ln.reshape(-1, pair_width), triangle_output_weight, preferred_element_type=jnp.float32
    ).reshape(rows_dev, residues_per_device, pair_width)
    pair_state_next = (pair_mid.astype(jnp.float32) + out_gate * tri_update).astype(jnp.bfloat16)
    return (stack_embedding_updated, pair_state_next)


def shards(x, pair, w_in, w_out, w_bias, w_side, w_outer, w_tri, w_last):
    p = Plan(lax.axis_size("row"), lax.axis_size("col"), x.shape, pair.shape, w_bias.shape[1],
             w_side.shape[1] // 2, w_last.shape[1])
    path = functools.partial(fast, p) if p.ok else general
    return path(x, pair, w_in, w_out, w_bias, w_side, w_outer, w_tri, w_last)


def solution(mesh):
    return jax.shard_map(
        shards,
        mesh=mesh,
        in_specs=(P("row", "col", None), P("row", "col", None), P(), P(), P(), P(), P(), P(), P()),
        out_specs=(P("row", "col", None), P("row", "col", None)),
        check_vma=False,
    )
```

```python
import functools

import jax
import jax.numpy as jnp
from jax import lax
from jax.experimental import pallas as pl
from jax.experimental.pallas import tpu as pltpu
from jax.sharding import PartitionSpec as P

epsilon = 1e-05
LANES = 128
SUBLANES = 8
F32 = jnp.float32
BF16 = jnp.bfloat16
ALL = ("row", "col")
NT = (((1,), (1,)), ((), ()))
VMEM = pl.BlockSpec(memory_space=pltpu.VMEM)
SMEM = pl.BlockSpec(memory_space=pltpu.SMEM)


def standardize_features(inputs, axis=-1):
    inputs = inputs.astype(jnp.float32)
    center = inputs - jnp.mean(inputs, axis=axis, keepdims=True)
    spread = jnp.mean(center * center, axis=axis, keepdims=True)
    return center * lax.rsqrt(spread + epsilon)


def dot(a, b):
    return jnp.dot(a, b, preferred_element_type=F32)


def dot_nt(a, b):
    return lax.dot_general(a, b, NT, preferred_element_type=F32)


def lane_iota(rows, width=LANES):
    return lax.broadcasted_iota(jnp.int32, (rows, width), 1)


def row_iota(rows, width=LANES):
    return lax.broadcasted_iota(jnp.int32, (rows, width), 0)


def over(index, size):
    return lax.shift_right_logical(index, jnp.int32(size.bit_length() - 1))


def modulo(index, size):
    return lax.bitwise_and(index, jnp.int32(size - 1))


def call(body, out_shape, scratch, in_specs, name):
    return pl.pallas_call(
        body,
        out_shape=out_shape,
        in_specs=in_specs,
        out_specs=jax.tree.map(lambda _: VMEM, out_shape),
        scratch_shapes=scratch,
        name=name,
        cost_estimate=pl.CostEstimate(flops=400_000_000, bytes_accessed=4_000_000, transcendentals=0),
        compiler_params=pltpu.CompilerParams(vmem_limit_bytes=24 * 1024 * 1024),
    )


class Plan:
    def __init__(self, n_row, n_col, x, pair, heads, outer, channels_out):
        self.n_row, self.n_col, self.n = n_row, n_col, n_row * n_col
        self.seqs, self.res, self.feat = x
        self.rows, self.cols, self.width = pair
        self.heads, self.outer = heads, outer
        self.hd = self.feat // heads
        self.total = self.res * n_col
        self.ok = False
        if any(size & (size - 1) for size in (heads, outer, self.hd, n_row, n_col)):
            return
        if self.seqs % n_col or self.width != LANES or heads != SUBLANES or self.cols != self.res:
            return
        if self.rows * n_row != self.total or self.feat % LANES:
            return
        self.split = 2
        if n_col % self.split:
            return
        self.n_group = n_col // self.split
        self.own = self.seqs // self.n_group
        self.seq_total = self.own * self.n_group * n_row
        if LANES % outer or outer % (LANES // outer):
            return
        self.pack = LANES // outer
        if self.rows % self.pack or self.cols % self.pack:
            return
        self.half = -(-self.rows // (self.split * self.pack)) * self.pack
        self.late = self.rows - self.half
        self.queries = n_row * self.half
        self.i_main = LANES // heads // 2
        self.i_rem = self.half - self.i_main
        if not 0 < self.i_rem or self.i_main % self.pack or self.i_rem % self.pack or LANES % (self.i_rem * heads) or self.cols % SUBLANES:
            return
        self.km = self.i_main // self.pack
        self.main, self.rem = self.i_main * heads, self.i_rem * heads
        self.groups = self.cols // SUBLANES
        self.tall = -(-self.groups // 2)
        self.fold = LANES // self.rem
        if n_row % 2 or n_row % self.fold:
            return
        self.main_at = [(g % self.tall, g // self.tall * self.main) for g in range(self.groups)]
        spare = [(self.tall, f * self.rem) for f in range(self.fold)]
        if self.groups % 2:
            spare += [(self.tall - 1, self.main + f * self.rem) for f in range(self.main // self.rem)]
        if len(spare) < self.groups:
            return
        self.rem_at = spare[:self.groups]
        self.bias_rows = (self.tall + 1) * SUBLANES
        self.per = n_row // n_col
        if n_row % n_col or self.per * self.rows != self.cols:
            return
        self.lk, self.rk = self.rows // self.pack, self.cols // self.pack
        self.hk = self.half // self.pack
        self.ek = self.lk - self.hk
        chunks = max(self.ek + self.per * self.hk, self.hk + self.per * self.ek)
        self.side_rows = -(-chunks * self.own // 16) * 16
        self.cpad = -(-self.cols // 16) * 16
        if self.width % self.n:
            return
        self.ch = self.width // self.n
        if 2 * self.ch != SUBLANES:
            return
        self.q = LANES // self.cols
        self.ig = -(-self.rows // self.q)
        self.ipad = self.ig * self.q
        self.jslot = self.per * self.ipad
        if self.q * self.jslot > LANES:
            return
        self.m = n_row * self.ig
        self.edge_rows = self.ig * SUBLANES
        self.back_rows = -(-self.ig * self.ch // 16) * 16
        self.ok = True

    def j_base(self, c):
        return (c // self.q) * LANES + (c % self.q) * self.jslot


def bias_kernel(p, pair_ref, w_ref, out_ref):
    normed = standardize_features(pair_ref[...])
    heads = p.heads
    spread = modulo(lane_iota(heads), heads) == row_iota(heads)
    tiled = lax.dot_general(w_ref[...], jnp.where(spread, 1.0, 0.0).astype(BF16), (((0,), (0,)), ((), ())),
                            preferred_element_type=F32)
    slot = over(lane_iota(p.width), heads)
    main_slot, rem_slot = modulo(slot, p.i_main), modulo(slot, p.i_rem)
    at = lane_iota(SUBLANES)
    pieces = []
    for h in range(p.split):
        main = jnp.zeros((p.cols, LANES), F32)
        rem = jnp.zeros((p.cols, LANES), F32)
        for m in range(p.half):
            i = h * p.late + m
            block = normed[i * p.cols:(i + 1) * p.cols].astype(BF16)
            if m < p.i_main:
                main += dot(block, jnp.where(main_slot == m, tiled, 0.0).astype(BF16))
            else:
                rem += dot(block, jnp.where(rem_slot == m - p.i_main, tiled, 0.0).astype(BF16))
        blocks = [jnp.zeros((SUBLANES, LANES), F32) for _ in range(p.tall + 1)]
        for value, places, wide in ((main, p.main_at, p.main), (rem, p.rem_at, p.rem)):
            for g, (b, lane) in enumerate(places):
                here = (at >= lane) & (at < lane + wide)
                blocks[b] = jnp.where(here, value[g * SUBLANES:(g + 1) * SUBLANES], blocks[b])
        pieces.append(jnp.concatenate(blocks, axis=0).astype(BF16))
    for d in range(p.n):
        out_ref[d] = pieces[d % p.n_col % p.split]


def pick_half(p, second, rows):
    main, rest = [], []
    for r in range(p.n_row):
        a, b = r * p.rows, r * p.rows + p.late
        main.append(jnp.where(second, rows[b:b + p.i_main], rows[a:a + p.i_main]))
        rest.append(jnp.where(second, rows[b + p.i_main:b + p.half], rows[a + p.i_main:a + p.half]))
    return jnp.concatenate(main + rest, axis=0)


def project_kernel(p, col_ref, *refs):
    x_refs = refs[:p.n_col]
    w_ref, q_ref, k_ref, v_ref, gate_ref, x_out, hold = refs[p.n_col:]
    me = col_ref[0]
    second = lax.rem(me, p.split) == 1
    for shift in range(p.n_col):
        hold[lax.rem(me + (p.n_col - shift), p.n_col)] = x_refs[shift][...].astype(F32)
    f = p.feat
    for s in range(p.own):
        x = jnp.concatenate([hold[c, s] for c in range(p.n_col)], axis=0)
        normed = standardize_features(x)
        x_out[s] = pick_half(p, second, x).astype(BF16)
        lines = dot(normed.astype(BF16), w_ref[:, f:3 * f])
        k_ref[s] = lines[:, :f].astype(BF16)
        v_ref[s] = lines[:, f:].astype(BF16)
        normed = pick_half(p, second, normed).astype(BF16)
        gate_ref[s] = jax.nn.sigmoid(dot(normed, w_ref[:, 3 * f:]))
        q_ref[s] = (dot(normed, w_ref[:, :f]) * p.hd ** (-0.5)).astype(BF16)


def attend_kernel(p, col_ref, q_ref, k_ref, v_ref, gate_ref, x_ref, bias_ref, wf_ref, ws_ref,
                  emb_ref, side_ref, bias, four, lint, rint, send):
    h, t, f, m = p.heads, p.queries, p.feat, p.half
    at = lane_iota(SUBLANES)
    for first, places, wide in ((0, p.main_at, p.main), (p.n_row * p.main, p.rem_at, p.rem)):
        fold = LANES // wide
        slot = over(at, wide)
        for c in range(p.n_col):
            for b in range(p.n_row // fold):
                for g, (block, lane) in enumerate(places):
                    built = None
                    for u in range(fold):
                        piece = bias_ref[(b * fold + u) * p.n_col + c,
                                         block * SUBLANES:(block + 1) * SUBLANES].astype(F32)
                        turn = (u * wide - lane) % LANES
                        piece = pltpu.roll(piece, turn, axis=1) if turn else piece
                        built = piece if u == 0 else jnp.where(slot == u, piece, built)
                    row = c * p.cols + g * SUBLANES
                    bias[row:row + SUBLANES, first + b * LANES:first + (b + 1) * LANES] = built
    wide = t * h
    own_head = over(row_iota(f, wide), p.hd) == modulo(lane_iota(f, wide), h)
    pick = jnp.where(over(lane_iota(t, wide), h) == row_iota(t, wide), 1.0, 0.0).astype(BF16)
    head_mask = jnp.where(over(lane_iota(h, f), p.hd) == row_iota(h, f), 1.0, 0.0)
    new = []
    for s in range(p.own):
        q = q_ref[s].astype(F32)
        spread = (jnp.broadcast_to(q[:, None, :], (t, h, f)) * head_mask[None]).reshape(wide, f).astype(BF16)
        scores = dot_nt(k_ref[s], spread) + bias[...]
        peak = jnp.max(scores, axis=0, keepdims=True)
        weights = jnp.exp(scores - peak)
        total = jnp.sum(weights, axis=0, keepdims=True)
        v_t = jnp.transpose(v_ref[s].astype(F32)).astype(BF16)
        mixed = dot(v_t, weights.astype(BF16)) * (1.0 / total)
        mixed = jnp.where(own_head, mixed, 0.0).astype(BF16)
        new.append((gate_ref[s] * dot_nt(pick, mixed)).astype(BF16))
    new = dot(jnp.concatenate(new, axis=0), wf_ref[...])
    new = (x_ref[...].astype(F32).reshape(p.own * t, f) + new).astype(BF16).astype(F32)
    a, b = p.per * p.i_main, p.per * p.i_rem
    for s in range(p.own):
        for c in range(p.n_col):
            row, tail = s * t + c * a, s * t + p.n_row * p.i_main + c * b
            emb_ref[c, s] = jnp.concatenate([new[row:row + a], new[tail:tail + b]], axis=0).astype(BF16)
    sides = dot(standardize_features(new).astype(BF16), ws_ref[...])
    four[0] = sides[:, :LANES]
    four[1] = sides[:, LANES:]
    n4 = t // p.pack
    lane = over(lane_iota(n4), p.outer)
    for s in range(p.own):
        for side, woven in enumerate((lint, rint)):
            packed = four[side, pl.ds(s * t, n4, stride=p.pack), :]
            for a in range(1, p.pack):
                packed = jnp.where(lane == a, four[side, pl.ds(s * t + a, n4, stride=p.pack), :], packed)
            woven[pl.ds(s, n4, stride=p.own), :] = packed
    o = p.own

    def place(r, k):
        return (r * p.km + k if k < p.km else p.n_row * p.km + r * (p.hk - p.km) + k - p.km) * o

    def fill(left, right):
        for r in range(p.n_row):
            for c in range(p.n_col):
                d, row = r * p.n_col + c, 0
                spans = [(lint, place(r, k)) for k in left]
                spans += [(rint, place(c * p.per + u, k)) for u in range(p.per) for k in right]
                for source, start in spans:
                    send[d, row:row + o] = source[start:start + o]
                    row += o
                if row < p.side_rows:
                    send[d, row:p.side_rows] = jnp.zeros((p.side_rows - row, LANES), F32)

    second = lax.rem(col_ref[0], p.split) == 1

    @pl.when(jnp.logical_not(second))
    def _():
        fill(range(p.ek), range(p.hk))

    @pl.when(second)
    def _():
        fill(range(p.hk), range(p.hk - p.ek, p.hk))

    side_ref[...] = send[...].astype(BF16)


def home_kernel(p, col_ref, *refs):
    part_refs = refs[:p.n_col]
    out_ref, hold = refs[p.n_col:]
    me = col_ref[0]
    for shift in range(p.n_col):
        hold[lax.rem(me + (p.n_col - shift), p.n_col)] = part_refs[shift][...].astype(F32)
    both = 2 * p.half - p.rows
    tail = p.per * p.i_main
    for g in range(p.n_group):
        for s in range(p.own):
            rows = []
            for u in range(p.per):
                for skip, half in ((0, hold[g * p.split, s]), (both, hold[g * p.split + 1, s])):
                    rows.append(half[u * p.i_main + min(skip, p.i_main):(u + 1) * p.i_main])
                    rows.append(half[tail + u * p.i_rem + max(skip - p.i_main, 0):tail + (u + 1) * p.i_rem])
            rows = [value for value in rows if value.shape[0]]
            out_ref[g * p.own + s] = jnp.concatenate(rows, axis=0).astype(BF16)


def outer_kernel(p, recv_ref, pair_ref, w_ref, wv_ref, wg_ref, mid_ref, edge_ref,
                 flat, rt, lhs, mid):
    flat[...] = recv_ref[...].reshape(p.n * p.side_rows, LANES).astype(F32)

    def chunk(h, k):
        return jnp.concatenate(
            [flat[pl.ds(h * p.side_rows + k * p.own + s, p.n // p.split, stride=p.split * p.side_rows), :]
             for s in range(p.own)], axis=0)

    hk, ek = p.hk, p.ek
    for u in range(p.per):
        for k in range(p.lk):
            value = chunk(0, ek + u * hk + k) if k < hk else chunk(1, hk + u * ek + k - hk)
            row = (u * p.lk + k) * LANES
            rt[row:row + LANES, :] = jnp.transpose(value)
    right = []
    for first in range(0, p.outer, p.pack):
        right.append(jnp.concatenate(
            [rt[pl.ds(first + d, p.cols, stride=p.outer), :] for d in range(p.pack)], axis=1))
    right = jnp.concatenate(right, axis=0).astype(BF16)
    at = over(lane_iota(p.seq_total), p.outer)
    left = []
    for g in range(p.lk):
        base = chunk(0, g) if g < ek else chunk(1, g - ek)
        turned = [base] + [pltpu.roll(base, t * p.outer, axis=1) for t in range(1, p.pack)]
        for a in range(p.pack):
            left.append(jnp.concatenate(
                [jnp.where(at == d, turned[(d - a) % p.pack], 0.0) for d in range(p.pack)], axis=0).astype(BF16))
    products = dot(right, jnp.concatenate(left, axis=1)) * (1.0 / p.seq_total)
    for i in range(p.rows):
        for g in range(p.outer // p.pack):
            lhs[i * p.cpad:i * p.cpad + p.cols, g * LANES:(g + 1) * LANES] = products[
                g * p.cols:(g + 1) * p.cols, i * LANES:(i + 1) * LANES].astype(BF16)
        if p.cpad > p.cols:
            lhs[i * p.cpad + p.cols:(i + 1) * p.cpad, :] = jnp.zeros((p.cpad - p.cols, lhs.shape[1]), BF16)
    update = dot(lhs[...], w_ref[...])
    for i in range(p.rows):
        fresh = (pair_ref[i].astype(F32) + update[i * p.cpad:i * p.cpad + p.cols]).astype(BF16)
        mid_ref[i] = fresh
        mid[i * p.cols:(i + 1) * p.cols, :] = fresh.astype(F32)
    tail = mid.shape[0] - p.rows * p.cols
    mid[p.rows * p.cols:, :] = jnp.zeros((tail, LANES), F32)
    step = p.q * p.cols
    for k in range(p.ig):
        normed = standardize_features(mid[k * step:k * step + LANES, :]).astype(BF16)
        value = dot_nt(wv_ref[...], normed)
        gate = jax.nn.sigmoid(dot_nt(wg_ref[...], normed))
        edge_ref[:, k * SUBLANES:(k + 1) * SUBLANES, :] = (gate * value).reshape(
            p.n, SUBLANES, LANES).astype(BF16)


def gate_kernel(p, mid_ref, w_ref, out_ref):
    normed = standardize_features(mid_ref[...]).reshape(p.rows * p.cols, p.width).astype(BF16)
    out_ref[...] = jax.nn.sigmoid(dot(normed, w_ref[...]))


def triangle_kernel(p, recv_ref, out_ref, flat, ls, rs, os, sb):
    for r in range(p.n_row):
        for c in range(p.n_col):
            flat[c, r * p.edge_rows:(r + 1) * p.edge_rows, :] = recv_ref[r * p.n_col + c].astype(F32)
    lane = lane_iota(p.m)
    part_of = jnp.broadcast_to(lane_iota(1) // p.jslot, (p.m, LANES))
    blocks = p.per * p.ig
    rs[...] = jnp.zeros_like(rs)
    for ch in range(p.ch):
        for c in range(p.n_col):
            left = flat[c, pl.ds(ch, p.m, stride=SUBLANES), :]
            right = flat[c, pl.ds(p.ch + ch, p.m, stride=SUBLANES), :]
            for a in range(p.q):
                turn = (-a * p.cols) % LANES
                lt = pltpu.roll(left, turn, axis=1) if turn else left
                rt = pltpu.roll(right, turn, axis=1) if turn else right
                ls[ch, c, pl.ds(a, p.m, stride=p.q), :] = jnp.where(lane < p.cols, lt, 0.0)
                for first in range(0, p.n_col, p.q):
                    many = min(p.q, p.n_col - first) * blocks
                    rs[ch, c, pl.ds(p.j_base(first) + a, many, stride=p.q), :] = rt[
                        first * blocks:first * blocks + many]
    for ch in range(p.ch):
        lfull = jnp.concatenate([ls[ch, c] for c in range(p.n_col)], axis=1).astype(BF16)
        rfull = jnp.concatenate([rs[ch, c] for c in range(p.n_col)], axis=1).astype(BF16)
        summed = dot_nt(lfull, rfull)
        for b in range(summed.shape[1] // LANES):
            os[ch, b] = summed[:, b * LANES:(b + 1) * LANES]
        rows = [[os[ch, b, pl.ds(a, p.m, stride=p.q), :] for a in range(p.q)]
                for b in range(summed.shape[1] // LANES)]
        for c in range(p.n_col):
            b, part = c // p.q, c % p.q
            packed = None
            for a in range(p.q):
                turn = ((a - part) * p.jslot) % LANES
                piece = pltpu.roll(rows[b][a], turn, axis=1) if turn else rows[b][a]
                packed = piece if packed is None else jnp.where(part_of == a, piece, packed)
            sb[c, pl.ds(ch, p.m, stride=p.ch), :] = packed
    used = p.ig * p.ch
    for r in range(p.n_row):
        for c in range(p.n_col):
            d = r * p.n_col + c
            out_ref[d, 0:used] = sb[c, r * used:(r + 1) * used, :].astype(BF16)
            if used < p.back_rows:
                out_ref[d, used:p.back_rows] = jnp.zeros((p.back_rows - used, LANES), BF16)


def final_kernel(p, recv_ref, mid_ref, gate_ref, w_ref, out_ref, flat, hold, update):
    flat[...] = recv_ref[...].reshape(p.n * p.back_rows, LANES).astype(F32)
    for k in range(p.ig):
        summed = jnp.concatenate(
            [flat[pl.ds(k * p.ch + ch, p.n, stride=p.back_rows), :] for ch in range(p.ch)], axis=0)
        normed = jnp.transpose(standardize_features(summed, axis=0)).astype(BF16)
        hold[...] = dot(normed, w_ref[...])
        for a in range(p.q):
            i = k * p.q + a
            if i < p.rows:
                for u in range(p.per):
                    update[i * p.cols + u * p.rows:i * p.cols + (u + 1) * p.rows, :] = hold[
                        a * p.jslot + u * p.ipad:a * p.jslot + u * p.ipad + p.rows, :]
    fresh = mid_ref[...].astype(F32).reshape(p.rows * p.cols, p.width) + gate_ref[...] * update[...]
    out_ref[...] = fresh.reshape(p.rows, p.cols, p.width).astype(BF16)


def fast(p, x, pair, w_in, w_out, w_bias, w_side, w_outer, w_tri, w_last):
    col = lax.axis_index("col")
    n, ch, width = p.n, p.ch, p.width
    sds = jax.ShapeDtypeStruct

    side_w = jnp.concatenate([w_side[:, :p.outer]] * p.pack + [w_side[:, p.outer:]] * p.pack, axis=1)
    by_d = jnp.transpose(w_outer.reshape(p.outer, p.outer, width), (1, 0, 2)).reshape(w_outer.shape)
    blocks = jnp.transpose(w_tri.reshape(width, 5, width), (1, 2, 0)).reshape(5, n, ch, width)
    value_w = jnp.concatenate([blocks[0], blocks[2]], axis=1).reshape(n * 2 * ch, width)
    gate_w = jnp.concatenate([blocks[1], blocks[3]], axis=1).reshape(n * 2 * ch, width)
    own_gate_w = w_tri[:, 4 * width:]
    last_w = jnp.transpose(w_last.reshape(n, ch, width), (1, 0, 2)).reshape(width, width)

    piece = call(functools.partial(bias_kernel, p), sds((n, p.bias_rows, LANES), BF16), [], [VMEM] * 2, "bias")(
        pair.reshape(p.rows * p.cols, width), w_bias.T)
    bias = lax.all_to_all(piece, ALL, 0, 0, tiled=True)
    def ring(send):
        parts = []
        for shift in range(p.n_col):
            part = send(lax.rem(col + shift, p.n_col))
            if shift:
                part = lax.ppermute(part, "col", [(c, (c + shift) % p.n_col) for c in range(p.n_col)])
            parts.append(part)
        return parts

    at = col.reshape(1)
    chunks = x.reshape(p.n_group, p.own, p.res, p.feat)
    parts = ring(lambda to: lax.dynamic_index_in_dim(chunks, to // p.split, 0, keepdims=False))
    mine, every = (p.own, p.queries, p.feat), (p.own, p.total, p.feat)
    q, k, v, gate, rest = call(
        functools.partial(project_kernel, p),
        (sds(mine, BF16), sds(every, BF16), sds(every, BF16), sds(mine, F32), sds(mine, BF16)),
        [pltpu.VMEM((p.n_col, p.own, p.res, p.feat), F32)],
        [SMEM] + [VMEM] * (p.n_col + 1), "project")(at, *parts, w_in)
    emb, sides = call(
        functools.partial(attend_kernel, p),
        (sds((p.n_col, p.own, p.per * p.half, p.feat), BF16), sds((n, p.side_rows, LANES), BF16)),
        [pltpu.VMEM((p.total, p.queries * p.heads), F32), pltpu.VMEM((2, p.own * p.queries, LANES), F32)]
        + [pltpu.VMEM((p.queries // p.pack * p.own, LANES), F32)] * 2
        + [pltpu.VMEM((n, p.side_rows, LANES), F32)],
        [SMEM] + [VMEM] * 8, "attend")(at, q, k, v, gate, rest, bias, w_out, side_w)

    sides = lax.all_to_all(sides, ALL, 0, 0, tiled=True)
    mid, edges = call(
        functools.partial(outer_kernel, p),
        (sds((p.rows, p.cols, width), BF16), sds((n, p.edge_rows, LANES), BF16)),
        [pltpu.VMEM((n * p.side_rows, LANES), F32),
         pltpu.VMEM((p.rk * LANES, p.seq_total), F32),
         pltpu.VMEM((p.rows * p.cpad, p.outer * p.outer), BF16),
         pltpu.VMEM(((p.ig - 1) * p.q * p.cols + LANES, LANES), F32)],
        [VMEM] * 5, "outer")(sides, pair, by_d, value_w, gate_w)

    edges = lax.all_to_all(edges, ALL, 0, 0, tiled=True)
    out_gate = call(functools.partial(gate_kernel, p), sds((p.rows * p.cols, width), F32), [], [VMEM] * 2, "gate")(
        mid, own_gate_w)
    n_lane = p.j_base(p.n_col - 1) // LANES + 1
    back = call(
        functools.partial(triangle_kernel, p), sds((n, p.back_rows, LANES), BF16),
        [pltpu.VMEM((p.n_col, p.n_row * p.edge_rows, LANES), F32),
         pltpu.VMEM((ch, p.n_col, p.m * p.q, LANES), F32),
         pltpu.VMEM((ch, p.n_col, n_lane * LANES, LANES), F32),
         pltpu.VMEM((ch, n_lane, p.m * p.q, LANES), F32),
         pltpu.VMEM((p.n_col, p.m * ch, LANES), F32)],
        [VMEM], "triangle")(edges)

    parts = ring(lambda to: lax.dynamic_index_in_dim(emb, to, 0, keepdims=False))
    home = call(functools.partial(home_kernel, p), sds(x.shape, BF16),
                [pltpu.VMEM((p.n_col, p.own, p.per * p.half, p.feat), F32)],
                [SMEM] + [VMEM] * p.n_col, "home")(at, *parts)

    back = lax.all_to_all(back, ALL, 0, 0, tiled=True)
    state = call(
        functools.partial(final_kernel, p), sds((p.rows, p.cols, width), BF16),
        [pltpu.VMEM((n * p.back_rows, LANES), F32), pltpu.VMEM((LANES, LANES), F32),
         pltpu.VMEM((p.rows * p.cols, LANES), F32)],
        [VMEM] * 4, "final")(back, mid, out_gate, last_w)
    return home, state


def general(
    stack_embedding,
    pair_representation,
    mixing_entry_coefficients,
    mixing_final_coefficients,
    pair_bias_matrix,
    tensor_side_coefficients,
    outer_output_weight,
    triangle_projection_weight,
    triangle_output_weight,
):
    sequences_per_device, residues_per_device, alignment_channels = stack_embedding.shape
    rows_dev = pair_representation.shape[0]
    pair_width = pair_representation.shape[2]
    number_heads = pair_bias_matrix.shape[1]
    head_channels = alignment_channels // number_heads
    outer_width = tensor_side_coefficients.shape[1] // 2
    row_count = lax.axis_size("row")
    seq_total = sequences_per_device * row_count
    row_index = lax.axis_index("row")
    normalized_input = (
        standardize_features(stack_embedding).astype(jnp.bfloat16).reshape(-1, alignment_channels)
    )
    mapped_lines = jnp.dot(
        normalized_input, mixing_entry_coefficients, preferred_element_type=jnp.float32
    )
    stack_probe_vectors = (
        (mapped_lines[:, :alignment_channels] * head_channels ** (-0.5))
        .astype(jnp.bfloat16)
        .reshape(sequences_per_device, residues_per_device, number_heads, head_channels)
    )
    stack_lookup_vectors = (
        mapped_lines[:, alignment_channels : 2 * alignment_channels]
        .astype(jnp.bfloat16)
        .reshape(sequences_per_device, residues_per_device, alignment_channels)
    )
    stack_content_vectors = (
        mapped_lines[:, 2 * alignment_channels : 3 * alignment_channels]
        .astype(jnp.bfloat16)
        .reshape(sequences_per_device, residues_per_device, alignment_channels)
    )
    sigmoid_factors = jax.nn.sigmoid(mapped_lines[:, 3 * alignment_channels :]).reshape(
        sequences_per_device, residues_per_device, alignment_channels
    )
    pair_normed = standardize_features(pair_representation).astype(jnp.bfloat16)
    bias_local = jnp.einsum(
        "ijc,ch->hij", pair_normed, pair_bias_matrix, preferred_element_type=jnp.float32
    ).astype(jnp.bfloat16)
    bias_all = lax.all_gather(bias_local, "row", axis=1, tiled=True)
    bias_query = lax.all_to_all(bias_all, "col", split_axis=1, concat_axis=2, tiled=True)
    best_score = jnp.full(
        (sequences_per_device, number_heads, residues_per_device), -1e30, jnp.float32
    )
    received_keys = lax.all_gather(stack_lookup_vectors, "col", axis=1, tiled=True)
    received_values = lax.all_gather(stack_content_vectors, "col", axis=1, tiled=True)
    key_count = received_keys.shape[1]
    received_keys = received_keys.reshape(
        sequences_per_device, key_count, number_heads, head_channels
    )
    received_values = received_values.reshape(
        sequences_per_device, key_count, number_heads, head_channels
    )
    bias_piece = bias_query.astype(jnp.float32)
    scores = (
        jnp.einsum(
            "yeca,yica->ycei",
            stack_probe_vectors,
            received_keys,
            preferred_element_type=jnp.float32,
        )
        + bias_piece[None]
    )
    next_best = jnp.maximum(best_score, jnp.max(scores, axis=-1))
    weights = jnp.exp(scores - next_best[..., None])
    next_sum = jnp.sum(weights, axis=-1)
    update = jnp.einsum(
        "shqk,skhd->sqhd",
        weights.astype(jnp.bfloat16),
        received_values,
        preferred_element_type=jnp.float32,
    )
    weighted_mixture = (update / jnp.transpose(next_sum, (0, 2, 1))[..., None]).reshape(
        sequences_per_device, residues_per_device, alignment_channels
    )
    scaled_mixture = (sigmoid_factors * weighted_mixture).astype(jnp.bfloat16)
    stack_increment = jnp.dot(
        scaled_mixture.reshape(-1, alignment_channels),
        mixing_final_coefficients,
        preferred_element_type=jnp.float32,
    ).reshape(sequences_per_device, residues_per_device, alignment_channels)
    stack_embedding_updated = (stack_embedding.astype(jnp.float32) + stack_increment).astype(
        jnp.bfloat16
    )
    tensor_standardized = (
        standardize_features(stack_embedding_updated)
        .astype(jnp.bfloat16)
        .reshape(-1, alignment_channels)
    )
    sides = jnp.dot(
        tensor_standardized, tensor_side_coefficients, preferred_element_type=jnp.float32
    ).astype(jnp.bfloat16)
    sides = sides.reshape(sequences_per_device, residues_per_device, 2 * outer_width)
    left_side = sides[..., :outer_width]
    right_side = sides[..., outer_width:]
    left_wide = lax.all_gather(left_side, "col", axis=1, tiled=True)
    left_every, right_all = (
        lax.all_gather(left_wide, "row", axis=0, tiled=True),
        lax.all_gather(right_side, "row", axis=0, tiled=True),
    )
    left_all = lax.dynamic_slice_in_dim(left_every, row_index * rows_dev, rows_dev, 1)
    products = jnp.einsum("sic,sjd->ijcd", left_all, right_all, preferred_element_type=jnp.float32)
    averaged = (products * (1.0 / seq_total)).astype(jnp.bfloat16)
    outer_update = jnp.dot(
        averaged.reshape(-1, outer_width * outer_width),
        outer_output_weight,
        preferred_element_type=jnp.float32,
    )
    pair_mid = (
        pair_representation.astype(jnp.float32)
        + outer_update.reshape(rows_dev, residues_per_device, pair_width)
    ).astype(jnp.bfloat16)
    tri_normed = standardize_features(pair_mid).astype(jnp.bfloat16).reshape(-1, pair_width)
    tri_parts = jnp.dot(
        tri_normed, triangle_projection_weight, preferred_element_type=jnp.float32
    ).reshape(rows_dev, residues_per_device, 5 * pair_width)
    left_edge = (
        jax.nn.sigmoid(tri_parts[..., pair_width : 2 * pair_width]) * tri_parts[..., :pair_width]
    ).astype(jnp.bfloat16)
    right_edge = (
        jax.nn.sigmoid(tri_parts[..., 3 * pair_width : 4 * pair_width])
        * tri_parts[..., 2 * pair_width : 3 * pair_width]
    ).astype(jnp.bfloat16)
    out_gate = jax.nn.sigmoid(tri_parts[..., 4 * pair_width :])
    right_rows = lax.all_gather(right_edge, "row", axis=0, tiled=True)
    right_query = lax.all_to_all(right_rows, "col", split_axis=0, concat_axis=1, tiled=True)
    arrived = lax.all_gather(left_edge, "col", axis=1, tiled=True)
    summed = jnp.einsum("ikc,jkc->ijc", arrived, right_query, preferred_element_type=jnp.float32)
    tri_ln = standardize_features(summed).astype(jnp.bfloat16)
    tri_update = jnp.dot(
        tri_ln.reshape(-1, pair_width), triangle_output_weight, preferred_element_type=jnp.float32
    ).reshape(rows_dev, residues_per_device, pair_width)
    pair_state_next = (pair_mid.astype(jnp.float32) + out_gate * tri_update).astype(jnp.bfloat16)
    return (stack_embedding_updated, pair_state_next)


def shards(x, pair, w_in, w_out, w_bias, w_side, w_outer, w_tri, w_last):
    p = Plan(lax.axis_size("row"), lax.axis_size("col"), x.shape, pair.shape, w_bias.shape[1],
             w_side.shape[1] // 2, w_last.shape[1])
    path = functools.partial(fast, p) if p.ok else general
    return path(x, pair, w_in, w_out, w_bias, w_side, w_outer, w_tri, w_last)


def solution(mesh):
    return jax.shard_map(
        shards,
        mesh=mesh,
        in_specs=(P("row", "col", None), P("row", "col", None), P(), P(), P(), P(), P(), P(), P()),
        out_specs=(P("row", "col", None), P("row", "col", None)),
        check_vma=False,
    )
```

```python
import functools

import jax
import jax.numpy as jnp
from jax import lax
from jax.experimental import pallas as pl
from jax.experimental.pallas import tpu as pltpu
from jax.sharding import PartitionSpec as P

epsilon = 1e-05
LANES = 128
MOST_VMEM = 67_043_328
SUBLANES = 8
F32 = jnp.float32
BF16 = jnp.bfloat16
ALL = ("row", "col")
NT = (((1,), (1,)), ((), ()))
VMEM = pl.BlockSpec(memory_space=pltpu.VMEM)
SMEM = pl.BlockSpec(memory_space=pltpu.SMEM)
HBM = pl.BlockSpec(memory_space=pltpu.HBM)


def standardize_features(inputs, axis=-1):
    inputs = inputs.astype(jnp.float32)
    center = inputs - jnp.mean(inputs, axis=axis, keepdims=True)
    spread = jnp.mean(center * center, axis=axis, keepdims=True)
    return center * lax.rsqrt(spread + epsilon)


def dot(a, b):
    return jnp.dot(a, b, preferred_element_type=F32)


def dot_nt(a, b):
    return lax.dot_general(a, b, NT, preferred_element_type=F32)


def lane_iota(rows, width=LANES):
    return lax.broadcasted_iota(jnp.int32, (rows, width), 1)


def row_iota(rows, width=LANES):
    return lax.broadcasted_iota(jnp.int32, (rows, width), 0)


def over(index, size):
    return lax.shift_right_logical(index, jnp.int32(size.bit_length() - 1))


def modulo(index, size):
    return lax.bitwise_and(index, jnp.int32(size - 1))


def call(body, out_shape, scratch, in_specs, name, limit=24, out_spec=VMEM):
    return pl.pallas_call(
        body,
        out_shape=out_shape,
        in_specs=in_specs,
        out_specs=out_spec if isinstance(out_spec, tuple) else jax.tree.map(lambda _: out_spec, out_shape),
        scratch_shapes=scratch,
        name=name,
        cost_estimate=pl.CostEstimate(flops=400_000_000, bytes_accessed=4_000_000, transcendentals=0),
        compiler_params=pltpu.CompilerParams(vmem_limit_bytes=min(limit * 1024 * 1024, MOST_VMEM)),
    )


class Plan:
    def __init__(self, n_row, n_col, x, pair, heads, outer, channels_out):
        self.n_row, self.n_col, self.n = n_row, n_col, n_row * n_col
        self.seqs, self.res, self.feat = x
        self.rows, self.cols, self.width = pair
        self.heads, self.outer = heads, outer
        self.hd = self.feat // heads
        self.total = self.res * n_col
        self.ok = False
        if any(size & (size - 1) for size in (heads, outer, self.hd, n_row, n_col)):
            return
        if self.seqs % n_col or self.width != LANES or heads != SUBLANES or self.cols != self.res:
            return
        if self.rows * n_row != self.total or self.feat % LANES:
            return
        self.split = 2
        if n_col % self.split:
            return
        self.n_group = n_col // self.split
        self.own = self.seqs // self.n_group
        self.seq_total = self.own * self.n_group * n_row
        if LANES % outer or outer % (LANES // outer):
            return
        self.pack = LANES // outer
        if self.rows % self.pack or self.cols % self.pack:
            return
        self.half = -(-self.rows // (self.split * self.pack)) * self.pack
        self.late = self.rows - self.half
        self.queries = n_row * self.half
        self.i_main = LANES // heads // 2
        self.i_rem = self.half - self.i_main
        if not 0 < self.i_rem or self.i_main % self.pack or self.i_rem % self.pack or LANES % (self.i_rem * heads) or self.cols % SUBLANES:
            return
        self.km = self.i_main // self.pack
        self.main, self.rem = self.i_main * heads, self.i_rem * heads
        self.groups = self.cols // SUBLANES
        self.tall = -(-self.groups // 2)
        self.fold = LANES // self.rem
        if n_row % 2 or n_row % self.fold:
            return
        self.main_at = [(g % self.tall, g // self.tall * self.main) for g in range(self.groups)]
        spare = [(self.tall, f * self.rem) for f in range(self.fold)]
        if self.groups % 2:
            spare += [(self.tall - 1, self.main + f * self.rem) for f in range(self.main // self.rem)]
        if len(spare) < self.groups:
            return
        self.rem_at = spare[:self.groups]
        self.bias_rows = (self.tall + 1) * SUBLANES
        self.per = n_row // n_col
        if n_row % n_col or self.per * self.rows != self.cols:
            return
        self.lk, self.rk = self.rows // self.pack, self.cols // self.pack
        self.hk = self.half // self.pack
        self.ek = self.lk - self.hk
        chunks = max(self.ek + self.per * self.hk, self.hk + self.per * self.ek)
        self.side_rows = -(-chunks * self.own // 16) * 16
        self.cpad = -(-self.cols // 16) * 16
        if self.width % self.n:
            return
        self.ch = self.width // self.n
        if 2 * self.ch != SUBLANES:
            return
        self.q = LANES // self.cols
        self.ig = -(-self.rows // self.q)
        self.ipad = self.ig * self.q
        self.jslot = self.per * self.ipad
        if self.q * self.jslot > LANES:
            return
        self.m = n_row * self.ig
        self.edge_rows = self.ig * SUBLANES
        self.ok = True

    def j_base(self, c):
        return (c // self.q) * LANES + (c % self.q) * self.jslot


def bias_kernel(p, pair_hbm, w_hbm, out_hbm, pair_ref, w_ref, piece_ref, sems, out_sems):
    copies = [pltpu.make_async_copy(pair_hbm, pair_ref, sems.at[0]), pltpu.make_async_copy(w_hbm, w_ref, sems.at[1])]
    for copy in copies:
        copy.start()
    for copy in copies:
        copy.wait()
    normed = standardize_features(pair_ref[...]).reshape(p.rows * p.cols, p.width)
    heads = p.heads
    spread = modulo(lane_iota(heads), heads) == row_iota(heads)
    tiled = lax.dot_general(w_ref[...], jnp.where(spread, 1.0, 0.0).astype(BF16), (((0,), (0,)), ((), ())),
                            preferred_element_type=F32)
    slot = over(lane_iota(p.width), heads)
    main_slot, rem_slot = modulo(slot, p.i_main), modulo(slot, p.i_rem)
    at = lane_iota(SUBLANES)
    pieces = []
    for h in range(p.split):
        main = jnp.zeros((p.cols, LANES), F32)
        rem = jnp.zeros((p.cols, LANES), F32)
        for m in range(p.half):
            i = h * p.late + m
            block = normed[i * p.cols:(i + 1) * p.cols].astype(BF16)
            if m < p.i_main:
                main += dot(block, jnp.where(main_slot == m, tiled, 0.0).astype(BF16))
            else:
                rem += dot(block, jnp.where(rem_slot == m - p.i_main, tiled, 0.0).astype(BF16))
        blocks = [jnp.zeros((SUBLANES, LANES), F32) for _ in range(p.tall + 1)]
        for value, places, wide in ((main, p.main_at, p.main), (rem, p.rem_at, p.rem)):
            for g, (b, lane) in enumerate(places):
                here = (at >= lane) & (at < lane + wide)
                blocks[b] = jnp.where(here, value[g * SUBLANES:(g + 1) * SUBLANES], blocks[b])
        piece_ref[h] = jnp.concatenate(blocks, axis=0).astype(BF16)
        for d in range(p.n):
            if d % p.n_col % p.split == h:
                pieces.append(pltpu.make_async_copy(piece_ref.at[h], out_hbm.at[d], out_sems.at[d]))
                pieces[-1].start()
    for copy in pieces:
        copy.wait()


def pick_half(p, second, rows):
    main, rest = [], []
    for r in range(p.n_row):
        a, b = r * p.rows, r * p.rows + p.late
        main.append(jnp.where(second, rows[b:b + p.i_main], rows[a:a + p.i_main]))
        rest.append(jnp.where(second, rows[b + p.i_main:b + p.half], rows[a + p.i_main:a + p.half]))
    return jnp.concatenate(main + rest, axis=0)


def project_kernel(p, col_ref, *refs):
    x_refs = refs[:p.n_col]
    w_ref, q_ref, k_ref, v_ref, gate_ref, x_out, hold = refs[p.n_col:]
    me = col_ref[0]
    second = lax.rem(me, p.split) == 1
    for shift in range(p.n_col):
        hold[lax.rem(me + (p.n_col - shift), p.n_col)] = x_refs[shift][...].astype(F32)
    f = p.feat
    for s in range(p.own):
        x = jnp.concatenate([hold[c, s] for c in range(p.n_col)], axis=0)
        normed = standardize_features(x)
        x_out[s] = pick_half(p, second, x).astype(BF16)
        lines = dot(normed.astype(BF16), w_ref[:, f:3 * f])
        k_ref[s] = lines[:, :f].astype(BF16)
        v_ref[s] = lines[:, f:].astype(BF16)
        normed = pick_half(p, second, normed).astype(BF16)
        gate_ref[s] = jax.nn.sigmoid(dot(normed, w_ref[:, 3 * f:]))
        q_ref[s] = (dot(normed, w_ref[:, :f]) * p.hd ** (-0.5)).astype(BF16)


def attend_kernel(p, col_ref, q_ref, k_ref, v_ref, gate_ref, x_ref, bias_ref, wf_ref, ws_ref,
                  emb_ref, side_hbm, bias, four, lint, rint, send, side_ref, sems):
    h, t, f, m = p.heads, p.queries, p.feat, p.half
    at = lane_iota(SUBLANES)
    for first, places, wide in ((0, p.main_at, p.main), (p.n_row * p.main, p.rem_at, p.rem)):
        fold = LANES // wide
        slot = over(at, wide)
        for c in range(p.n_col):
            for b in range(p.n_row // fold):
                for g, (block, lane) in enumerate(places):
                    built = None
                    for u in range(fold):
                        piece = bias_ref[(b * fold + u) * p.n_col + c,
                                         block * SUBLANES:(block + 1) * SUBLANES].astype(F32)
                        turn = (u * wide - lane) % LANES
                        piece = pltpu.roll(piece, turn, axis=1) if turn else piece
                        built = piece if u == 0 else jnp.where(slot == u, piece, built)
                    row = c * p.cols + g * SUBLANES
                    bias[row:row + SUBLANES, first + b * LANES:first + (b + 1) * LANES] = built
    wide = t * h
    own_head = over(row_iota(f, wide), p.hd) == modulo(lane_iota(f, wide), h)
    pick = jnp.where(over(lane_iota(t, wide), h) == row_iota(t, wide), 1.0, 0.0).astype(BF16)
    head_mask = jnp.where(over(lane_iota(h, f), p.hd) == row_iota(h, f), 1.0, 0.0)
    new = []
    for s in range(p.own):
        q = q_ref[s].astype(F32)
        spread = (jnp.broadcast_to(q[:, None, :], (t, h, f)) * head_mask[None]).reshape(wide, f).astype(BF16)
        scores = dot_nt(k_ref[s], spread) + bias[...]
        peak = jnp.max(scores, axis=0, keepdims=True)
        weights = jnp.exp(scores - peak)
        total = jnp.sum(weights, axis=0, keepdims=True)
        v_t = jnp.transpose(v_ref[s].astype(F32)).astype(BF16)
        mixed = dot(v_t, weights.astype(BF16)) * (1.0 / total)
        mixed = jnp.where(own_head, mixed, 0.0).astype(BF16)
        new.append((gate_ref[s] * dot_nt(pick, mixed)).astype(BF16))
    new = dot(jnp.concatenate(new, axis=0), wf_ref[...])
    new = (x_ref[...].astype(F32).reshape(p.own * t, f) + new).astype(BF16).astype(F32)
    a, b = p.per * p.i_main, p.per * p.i_rem
    for s in range(p.own):
        for c in range(p.n_col):
            row, tail = s * t + c * a, s * t + p.n_row * p.i_main + c * b
            emb_ref[c, s] = jnp.concatenate([new[row:row + a], new[tail:tail + b]], axis=0).astype(BF16)
    sides = dot(standardize_features(new).astype(BF16), ws_ref[...])
    four[0] = sides[:, :LANES]
    four[1] = sides[:, LANES:]
    n4 = t // p.pack
    lane = over(lane_iota(n4), p.outer)
    for s in range(p.own):
        for side, woven in enumerate((lint, rint)):
            packed = four[side, pl.ds(s * t, n4, stride=p.pack), :]
            for a in range(1, p.pack):
                packed = jnp.where(lane == a, four[side, pl.ds(s * t + a, n4, stride=p.pack), :], packed)
            woven[pl.ds(s, n4, stride=p.own), :] = packed
    o = p.own

    def place(r, k):
        return (r * p.km + k if k < p.km else p.n_row * p.km + r * (p.hk - p.km) + k - p.km) * o

    def fill(left, right):
        for r in range(p.n_row):
            for c in range(p.n_col):
                d, row = r * p.n_col + c, 0
                spans = [(lint, place(r, k)) for k in left]
                spans += [(rint, place(c * p.per + u, k)) for u in range(p.per) for k in right]
                for source, start in spans:
                    send[d, row:row + o] = source[start:start + o]
                    row += o
                if row < p.side_rows:
                    send[d, row:p.side_rows] = jnp.zeros((p.side_rows - row, LANES), F32)
            block = slice(r * p.n_col, (r + 1) * p.n_col)
            side_ref[block] = send[block].astype(BF16)
            leave(r).start()

    def leave(r):
        block = pl.ds(r * p.n_col, p.n_col)
        return pltpu.make_async_copy(side_ref.at[block], side_hbm.at[block], sems.at[r])

    second = lax.rem(col_ref[0], p.split) == 1

    @pl.when(jnp.logical_not(second))
    def _():
        fill(range(p.ek), range(p.hk))

    @pl.when(second)
    def _():
        fill(range(p.hk), range(p.hk - p.ek, p.hk))

    for r in range(p.n_row):
        leave(r).wait()


def home_kernel(p, col_ref, *refs):
    part_refs = refs[:p.n_col]
    out_ref, hold = refs[p.n_col:]
    me = col_ref[0]
    for shift in range(p.n_col):
        hold[lax.rem(me + (p.n_col - shift), p.n_col)] = part_refs[shift][...].astype(F32)
    both = 2 * p.half - p.rows
    tail = p.per * p.i_main
    for g in range(p.n_group):
        for s in range(p.own):
            rows = []
            for u in range(p.per):
                for skip, half in ((0, hold[g * p.split, s]), (both, hold[g * p.split + 1, s])):
                    rows.append(half[u * p.i_main + min(skip, p.i_main):(u + 1) * p.i_main])
                    rows.append(half[tail + u * p.i_rem + max(skip - p.i_main, 0):tail + (u + 1) * p.i_rem])
            rows = [value for value in rows if value.shape[0]]
            out_ref[g * p.own + s] = jnp.concatenate(rows, axis=0).astype(BF16)


def outer_kernel(p, recv_ref, pair_ref, w_ref, wv_ref, wg_ref, wo_ref, mid_ref, edge_ref, gate_ref,
                 flat, rt, lhs, mid):
    flat[...] = recv_ref[...].reshape(p.n * p.side_rows, LANES).astype(F32)

    def chunk(h, k):
        return jnp.concatenate(
            [flat[pl.ds(h * p.side_rows + k * p.own + s, p.n // p.split, stride=p.split * p.side_rows), :]
             for s in range(p.own)], axis=0)

    hk, ek = p.hk, p.ek
    for u in range(p.per):
        for k in range(p.lk):
            value = chunk(0, ek + u * hk + k) if k < hk else chunk(1, hk + u * ek + k - hk)
            row = (u * p.lk + k) * LANES
            rt[row:row + LANES, :] = jnp.transpose(value)
    right = []
    for first in range(0, p.outer, p.pack):
        right.append(jnp.concatenate(
            [rt[pl.ds(first + d, p.cols, stride=p.outer), :] for d in range(p.pack)], axis=1))
    right = jnp.concatenate(right, axis=0).astype(BF16)
    at = over(lane_iota(p.seq_total), p.outer)
    left = []
    for g in range(p.lk):
        base = chunk(0, g) if g < ek else chunk(1, g - ek)
        turned = [base] + [pltpu.roll(base, t * p.outer, axis=1) for t in range(1, p.pack)]
        for a in range(p.pack):
            left.append(jnp.concatenate(
                [jnp.where(at == d, turned[(d - a) % p.pack], 0.0) for d in range(p.pack)], axis=0).astype(BF16))
    products = dot(right, jnp.concatenate(left, axis=1)) * (1.0 / p.seq_total)
    for i in range(p.rows):
        for g in range(p.outer // p.pack):
            lhs[i * p.cpad:i * p.cpad + p.cols, g * LANES:(g + 1) * LANES] = products[
                g * p.cols:(g + 1) * p.cols, i * LANES:(i + 1) * LANES].astype(BF16)
        if p.cpad > p.cols:
            lhs[i * p.cpad + p.cols:(i + 1) * p.cpad, :] = jnp.zeros((p.cpad - p.cols, lhs.shape[1]), BF16)
    update = dot(lhs[...], w_ref[...])
    for i in range(p.rows):
        fresh = (pair_ref[i].astype(F32) + update[i * p.cpad:i * p.cpad + p.cols]).astype(BF16)
        mid_ref[i] = fresh
        mid[i * p.cols:(i + 1) * p.cols, :] = fresh.astype(F32)
    tail = mid.shape[0] - p.rows * p.cols
    mid[p.rows * p.cols:, :] = jnp.zeros((tail, LANES), F32)
    step = p.q * p.cols
    for k in range(p.ig):
        normed = standardize_features(mid[k * step:k * step + LANES, :]).astype(BF16)
        value = dot_nt(wv_ref[...], normed)
        gate = jax.nn.sigmoid(dot_nt(wg_ref[...], normed))
        edge_ref[:, k * SUBLANES:(k + 1) * SUBLANES, :] = (gate * value).reshape(
            p.n, SUBLANES, LANES).astype(BF16)
        many = min(step, p.rows * p.cols - k * step)
        gate_ref[k * step:k * step + many, :] = jax.nn.sigmoid(dot(normed, wo_ref[...]))[:many]


def triangle_kernel(p, recv_ref, out_ref, flat, ls, rs, os, sb):
    for r in range(p.n_row):
        for c in range(p.n_col):
            flat[c, r * p.edge_rows:(r + 1) * p.edge_rows, :] = recv_ref[r * p.n_col + c].astype(F32)
    lane = lane_iota(p.m)
    part_of = jnp.broadcast_to(lane_iota(1) // p.jslot, (p.m, LANES))
    blocks = p.per * p.ig
    rs[...] = jnp.zeros_like(rs)
    for ch in range(p.ch):
        for c in range(p.n_col):
            left = flat[c, pl.ds(ch, p.m, stride=SUBLANES), :]
            right = flat[c, pl.ds(p.ch + ch, p.m, stride=SUBLANES), :]
            for a in range(p.q):
                turn = (-a * p.cols) % LANES
                lt = pltpu.roll(left, turn, axis=1) if turn else left
                rt = pltpu.roll(right, turn, axis=1) if turn else right
                ls[ch, c, pl.ds(a, p.m, stride=p.q), :] = jnp.where(lane < p.cols, lt, 0.0)
                for first in range(0, p.n_col, p.q):
                    many = min(p.q, p.n_col - first) * blocks
                    rs[ch, c, pl.ds(p.j_base(first) + a, many, stride=p.q), :] = rt[
                        first * blocks:first * blocks + many]
    for ch in range(p.ch):
        lfull = jnp.concatenate([ls[ch, c] for c in range(p.n_col)], axis=1).astype(BF16)
        rfull = jnp.concatenate([rs[ch, c] for c in range(p.n_col)], axis=1).astype(BF16)
        summed = dot_nt(lfull, rfull)
        for b in range(summed.shape[1] // LANES):
            os[ch, b] = summed[:, b * LANES:(b + 1) * LANES]
        rows = [[os[ch, b, pl.ds(a, p.m, stride=p.q), :] for a in range(p.q)]
                for b in range(summed.shape[1] // LANES)]
        for c in range(p.n_col):
            b, part = c // p.q, c % p.q
            packed = None
            for a in range(p.q):
                turn = ((a - part) * p.jslot) % LANES
                piece = pltpu.roll(rows[b][a], turn, axis=1) if turn else rows[b][a]
                packed = piece if packed is None else jnp.where(part_of == a, piece, packed)
            sb[c, pl.ds(ch, p.m, stride=p.ch), :] = packed
    for r in range(p.n_row):
        for c in range(p.n_col):
            for k in range(p.ig):
                row = (r * p.ig + k) * p.ch
                out_ref[r * p.n_col + c, k] = sb[c, row:row + p.ch, :].astype(BF16)


def final_kernel(p, recv_ref, mid_ref, gate_ref, w_ref, out_hbm, flat, hold, update, out_ref, sems):
    copies = []
    for k in range(p.ig):
        for d in range(p.n):
            flat[k, d * p.ch:(d + 1) * p.ch, :] = recv_ref[d, k].astype(F32)
    for k in range(p.ig):
        normed = jnp.transpose(standardize_features(flat[k], axis=0)).astype(BF16)
        hold[k] = dot(normed, w_ref[...])
        first, last = k * p.q, min((k + 1) * p.q, p.rows)
        for i in range(first, last):
            for u in range(p.per):
                row = (i - first) * p.jslot + u * p.ipad
                update[i * p.cols + u * p.rows:i * p.cols + (u + 1) * p.rows, :] = hold[k, row:row + p.rows, :]
        span = slice(first * p.cols, last * p.cols)
        fresh = mid_ref[first:last].astype(F32) + (gate_ref[span] * update[span]).reshape(
            last - first, p.cols, p.width)
        out_ref[first:last] = fresh.astype(BF16)
        rows = pl.ds(first, last - first)
        copies.append(pltpu.make_async_copy(out_ref.at[rows], out_hbm.at[rows], sems.at[k]))
        copies[-1].start()
    for copy in copies:
        copy.wait()


def fast(p, x, pair, w_in, w_out, w_bias, w_side, w_outer, w_tri, w_last):
    col = lax.axis_index("col")
    n, ch, width = p.n, p.ch, p.width
    sds = jax.ShapeDtypeStruct

    side_w = jnp.concatenate([w_side[:, :p.outer]] * p.pack + [w_side[:, p.outer:]] * p.pack, axis=1)
    by_d = jnp.transpose(w_outer.reshape(p.outer, p.outer, width), (1, 0, 2)).reshape(w_outer.shape)
    blocks = jnp.transpose(w_tri.reshape(width, 5, width), (1, 2, 0)).reshape(5, n, ch, width)
    value_w = jnp.concatenate([blocks[0], blocks[2]], axis=1).reshape(n * 2 * ch, width)
    gate_w = jnp.concatenate([blocks[1], blocks[3]], axis=1).reshape(n * 2 * ch, width)
    own_gate_w = w_tri[:, 4 * width:]

    piece = call(functools.partial(bias_kernel, p), sds((n, p.bias_rows, LANES), BF16),
                 [pltpu.VMEM(pair.shape, BF16), pltpu.VMEM((p.heads, width), BF16),
                  pltpu.VMEM((p.split, p.bias_rows, LANES), BF16), pltpu.SemaphoreType.DMA((2,)),
                  pltpu.SemaphoreType.DMA((n,))], [HBM] * 2, "bias", limit=64, out_spec=HBM)(pair, w_bias.T)
    bias = lax.all_to_all(piece, ALL, 0, 0, tiled=True)
    def ring(send):
        parts = []
        for shift in range(p.n_col):
            part = send(lax.rem(col + shift, p.n_col))
            if shift:
                part = lax.ppermute(part, "col", [(c, (c + shift) % p.n_col) for c in range(p.n_col)])
            parts.append(part)
        return parts

    at = col.reshape(1)
    chunks = x.reshape(p.n_group, p.own, p.res, p.feat)
    parts = ring(lambda to: lax.dynamic_index_in_dim(chunks, to // p.split, 0, keepdims=False))
    mine, every = (p.own, p.queries, p.feat), (p.own, p.total, p.feat)
    q, k, v, gate, rest = call(
        functools.partial(project_kernel, p),
        (sds(mine, BF16), sds(every, BF16), sds(every, BF16), sds(mine, F32), sds(mine, BF16)),
        [pltpu.VMEM((p.n_col, p.own, p.res, p.feat), F32)],
        [SMEM] + [VMEM] * (p.n_col + 1), "project")(at, *parts, w_in)
    emb, sides = call(
        functools.partial(attend_kernel, p),
        (sds((p.n_col, p.own, p.per * p.half, p.feat), BF16), sds((n, p.side_rows, LANES), BF16)),
        [pltpu.VMEM((p.total, p.queries * p.heads), F32), pltpu.VMEM((2, p.own * p.queries, LANES), F32)]
        + [pltpu.VMEM((p.queries // p.pack * p.own, LANES), F32)] * 2
        + [pltpu.VMEM((n, p.side_rows, LANES), F32), pltpu.VMEM((n, p.side_rows, LANES), BF16),
           pltpu.SemaphoreType.DMA((p.n_row,))],
        [SMEM] + [VMEM] * 8, "attend", out_spec=(VMEM, HBM))(at, q, k, v, gate, rest, bias, w_out, side_w)

    sides = lax.all_to_all(sides, ALL, 0, 0, tiled=True)

    parts = ring(lambda to: lax.dynamic_index_in_dim(emb, to, 0, keepdims=False))
    home = call(functools.partial(home_kernel, p), sds(x.shape, BF16),
                [pltpu.VMEM((p.n_col, p.own, p.per * p.half, p.feat), F32)],
                [SMEM] + [VMEM] * p.n_col, "home")(at, *parts)

    mid, edges, out_gate = call(
        functools.partial(outer_kernel, p),
        (sds((p.rows, p.cols, width), BF16), sds((n, p.edge_rows, LANES), BF16),
         sds((p.rows * p.cols, width), F32)),
        [pltpu.VMEM((n * p.side_rows, LANES), F32),
         pltpu.VMEM((p.rk * LANES, p.seq_total), F32),
         pltpu.VMEM((p.rows * p.cpad, p.outer * p.outer), BF16),
         pltpu.VMEM(((p.ig - 1) * p.q * p.cols + LANES, LANES), F32)],
        [VMEM] * 6, "outer")(sides, pair, by_d, value_w, gate_w, own_gate_w)

    edges, home = lax.optimization_barrier((edges, home))
    edges = lax.all_to_all(edges, ALL, 0, 0, tiled=True)
    n_lane = p.j_base(p.n_col - 1) // LANES + 1
    back = call(
        functools.partial(triangle_kernel, p), sds((n, p.ig, ch, LANES), BF16),
        [pltpu.VMEM((p.n_col, p.n_row * p.edge_rows, LANES), F32),
         pltpu.VMEM((ch, p.n_col, p.m * p.q, LANES), F32),
         pltpu.VMEM((ch, p.n_col, n_lane * LANES, LANES), F32),
         pltpu.VMEM((ch, n_lane, p.m * p.q, LANES), F32),
         pltpu.VMEM((p.n_col, p.m * ch, LANES), F32)],
        [VMEM], "triangle")(edges)

    back = lax.all_to_all(back, ALL, 0, 0, tiled=True)
    state = call(
        functools.partial(final_kernel, p), sds((p.rows, p.cols, width), BF16),
        [pltpu.VMEM((p.ig, width, LANES), F32), pltpu.VMEM((p.ig, LANES, LANES), F32),
         pltpu.VMEM((p.rows * p.cols, LANES), F32), pltpu.VMEM((p.rows, p.cols, width), BF16),
         pltpu.SemaphoreType.DMA((p.ig,))],
        [VMEM] * 4, "final", out_spec=HBM)(back, mid, out_gate, w_last)
    return home, state


def general(
    stack_embedding,
    pair_representation,
    mixing_entry_coefficients,
    mixing_final_coefficients,
    pair_bias_matrix,
    tensor_side_coefficients,
    outer_output_weight,
    triangle_projection_weight,
    triangle_output_weight,
):
    sequences_per_device, residues_per_device, alignment_channels = stack_embedding.shape
    rows_dev = pair_representation.shape[0]
    pair_width = pair_representation.shape[2]
    number_heads = pair_bias_matrix.shape[1]
    head_channels = alignment_channels // number_heads
    outer_width = tensor_side_coefficients.shape[1] // 2
    row_count = lax.axis_size("row")
    seq_total = sequences_per_device * row_count
    row_index = lax.axis_index("row")
    normalized_input = (
        standardize_features(stack_embedding).astype(jnp.bfloat16).reshape(-1, alignment_channels)
    )
    mapped_lines = jnp.dot(
        normalized_input, mixing_entry_coefficients, preferred_element_type=jnp.float32
    )
    stack_probe_vectors = (
        (mapped_lines[:, :alignment_channels] * head_channels ** (-0.5))
        .astype(jnp.bfloat16)
        .reshape(sequences_per_device, residues_per_device, number_heads, head_channels)
    )
    stack_lookup_vectors = (
        mapped_lines[:, alignment_channels : 2 * alignment_channels]
        .astype(jnp.bfloat16)
        .reshape(sequences_per_device, residues_per_device, alignment_channels)
    )
    stack_content_vectors = (
        mapped_lines[:, 2 * alignment_channels : 3 * alignment_channels]
        .astype(jnp.bfloat16)
        .reshape(sequences_per_device, residues_per_device, alignment_channels)
    )
    sigmoid_factors = jax.nn.sigmoid(mapped_lines[:, 3 * alignment_channels :]).reshape(
        sequences_per_device, residues_per_device, alignment_channels
    )
    pair_normed = standardize_features(pair_representation).astype(jnp.bfloat16)
    bias_local = jnp.einsum(
        "ijc,ch->hij", pair_normed, pair_bias_matrix, preferred_element_type=jnp.float32
    ).astype(jnp.bfloat16)
    bias_all = lax.all_gather(bias_local, "row", axis=1, tiled=True)
    bias_query = lax.all_to_all(bias_all, "col", split_axis=1, concat_axis=2, tiled=True)
    best_score = jnp.full(
        (sequences_per_device, number_heads, residues_per_device), -1e30, jnp.float32
    )
    received_keys = lax.all_gather(stack_lookup_vectors, "col", axis=1, tiled=True)
    received_values = lax.all_gather(stack_content_vectors, "col", axis=1, tiled=True)
    key_count = received_keys.shape[1]
    received_keys = received_keys.reshape(
        sequences_per_device, key_count, number_heads, head_channels
    )
    received_values = received_values.reshape(
        sequences_per_device, key_count, number_heads, head_channels
    )
    bias_piece = bias_query.astype(jnp.float32)
    scores = (
        jnp.einsum(
            "yeca,yica->ycei",
            stack_probe_vectors,
            received_keys,
            preferred_element_type=jnp.float32,
        )
        + bias_piece[None]
    )
    next_best = jnp.maximum(best_score, jnp.max(scores, axis=-1))
    weights = jnp.exp(scores - next_best[..., None])
    next_sum = jnp.sum(weights, axis=-1)
    update = jnp.einsum(
        "shqk,skhd->sqhd",
        weights.astype(jnp.bfloat16),
        received_values,
        preferred_element_type=jnp.float32,
    )
    weighted_mixture = (update / jnp.transpose(next_sum, (0, 2, 1))[..., None]).reshape(
        sequences_per_device, residues_per_device, alignment_channels
    )
    scaled_mixture = (sigmoid_factors * weighted_mixture).astype(jnp.bfloat16)
    stack_increment = jnp.dot(
        scaled_mixture.reshape(-1, alignment_channels),
        mixing_final_coefficients,
        preferred_element_type=jnp.float32,
    ).reshape(sequences_per_device, residues_per_device, alignment_channels)
    stack_embedding_updated = (stack_embedding.astype(jnp.float32) + stack_increment).astype(
        jnp.bfloat16
    )
    tensor_standardized = (
        standardize_features(stack_embedding_updated)
        .astype(jnp.bfloat16)
        .reshape(-1, alignment_channels)
    )
    sides = jnp.dot(
        tensor_standardized, tensor_side_coefficients, preferred_element_type=jnp.float32
    ).astype(jnp.bfloat16)
    sides = sides.reshape(sequences_per_device, residues_per_device, 2 * outer_width)
    left_side = sides[..., :outer_width]
    right_side = sides[..., outer_width:]
    left_wide = lax.all_gather(left_side, "col", axis=1, tiled=True)
    left_every, right_all = (
        lax.all_gather(left_wide, "row", axis=0, tiled=True),
        lax.all_gather(right_side, "row", axis=0, tiled=True),
    )
    left_all = lax.dynamic_slice_in_dim(left_every, row_index * rows_dev, rows_dev, 1)
    products = jnp.einsum("sic,sjd->ijcd", left_all, right_all, preferred_element_type=jnp.float32)
    averaged = (products * (1.0 / seq_total)).astype(jnp.bfloat16)
    outer_update = jnp.dot(
        averaged.reshape(-1, outer_width * outer_width),
        outer_output_weight,
        preferred_element_type=jnp.float32,
    )
    pair_mid = (
        pair_representation.astype(jnp.float32)
        + outer_update.reshape(rows_dev, residues_per_device, pair_width)
    ).astype(jnp.bfloat16)
    tri_normed = standardize_features(pair_mid).astype(jnp.bfloat16).reshape(-1, pair_width)
    tri_parts = jnp.dot(
        tri_normed, triangle_projection_weight, preferred_element_type=jnp.float32
    ).reshape(rows_dev, residues_per_device, 5 * pair_width)
    left_edge = (
        jax.nn.sigmoid(tri_parts[..., pair_width : 2 * pair_width]) * tri_parts[..., :pair_width]
    ).astype(jnp.bfloat16)
    right_edge = (
        jax.nn.sigmoid(tri_parts[..., 3 * pair_width : 4 * pair_width])
        * tri_parts[..., 2 * pair_width : 3 * pair_width]
    ).astype(jnp.bfloat16)
    out_gate = jax.nn.sigmoid(tri_parts[..., 4 * pair_width :])
    right_rows = lax.all_gather(right_edge, "row", axis=0, tiled=True)
    right_query = lax.all_to_all(right_rows, "col", split_axis=0, concat_axis=1, tiled=True)
    arrived = lax.all_gather(left_edge, "col", axis=1, tiled=True)
    summed = jnp.einsum("ikc,jkc->ijc", arrived, right_query, preferred_element_type=jnp.float32)
    tri_ln = standardize_features(summed).astype(jnp.bfloat16)
    tri_update = jnp.dot(
        tri_ln.reshape(-1, pair_width), triangle_output_weight, preferred_element_type=jnp.float32
    ).reshape(rows_dev, residues_per_device, pair_width)
    pair_state_next = (pair_mid.astype(jnp.float32) + out_gate * tri_update).astype(jnp.bfloat16)
    return (stack_embedding_updated, pair_state_next)


def shards(x, pair, w_in, w_out, w_bias, w_side, w_outer, w_tri, w_last):
    p = Plan(lax.axis_size("row"), lax.axis_size("col"), x.shape, pair.shape, w_bias.shape[1],
             w_side.shape[1] // 2, w_last.shape[1])
    path = functools.partial(fast, p) if p.ok else general
    return path(x, pair, w_in, w_out, w_bias, w_side, w_outer, w_tri, w_last)


def solution(mesh):
    return jax.shard_map(
        shards,
        mesh=mesh,
        in_specs=(P("row", "col", None), P("row", "col", None), P(), P(), P(), P(), P(), P(), P()),
        out_specs=(P("row", "col", None), P("row", "col", None)),
        check_vma=False,
    )
```

```python
import functools

import jax
import jax.numpy as jnp
from jax import lax
from jax.experimental import pallas as pl
from jax.experimental.pallas import tpu as pltpu
from jax.sharding import PartitionSpec as P

epsilon = 1e-05
LANES = 128
MOST_VMEM = 67_043_328
SUBLANES = 8
F32 = jnp.float32
BF16 = jnp.bfloat16
ALL = ("row", "col")
NT = (((1,), (1,)), ((), ()))
VMEM = pl.BlockSpec(memory_space=pltpu.VMEM)
SMEM = pl.BlockSpec(memory_space=pltpu.SMEM)
HBM = pl.BlockSpec(memory_space=pltpu.HBM)


def standardize_features(inputs, axis=-1):
    inputs = inputs.astype(jnp.float32)
    center = inputs - jnp.mean(inputs, axis=axis, keepdims=True)
    spread = jnp.mean(center * center, axis=axis, keepdims=True)
    return center * lax.rsqrt(spread + epsilon)


def dot(a, b):
    return jnp.dot(a, b, preferred_element_type=F32)


def dot_nt(a, b):
    return lax.dot_general(a, b, NT, preferred_element_type=F32)


def lane_iota(rows, width=LANES):
    return lax.broadcasted_iota(jnp.int32, (rows, width), 1)


def row_iota(rows, width=LANES):
    return lax.broadcasted_iota(jnp.int32, (rows, width), 0)


def over(index, size):
    return lax.shift_right_logical(index, jnp.int32(size.bit_length() - 1))


def modulo(index, size):
    return lax.bitwise_and(index, jnp.int32(size - 1))


def call(body, out_shape, scratch, in_specs, name, limit=24, out_spec=VMEM):
    return pl.pallas_call(
        body,
        out_shape=out_shape,
        in_specs=in_specs,
        out_specs=out_spec if isinstance(out_spec, tuple) else jax.tree.map(lambda _: out_spec, out_shape),
        scratch_shapes=scratch,
        name=name,
        cost_estimate=pl.CostEstimate(flops=400_000_000, bytes_accessed=4_000_000, transcendentals=0),
        compiler_params=pltpu.CompilerParams(vmem_limit_bytes=min(limit * 1024 * 1024, MOST_VMEM)),
    )


class Plan:
    def __init__(self, n_row, n_col, x, pair, heads, outer, channels_out):
        self.n_row, self.n_col, self.n = n_row, n_col, n_row * n_col
        self.seqs, self.res, self.feat = x
        self.rows, self.cols, self.width = pair
        self.heads, self.outer = heads, outer
        self.hd = self.feat // heads
        self.total = self.res * n_col
        self.ok = False
        if any(size & (size - 1) for size in (heads, outer, self.hd, n_row, n_col)):
            return
        if self.seqs % n_col or self.width != LANES or heads != SUBLANES or self.cols != self.res:
            return
        if self.rows * n_row != self.total or self.feat % LANES:
            return
        self.split = 2
        if n_col % self.split:
            return
        self.n_group = n_col // self.split
        self.own = self.seqs // self.n_group
        self.seq_total = self.own * self.n_group * n_row
        if LANES % outer or outer % (LANES // outer):
            return
        self.pack = LANES // outer
        if self.rows % self.pack or self.cols % self.pack:
            return
        self.half = -(-self.rows // (self.split * self.pack)) * self.pack
        self.late = self.rows - self.half
        self.queries = n_row * self.half
        self.i_main = LANES // heads // 2
        self.i_rem = self.half - self.i_main
        if self.i_main != SUBLANES or 2 * self.i_rem != SUBLANES or self.i_main % self.pack or self.i_rem % self.pack or LANES % (self.i_rem * heads) or self.cols % SUBLANES:
            return
        self.km = self.i_main // self.pack
        self.main, self.rem = self.i_main * heads, self.i_rem * heads
        self.groups = self.cols // SUBLANES
        self.tall = -(-self.groups // 2)
        self.fold = LANES // self.rem
        if n_row % 2 or n_row % self.fold or n_row * self.main % (2 * LANES) or n_row * self.rem % (2 * LANES):
            return
        self.main_at = [(g % self.tall, g // self.tall * self.main) for g in range(self.groups)]
        spare = [(self.tall, f * self.rem) for f in range(self.fold)]
        if self.groups % 2:
            spare += [(self.tall - 1, self.main + f * self.rem) for f in range(self.main // self.rem)]
        if len(spare) < self.groups:
            return
        self.rem_at = spare[:self.groups]
        self.bias_rows = (self.tall + 1) * SUBLANES
        self.per = n_row // n_col
        if n_row % n_col or self.per * self.rows != self.cols:
            return
        self.lk, self.rk = self.rows // self.pack, self.cols // self.pack
        self.hk = self.half // self.pack
        self.ek = self.lk - self.hk
        chunks = max(self.ek + self.per * self.hk, self.hk + self.per * self.ek)
        self.side_rows = -(-chunks * self.own // 16) * 16
        self.cpad = -(-self.cols // 16) * 16
        if self.width % self.n:
            return
        self.ch = self.width // self.n
        if 2 * self.ch != SUBLANES:
            return
        self.q = LANES // self.cols
        self.ig = -(-self.rows // self.q)
        self.ipad = self.ig * self.q
        self.jslot = self.per * self.ipad
        if self.q * self.jslot > LANES:
            return
        self.m = n_row * self.ig
        self.edge_rows = self.ig * SUBLANES
        self.ok = True

    def j_base(self, c):
        return (c // self.q) * LANES + (c % self.q) * self.jslot


def bias_kernel(p, col_ref, pair_hbm, w_hbm, x_hbm, *refs):
    out_hbm, *part_hbm = refs[:p.n_col + 1]
    pair_ref, w_ref, x_ref, piece_ref, sems, out_sems, part_sems = refs[p.n_col + 1:]
    copies = [pltpu.make_async_copy(pair_hbm, pair_ref, sems.at[0]), pltpu.make_async_copy(w_hbm, w_ref, sems.at[1]),
              pltpu.make_async_copy(x_hbm, x_ref, sems.at[2])]
    for copy in copies:
        copy.start()
    for copy in copies:
        copy.wait()
    parts = []
    for shift in range(p.n_col):
        group = over(lax.rem(col_ref[0] + shift, p.n_col), p.split)
        parts.append(pltpu.make_async_copy(x_ref.at[group], part_hbm[shift], part_sems.at[shift]))
        parts[-1].start()
    normed = standardize_features(pair_ref[...]).reshape(p.rows * p.cols, p.width)
    heads = p.heads

    def tile(many):
        spread = modulo(over(lane_iota(heads), many), heads) == row_iota(heads)
        return lax.dot_general(w_ref[...], jnp.where(spread, 1.0, 0.0).astype(BF16), (((0,), (0,)), ((), ())),
                               preferred_element_type=F32)

    main_w, rem_w = tile(p.i_main), tile(p.i_rem)
    main_slot, rem_slot = modulo(lane_iota(p.width), p.i_main), modulo(lane_iota(p.width), p.i_rem)
    at = lane_iota(SUBLANES)
    for h in range(p.split):
        main = jnp.zeros((p.cols, LANES), F32)
        rem = jnp.zeros((p.cols, LANES), F32)
        for m in range(p.half):
            i = h * p.late + m
            block = normed[i * p.cols:(i + 1) * p.cols].astype(BF16)
            if m < p.i_main:
                main += dot(block, jnp.where(main_slot == m, main_w, 0.0).astype(BF16))
            else:
                rem += dot(block, jnp.where(rem_slot == m - p.i_main, rem_w, 0.0).astype(BF16))
        blocks = [jnp.zeros((SUBLANES, LANES), F32) for _ in range(p.tall + 1)]
        for value, places, wide in ((main, p.main_at, p.main), (rem, p.rem_at, p.rem)):
            for g, (b, lane) in enumerate(places):
                here = (at >= lane) & (at < lane + wide)
                blocks[b] = jnp.where(here, value[g * SUBLANES:(g + 1) * SUBLANES], blocks[b])
        piece = jnp.concatenate(blocks, axis=0).astype(BF16)
        for c in range(h, p.n_col, p.split):
            piece_ref[c] = piece
    pieces = [pltpu.make_async_copy(piece_ref, out_hbm.at[pl.ds(r * p.n_col, p.n_col)], out_sems.at[r])
              for r in range(p.n_row)]
    for copy in pieces:
        copy.start()
    for copy in pieces + parts:
        copy.wait()


def pick_half(p, second, rows):
    main, rest = [], []
    for r in range(p.n_row):
        a, b = r * p.rows, r * p.rows + p.late
        main.append(jnp.where(second, rows[b:b + p.i_main], rows[a:a + p.i_main]))
        rest.append(jnp.where(second, rows[b + p.i_main:b + p.half], rows[a + p.i_main:a + p.half]))
    return jnp.concatenate(main + rest, axis=0)


def project_kernel(p, col_ref, *refs):
    x_refs = refs[:p.n_col]
    w_ref, q_ref, k_ref, v_ref, gate_ref, x_out, hold = refs[p.n_col:]
    me = col_ref[0]
    second = lax.rem(me, p.split) == 1
    for shift in range(p.n_col):
        hold[lax.rem(me + (p.n_col - shift), p.n_col)] = x_refs[shift][...].astype(F32)
    f = p.feat
    for s in range(p.own):
        x = jnp.concatenate([hold[c, s] for c in range(p.n_col)], axis=0)
        normed = standardize_features(x)
        x_out[s] = pick_half(p, second, x).astype(BF16)
        lines = dot(normed.astype(BF16), w_ref[:, f:3 * f])
        k_ref[s] = lines[:, :f].astype(BF16)
        v_ref[s] = lines[:, f:].astype(BF16)
        normed = pick_half(p, second, normed).astype(BF16)
        gate_ref[s] = jax.nn.sigmoid(dot(normed, w_ref[:, 3 * f:]))
        q_ref[s] = (dot(normed, w_ref[:, :f]) * p.hd ** (-0.5)).astype(BF16)


def attend_kernel(p, col_ref, q_ref, k_ref, v_ref, gate_ref, x_ref, bias_ref, wf_ref, ws_ref,
                  emb_ref, side_hbm, bias, four, lint, rint, send, side_ref, sems):
    h, t, f, m = p.heads, p.queries, p.feat, p.half
    at = lane_iota(SUBLANES)
    for first, places, wide in ((0, p.main_at, p.main), (p.n_row * p.main, p.rem_at, p.rem)):
        fold = LANES // wide
        slot = over(at, wide)
        for c in range(p.n_col):
            for b in range(p.n_row // fold):
                for g, (block, lane) in enumerate(places):
                    built = None
                    for u in range(fold):
                        piece = bias_ref[(b * fold + u) * p.n_col + c,
                                         block * SUBLANES:(block + 1) * SUBLANES].astype(F32)
                        turn = (u * wide - lane) % LANES
                        piece = pltpu.roll(piece, turn, axis=1) if turn else piece
                        built = piece if u == 0 else jnp.where(slot == u, piece, built)
                    row = c * p.cols + g * SUBLANES
                    bias[row:row + SUBLANES, first + b * LANES:first + (b + 1) * LANES] = built
    step = 2 * LANES
    lane, row = lane_iota(f, step), row_iota(f, step)
    blocks = []
    for many, wide, count in ((p.i_main, p.main, p.n_row * p.main // step), (p.i_rem, p.rem, p.n_row * p.rem // step)):
        own_head = over(row, p.hd) == modulo(over(lane, many), h)
        at = lane_iota(step // h, step)
        pick = jnp.where(row_iota(step // h, step) == over(at, wide) * many + modulo(at, many), 1.0, 0.0).astype(BF16)
        blocks += [(own_head, pick)] * count
    head_lane, low = over(lane_iota(SUBLANES, f), p.hd), row_iota(SUBLANES, f) >= p.i_rem
    own_lane = [jnp.where(head_lane == g, 1.0, 0.0) for g in range(h)]
    own_pair = [jnp.where(low, own_lane[g + 1], own_lane[g]) for g in range(0, h, 2)]
    new, tall, together = [], step // SUBLANES, 4
    for first in range(0, p.own, together):
        jobs = []
        for s in range(first, min(first + together, p.own)):
            q = q_ref[s].astype(F32)
            spread = []
            for r in range(p.n_row):
                rows = q[r * p.i_main:(r + 1) * p.i_main]
                spread += [rows * mask for mask in own_lane]
            for r in range(p.n_row):
                start = p.n_row * p.i_main + r * p.i_rem
                rows = jnp.concatenate([q[start:start + p.i_rem]] * 2, axis=0)
                spread += [rows * mask for mask in own_pair]
            for n in range(len(blocks)):
                jobs.append((s, n, jnp.concatenate(spread[n * tall:(n + 1) * tall], axis=0).astype(BF16)))
        v_t = {s: jnp.transpose(v_ref[s].astype(F32)).astype(BF16) for s in range(first, first + together)
               if s < p.own}
        scores = [dot_nt(k_ref[s], rows) + bias[:, n * step:(n + 1) * step] for s, n, rows in jobs]
        weights = [jnp.exp(score - jnp.max(score, axis=0, keepdims=True)) for score in scores]
        share = [1.0 / jnp.sum(weight, axis=0, keepdims=True) for weight in weights]
        mixed = [dot(v_t[s], weight.astype(BF16)) for (s, _, _), weight in zip(jobs, weights)]
        mixed = [jnp.where(blocks[n][0], value * part, 0.0).astype(BF16)
                 for (_, n, _), value, part in zip(jobs, mixed, share)]
        attended = [dot_nt(blocks[n][1], value) for (_, n, _), value in zip(jobs, mixed)]
        for i, at in enumerate(range(0, len(jobs), len(blocks))):
            rows = jnp.concatenate(attended[at:at + len(blocks)], axis=0)
            new.append((gate_ref[first + i] * rows).astype(BF16))
    new = dot(jnp.concatenate(new, axis=0), wf_ref[...])
    new = (x_ref[...].astype(F32).reshape(p.own * t, f) + new).astype(BF16).astype(F32)
    a, b = p.per * p.i_main, p.per * p.i_rem
    for s in range(p.own):
        for c in range(p.n_col):
            row, tail = s * t + c * a, s * t + p.n_row * p.i_main + c * b
            emb_ref[c, s] = jnp.concatenate([new[row:row + a], new[tail:tail + b]], axis=0).astype(BF16)
    sides = dot(standardize_features(new).astype(BF16), ws_ref[...])
    four[0] = sides[:, :LANES]
    four[1] = sides[:, LANES:]
    n4 = t // p.pack
    lane = over(lane_iota(n4), p.outer)
    for s in range(p.own):
        for side, woven in enumerate((lint, rint)):
            packed = four[side, pl.ds(s * t, n4, stride=p.pack), :]
            for a in range(1, p.pack):
                packed = jnp.where(lane == a, four[side, pl.ds(s * t + a, n4, stride=p.pack), :], packed)
            woven[pl.ds(s, n4, stride=p.own), :] = packed
    o = p.own

    def place(r, k):
        return (r * p.km + k if k < p.km else p.n_row * p.km + r * (p.hk - p.km) + k - p.km) * o

    def fill(left, right):
        for r in range(p.n_row):
            for c in range(p.n_col):
                d, row = r * p.n_col + c, 0
                spans = [(lint, place(r, k)) for k in left]
                spans += [(rint, place(c * p.per + u, k)) for u in range(p.per) for k in right]
                for source, start in spans:
                    send[d, row:row + o] = source[start:start + o]
                    row += o
                if row < p.side_rows:
                    send[d, row:p.side_rows] = jnp.zeros((p.side_rows - row, LANES), F32)
            block = slice(r * p.n_col, (r + 1) * p.n_col)
            side_ref[block] = send[block].astype(BF16)
            leave(r).start()

    def leave(r):
        block = pl.ds(r * p.n_col, p.n_col)
        return pltpu.make_async_copy(side_ref.at[block], side_hbm.at[block], sems.at[r])

    second = lax.rem(col_ref[0], p.split) == 1

    @pl.when(jnp.logical_not(second))
    def _():
        fill(range(p.ek), range(p.hk))

    @pl.when(second)
    def _():
        fill(range(p.hk), range(p.hk - p.ek, p.hk))

    for r in range(p.n_row):
        leave(r).wait()


def home_kernel(p, col_ref, *refs):
    part_refs = refs[:p.n_col]
    out_ref, hold = refs[p.n_col:]
    me = col_ref[0]
    for shift in range(p.n_col):
        hold[lax.rem(me + (p.n_col - shift), p.n_col)] = part_refs[shift][...].astype(F32)
    both = 2 * p.half - p.rows
    tail = p.per * p.i_main
    for g in range(p.n_group):
        for s in range(p.own):
            rows = []
            for u in range(p.per):
                for skip, half in ((0, hold[g * p.split, s]), (both, hold[g * p.split + 1, s])):
                    rows.append(half[u * p.i_main + min(skip, p.i_main):(u + 1) * p.i_main])
                    rows.append(half[tail + u * p.i_rem + max(skip - p.i_main, 0):tail + (u + 1) * p.i_rem])
            rows = [value for value in rows if value.shape[0]]
            out_ref[g * p.own + s] = jnp.concatenate(rows, axis=0).astype(BF16)


def outer_kernel(p, recv_ref, pair_ref, w_ref, wv_ref, wg_ref, wo_ref, mid_ref, edge_ref, gate_ref,
                 flat, rt, lhs, mid):
    flat[...] = recv_ref[...].reshape(p.n * p.side_rows, LANES).astype(F32)

    def chunk(h, k):
        return jnp.concatenate(
            [flat[pl.ds(h * p.side_rows + k * p.own + s, p.n // p.split, stride=p.split * p.side_rows), :]
             for s in range(p.own)], axis=0)

    hk, ek = p.hk, p.ek
    for u in range(p.per):
        for k in range(p.lk):
            value = chunk(0, ek + u * hk + k) if k < hk else chunk(1, hk + u * ek + k - hk)
            row = (u * p.lk + k) * LANES
            rt[row:row + LANES, :] = jnp.transpose(value)
    right = []
    for first in range(0, p.outer, p.pack):
        right.append(jnp.concatenate(
            [rt[pl.ds(first + d, p.cols, stride=p.outer), :] for d in range(p.pack)], axis=1))
    right = jnp.concatenate(right, axis=0).astype(BF16)
    at = over(lane_iota(p.seq_total), p.outer)
    left = []
    for g in range(p.lk):
        base = chunk(0, g) if g < ek else chunk(1, g - ek)
        turned = [base] + [pltpu.roll(base, t * p.outer, axis=1) for t in range(1, p.pack)]
        for a in range(p.pack):
            left.append(jnp.concatenate(
                [jnp.where(at == d, turned[(d - a) % p.pack], 0.0) for d in range(p.pack)], axis=0).astype(BF16))
    products = dot(right, jnp.concatenate(left, axis=1)) * (1.0 / p.seq_total)
    for i in range(p.rows):
        for g in range(p.outer // p.pack):
            lhs[i * p.cpad:i * p.cpad + p.cols, g * LANES:(g + 1) * LANES] = products[
                g * p.cols:(g + 1) * p.cols, i * LANES:(i + 1) * LANES].astype(BF16)
        if p.cpad > p.cols:
            lhs[i * p.cpad + p.cols:(i + 1) * p.cpad, :] = jnp.zeros((p.cpad - p.cols, lhs.shape[1]), BF16)
    update = dot(lhs[...], w_ref[...])
    for i in range(p.rows):
        fresh = (pair_ref[i].astype(F32) + update[i * p.cpad:i * p.cpad + p.cols]).astype(BF16)
        mid_ref[i] = fresh
        mid[i * p.cols:(i + 1) * p.cols, :] = fresh.astype(F32)
    tail = mid.shape[0] - p.rows * p.cols
    mid[p.rows * p.cols:, :] = jnp.zeros((tail, LANES), F32)
    step = p.q * p.cols
    for k in range(p.ig):
        normed = standardize_features(mid[k * step:k * step + LANES, :]).astype(BF16)
        value = dot_nt(wv_ref[...], normed)
        gate = jax.nn.sigmoid(dot_nt(wg_ref[...], normed))
        edge_ref[:, k * SUBLANES:(k + 1) * SUBLANES, :] = (gate * value).reshape(
            p.n, SUBLANES, LANES).astype(BF16)
        many = min(step, p.rows * p.cols - k * step)
        gate_ref[k * step:k * step + many, :] = jax.nn.sigmoid(dot(normed, wo_ref[...]))[:many]


def triangle_kernel(p, recv_ref, out_ref, flat, ls, rs, os, sb):
    for r in range(p.n_row):
        for c in range(p.n_col):
            flat[c, r * p.edge_rows:(r + 1) * p.edge_rows, :] = recv_ref[r * p.n_col + c].astype(F32)
    lane = lane_iota(p.m)
    part_of = jnp.broadcast_to(lane_iota(1) // p.jslot, (p.m, LANES))
    blocks = p.per * p.ig
    rs[...] = jnp.zeros_like(rs)
    for ch in range(p.ch):
        for c in range(p.n_col):
            left = flat[c, pl.ds(ch, p.m, stride=SUBLANES), :]
            right = flat[c, pl.ds(p.ch + ch, p.m, stride=SUBLANES), :]
            for a in range(p.q):
                turn = (-a * p.cols) % LANES
                lt = pltpu.roll(left, turn, axis=1) if turn else left
                rt = pltpu.roll(right, turn, axis=1) if turn else right
                ls[ch, c, pl.ds(a, p.m, stride=p.q), :] = jnp.where(lane < p.cols, lt, 0.0)
                for first in range(0, p.n_col, p.q):
                    many = min(p.q, p.n_col - first) * blocks
                    rs[ch, c, pl.ds(p.j_base(first) + a, many, stride=p.q), :] = rt[
                        first * blocks:first * blocks + many]
    for ch in range(p.ch):
        lfull = jnp.concatenate([ls[ch, c] for c in range(p.n_col)], axis=1).astype(BF16)
        rfull = jnp.concatenate([rs[ch, c] for c in range(p.n_col)], axis=1).astype(BF16)
        summed = dot_nt(lfull, rfull)
        for b in range(summed.shape[1] // LANES):
            os[ch, b] = summed[:, b * LANES:(b + 1) * LANES]
        rows = [[os[ch, b, pl.ds(a, p.m, stride=p.q), :] for a in range(p.q)]
                for b in range(summed.shape[1] // LANES)]
        for c in range(p.n_col):
            b, part = c // p.q, c % p.q
            packed = None
            for a in range(p.q):
                turn = ((a - part) * p.jslot) % LANES
                piece = pltpu.roll(rows[b][a], turn, axis=1) if turn else rows[b][a]
                packed = piece if packed is None else jnp.where(part_of == a, piece, packed)
            sb[c, pl.ds(ch, p.m, stride=p.ch), :] = packed
    for r in range(p.n_row):
        for c in range(p.n_col):
            for k in range(p.ig):
                row = (r * p.ig + k) * p.ch
                out_ref[r * p.n_col + c, k] = sb[c, row:row + p.ch, :].astype(BF16)


def final_kernel(p, recv_ref, mid_ref, gate_ref, w_ref, out_hbm, flat, hold, update, out_ref, sems):
    copies = []
    for k in range(p.ig):
        for d in range(p.n):
            flat[k, d * p.ch:(d + 1) * p.ch, :] = recv_ref[d, k].astype(F32)
    for k in range(p.ig):
        normed = jnp.transpose(standardize_features(flat[k], axis=0)).astype(BF16)
        hold[k] = dot(normed, w_ref[...])
        first, last = k * p.q, min((k + 1) * p.q, p.rows)
        for i in range(first, last):
            for u in range(p.per):
                row = (i - first) * p.jslot + u * p.ipad
                update[i * p.cols + u * p.rows:i * p.cols + (u + 1) * p.rows, :] = hold[k, row:row + p.rows, :]
        span = slice(first * p.cols, last * p.cols)
        fresh = mid_ref[first:last].astype(F32) + (gate_ref[span] * update[span]).reshape(
            last - first, p.cols, p.width)
        out_ref[first:last] = fresh.astype(BF16)
        rows = pl.ds(first, last - first)
        copies.append(pltpu.make_async_copy(out_ref.at[rows], out_hbm.at[rows], sems.at[k]))
        copies[-1].start()
    for copy in copies:
        copy.wait()


def fast(p, x, pair, w_in, w_out, w_bias, w_side, w_outer, w_tri, w_last):
    col = lax.axis_index("col")
    n, ch, width = p.n, p.ch, p.width
    sds = jax.ShapeDtypeStruct

    side_w = jnp.concatenate([w_side[:, :p.outer]] * p.pack + [w_side[:, p.outer:]] * p.pack, axis=1)
    by_d = jnp.transpose(w_outer.reshape(p.outer, p.outer, width), (1, 0, 2)).reshape(w_outer.shape)
    blocks = jnp.transpose(w_tri.reshape(width, 5, width), (1, 2, 0)).reshape(5, n, ch, width)
    value_w = jnp.concatenate([blocks[0], blocks[2]], axis=1).reshape(n * 2 * ch, width)
    gate_w = jnp.concatenate([blocks[1], blocks[3]], axis=1).reshape(n * 2 * ch, width)
    own_gate_w = w_tri[:, 4 * width:]

    at = col.reshape(1)
    chunks = (p.own, p.res, p.feat)
    piece, *parts = call(
        functools.partial(bias_kernel, p), (sds((n, p.bias_rows, LANES), BF16),) + (sds(chunks, BF16),) * p.n_col,
        [pltpu.VMEM(pair.shape, BF16), pltpu.VMEM((p.heads, width), BF16), pltpu.VMEM((p.n_group,) + chunks, BF16),
         pltpu.VMEM((p.n_col, p.bias_rows, LANES), BF16), pltpu.SemaphoreType.DMA((3,)),
         pltpu.SemaphoreType.DMA((p.n_row,)), pltpu.SemaphoreType.DMA((p.n_col,))],
        [SMEM] + [HBM] * 3, "bias", limit=64, out_spec=HBM)(at, pair, w_bias.T, x.reshape((p.n_group,) + chunks))
    bias = lax.all_to_all(piece, ALL, 0, 0, tiled=True)

    def ring(parts):
        return [parts[0]] + [
            lax.ppermute(parts[shift], "col", [(c, (c + shift) % p.n_col) for c in range(p.n_col)])
            for shift in range(1, p.n_col)]

    parts = ring(parts)
    mine, every = (p.own, p.queries, p.feat), (p.own, p.total, p.feat)
    q, k, v, gate, rest = call(
        functools.partial(project_kernel, p),
        (sds(mine, BF16), sds(every, BF16), sds(every, BF16), sds(mine, F32), sds(mine, BF16)),
        [pltpu.VMEM((p.n_col, p.own, p.res, p.feat), F32)],
        [SMEM] + [VMEM] * (p.n_col + 1), "project")(at, *parts, w_in)
    emb, sides = call(
        functools.partial(attend_kernel, p),
        (sds((p.n_col, p.own, p.per * p.half, p.feat), BF16), sds((n, p.side_rows, LANES), BF16)),
        [pltpu.VMEM((p.total, p.queries * p.heads), F32), pltpu.VMEM((2, p.own * p.queries, LANES), F32)]
        + [pltpu.VMEM((p.queries // p.pack * p.own, LANES), F32)] * 2
        + [pltpu.VMEM((n, p.side_rows, LANES), F32), pltpu.VMEM((n, p.side_rows, LANES), BF16),
           pltpu.SemaphoreType.DMA((p.n_row,))],
        [SMEM] + [VMEM] * 8, "attend", out_spec=(VMEM, HBM))(at, q, k, v, gate, rest, bias, w_out, side_w)

    sides = lax.all_to_all(sides, ALL, 0, 0, tiled=True)

    parts = ring([lax.dynamic_index_in_dim(emb, lax.rem(col + shift, p.n_col), 0, keepdims=False)
                  for shift in range(p.n_col)])
    home = call(functools.partial(home_kernel, p), sds(x.shape, BF16),
                [pltpu.VMEM((p.n_col, p.own, p.per * p.half, p.feat), F32)],
                [SMEM] + [VMEM] * p.n_col, "home")(at, *parts)

    mid, edges, out_gate = call(
        functools.partial(outer_kernel, p),
        (sds((p.rows, p.cols, width), BF16), sds((n, p.edge_rows, LANES), BF16),
         sds((p.rows * p.cols, width), F32)),
        [pltpu.VMEM((n * p.side_rows, LANES), F32),
         pltpu.VMEM((p.rk * LANES, p.seq_total), F32),
         pltpu.VMEM((p.rows * p.cpad, p.outer * p.outer), BF16),
         pltpu.VMEM(((p.ig - 1) * p.q * p.cols + LANES, LANES), F32)],
        [VMEM] * 6, "outer")(sides, pair, by_d, value_w, gate_w, own_gate_w)

    edges, home = lax.optimization_barrier((edges, home))
    edges = lax.all_to_all(edges, ALL, 0, 0, tiled=True)
    n_lane = p.j_base(p.n_col - 1) // LANES + 1
    back = call(
        functools.partial(triangle_kernel, p), sds((n, p.ig, ch, LANES), BF16),
        [pltpu.VMEM((p.n_col, p.n_row * p.edge_rows, LANES), F32),
         pltpu.VMEM((ch, p.n_col, p.m * p.q, LANES), F32),
         pltpu.VMEM((ch, p.n_col, n_lane * LANES, LANES), F32),
         pltpu.VMEM((ch, n_lane, p.m * p.q, LANES), F32),
         pltpu.VMEM((p.n_col, p.m * ch, LANES), F32)],
        [VMEM], "triangle")(edges)

    back = lax.all_to_all(back, ALL, 0, 0, tiled=True)
    state = call(
        functools.partial(final_kernel, p), sds((p.rows, p.cols, width), BF16),
        [pltpu.VMEM((p.ig, width, LANES), F32), pltpu.VMEM((p.ig, LANES, LANES), F32),
         pltpu.VMEM((p.rows * p.cols, LANES), F32), pltpu.VMEM((p.rows, p.cols, width), BF16),
         pltpu.SemaphoreType.DMA((p.ig,))],
        [VMEM] * 4, "final", out_spec=HBM)(back, mid, out_gate, w_last)
    return home, state


def general(
    stack_embedding,
    pair_representation,
    mixing_entry_coefficients,
    mixing_final_coefficients,
    pair_bias_matrix,
    tensor_side_coefficients,
    outer_output_weight,
    triangle_projection_weight,
    triangle_output_weight,
):
    sequences_per_device, residues_per_device, alignment_channels = stack_embedding.shape
    rows_dev = pair_representation.shape[0]
    pair_width = pair_representation.shape[2]
    number_heads = pair_bias_matrix.shape[1]
    head_channels = alignment_channels // number_heads
    outer_width = tensor_side_coefficients.shape[1] // 2
    row_count = lax.axis_size("row")
    seq_total = sequences_per_device * row_count
    row_index = lax.axis_index("row")
    normalized_input = (
        standardize_features(stack_embedding).astype(jnp.bfloat16).reshape(-1, alignment_channels)
    )
    mapped_lines = jnp.dot(
        normalized_input, mixing_entry_coefficients, preferred_element_type=jnp.float32
    )
    stack_probe_vectors = (
        (mapped_lines[:, :alignment_channels] * head_channels ** (-0.5))
        .astype(jnp.bfloat16)
        .reshape(sequences_per_device, residues_per_device, number_heads, head_channels)
    )
    stack_lookup_vectors = (
        mapped_lines[:, alignment_channels : 2 * alignment_channels]
        .astype(jnp.bfloat16)
        .reshape(sequences_per_device, residues_per_device, alignment_channels)
    )
    stack_content_vectors = (
        mapped_lines[:, 2 * alignment_channels : 3 * alignment_channels]
        .astype(jnp.bfloat16)
        .reshape(sequences_per_device, residues_per_device, alignment_channels)
    )
    sigmoid_factors = jax.nn.sigmoid(mapped_lines[:, 3 * alignment_channels :]).reshape(
        sequences_per_device, residues_per_device, alignment_channels
    )
    pair_normed = standardize_features(pair_representation).astype(jnp.bfloat16)
    bias_local = jnp.einsum(
        "ijc,ch->hij", pair_normed, pair_bias_matrix, preferred_element_type=jnp.float32
    ).astype(jnp.bfloat16)
    bias_all = lax.all_gather(bias_local, "row", axis=1, tiled=True)
    bias_query = lax.all_to_all(bias_all, "col", split_axis=1, concat_axis=2, tiled=True)
    best_score = jnp.full(
        (sequences_per_device, number_heads, residues_per_device), -1e30, jnp.float32
    )
    received_keys = lax.all_gather(stack_lookup_vectors, "col", axis=1, tiled=True)
    received_values = lax.all_gather(stack_content_vectors, "col", axis=1, tiled=True)
    key_count = received_keys.shape[1]
    received_keys = received_keys.reshape(
        sequences_per_device, key_count, number_heads, head_channels
    )
    received_values = received_values.reshape(
        sequences_per_device, key_count, number_heads, head_channels
    )
    bias_piece = bias_query.astype(jnp.float32)
    scores = (
        jnp.einsum(
            "yeca,yica->ycei",
            stack_probe_vectors,
            received_keys,
            preferred_element_type=jnp.float32,
        )
        + bias_piece[None]
    )
    next_best = jnp.maximum(best_score, jnp.max(scores, axis=-1))
    weights = jnp.exp(scores - next_best[..., None])
    next_sum = jnp.sum(weights, axis=-1)
    update = jnp.einsum(
        "shqk,skhd->sqhd",
        weights.astype(jnp.bfloat16),
        received_values,
        preferred_element_type=jnp.float32,
    )
    weighted_mixture = (update / jnp.transpose(next_sum, (0, 2, 1))[..., None]).reshape(
        sequences_per_device, residues_per_device, alignment_channels
    )
    scaled_mixture = (sigmoid_factors * weighted_mixture).astype(jnp.bfloat16)
    stack_increment = jnp.dot(
        scaled_mixture.reshape(-1, alignment_channels),
        mixing_final_coefficients,
        preferred_element_type=jnp.float32,
    ).reshape(sequences_per_device, residues_per_device, alignment_channels)
    stack_embedding_updated = (stack_embedding.astype(jnp.float32) + stack_increment).astype(
        jnp.bfloat16
    )
    tensor_standardized = (
        standardize_features(stack_embedding_updated)
        .astype(jnp.bfloat16)
        .reshape(-1, alignment_channels)
    )
    sides = jnp.dot(
        tensor_standardized, tensor_side_coefficients, preferred_element_type=jnp.float32
    ).astype(jnp.bfloat16)
    sides = sides.reshape(sequences_per_device, residues_per_device, 2 * outer_width)
    left_side = sides[..., :outer_width]
    right_side = sides[..., outer_width:]
    left_wide = lax.all_gather(left_side, "col", axis=1, tiled=True)
    left_every, right_all = (
        lax.all_gather(left_wide, "row", axis=0, tiled=True),
        lax.all_gather(right_side, "row", axis=0, tiled=True),
    )
    left_all = lax.dynamic_slice_in_dim(left_every, row_index * rows_dev, rows_dev, 1)
    products = jnp.einsum("sic,sjd->ijcd", left_all, right_all, preferred_element_type=jnp.float32)
    averaged = (products * (1.0 / seq_total)).astype(jnp.bfloat16)
    outer_update = jnp.dot(
        averaged.reshape(-1, outer_width * outer_width),
        outer_output_weight,
        preferred_element_type=jnp.float32,
    )
    pair_mid = (
        pair_representation.astype(jnp.float32)
        + outer_update.reshape(rows_dev, residues_per_device, pair_width)
    ).astype(jnp.bfloat16)
    tri_normed = standardize_features(pair_mid).astype(jnp.bfloat16).reshape(-1, pair_width)
    tri_parts = jnp.dot(
        tri_normed, triangle_projection_weight, preferred_element_type=jnp.float32
    ).reshape(rows_dev, residues_per_device, 5 * pair_width)
    left_edge = (
        jax.nn.sigmoid(tri_parts[..., pair_width : 2 * pair_width]) * tri_parts[..., :pair_width]
    ).astype(jnp.bfloat16)
    right_edge = (
        jax.nn.sigmoid(tri_parts[..., 3 * pair_width : 4 * pair_width])
        * tri_parts[..., 2 * pair_width : 3 * pair_width]
    ).astype(jnp.bfloat16)
    out_gate = jax.nn.sigmoid(tri_parts[..., 4 * pair_width :])
    right_rows = lax.all_gather(right_edge, "row", axis=0, tiled=True)
    right_query = lax.all_to_all(right_rows, "col", split_axis=0, concat_axis=1, tiled=True)
    arrived = lax.all_gather(left_edge, "col", axis=1, tiled=True)
    summed = jnp.einsum("ikc,jkc->ijc", arrived, right_query, preferred_element_type=jnp.float32)
    tri_ln = standardize_features(summed).astype(jnp.bfloat16)
    tri_update = jnp.dot(
        tri_ln.reshape(-1, pair_width), triangle_output_weight, preferred_element_type=jnp.float32
    ).reshape(rows_dev, residues_per_device, pair_width)
    pair_state_next = (pair_mid.astype(jnp.float32) + out_gate * tri_update).astype(jnp.bfloat16)
    return (stack_embedding_updated, pair_state_next)


def shards(x, pair, w_in, w_out, w_bias, w_side, w_outer, w_tri, w_last):
    p = Plan(lax.axis_size("row"), lax.axis_size("col"), x.shape, pair.shape, w_bias.shape[1],
             w_side.shape[1] // 2, w_last.shape[1])
    path = functools.partial(fast, p) if p.ok else general
    return path(x, pair, w_in, w_out, w_bias, w_side, w_outer, w_tri, w_last)


def solution(mesh):
    return jax.shard_map(
        shards,
        mesh=mesh,
        in_specs=(P("row", "col", None), P("row", "col", None), P(), P(), P(), P(), P(), P(), P()),
        out_specs=(P("row", "col", None), P("row", "col", None)),
        check_vma=False,
    )
```

```python
import functools

import jax
import jax.numpy as jnp
from jax import lax
from jax.experimental import pallas as pl
from jax.experimental.pallas import tpu as pltpu
from jax.sharding import PartitionSpec as P

epsilon = 1e-05
LANES = 128
MOST_VMEM = 67_043_328
SUBLANES = 8
F32 = jnp.float32
BF16 = jnp.bfloat16
ALL = ("row", "col")
NT = (((1,), (1,)), ((), ()))
VMEM = pl.BlockSpec(memory_space=pltpu.VMEM)
SMEM = pl.BlockSpec(memory_space=pltpu.SMEM)
HBM = pl.BlockSpec(memory_space=pltpu.HBM)


def standardize_features(inputs, axis=-1):
    inputs = inputs.astype(jnp.float32)
    center = inputs - jnp.mean(inputs, axis=axis, keepdims=True)
    spread = jnp.mean(center * center, axis=axis, keepdims=True)
    return center * lax.rsqrt(spread + epsilon)


def dot(a, b):
    return jnp.dot(a, b, preferred_element_type=F32)


def dot_nt(a, b):
    return lax.dot_general(a, b, NT, preferred_element_type=F32)


def lane_iota(rows, width=LANES):
    return lax.broadcasted_iota(jnp.int32, (rows, width), 1)


def row_iota(rows, width=LANES):
    return lax.broadcasted_iota(jnp.int32, (rows, width), 0)


def over(index, size):
    return lax.shift_right_logical(index, jnp.int32(size.bit_length() - 1))


def modulo(index, size):
    return lax.bitwise_and(index, jnp.int32(size - 1))


def call(body, out_shape, scratch, in_specs, name, limit=24, out_spec=VMEM):
    return pl.pallas_call(
        body,
        out_shape=out_shape,
        in_specs=in_specs,
        out_specs=out_spec if isinstance(out_spec, tuple) else jax.tree.map(lambda _: out_spec, out_shape),
        scratch_shapes=scratch,
        name=name,
        cost_estimate=pl.CostEstimate(flops=400_000_000, bytes_accessed=4_000_000, transcendentals=0),
        compiler_params=pltpu.CompilerParams(vmem_limit_bytes=min(limit * 1024 * 1024, MOST_VMEM)),
    )


class Plan:
    def __init__(self, n_row, n_col, x, pair, heads, outer, channels_out):
        self.n_row, self.n_col, self.n = n_row, n_col, n_row * n_col
        self.seqs, self.res, self.feat = x
        self.rows, self.cols, self.width = pair
        self.heads, self.outer = heads, outer
        self.hd = self.feat // heads
        self.total = self.res * n_col
        self.ok = False
        if any(size & (size - 1) for size in (heads, outer, self.hd, n_row, n_col)) or self.hd * 2 > LANES:
            return
        if self.seqs % n_col or self.width != LANES or heads != SUBLANES or self.cols != self.res:
            return
        if self.rows * n_row != self.total or self.feat % LANES:
            return
        self.split = 2
        if n_col % self.split:
            return
        self.n_group = n_col // self.split
        self.own = self.seqs // self.n_group
        self.seq_total = self.own * self.n_group * n_row
        if LANES % outer or outer % (LANES // outer):
            return
        self.pack = LANES // outer
        if self.rows % self.pack or self.cols % self.pack:
            return
        self.half = -(-self.rows // (self.split * self.pack)) * self.pack
        self.late = self.rows - self.half
        self.queries = n_row * self.half
        self.i_main = LANES // heads // 2
        self.i_rem = self.half - self.i_main
        if self.i_main != SUBLANES or 2 * self.i_rem != SUBLANES or self.i_main % self.pack or self.i_rem % self.pack or LANES % (self.i_rem * heads) or self.cols % SUBLANES:
            return
        self.km = self.i_main // self.pack
        self.main, self.rem = self.i_main * heads, self.i_rem * heads
        self.groups = self.cols // SUBLANES
        self.tall = -(-self.groups // 2)
        self.fold = LANES // self.rem
        if n_row % 2 or n_row % self.fold or n_row * self.main % (2 * LANES) or n_row * self.rem % (2 * LANES):
            return
        self.main_at = [(g % self.tall, g // self.tall * self.main) for g in range(self.groups)]
        spare = [(self.tall, f * self.rem) for f in range(self.fold)]
        if self.groups % 2:
            spare += [(self.tall - 1, self.main + f * self.rem) for f in range(self.main // self.rem)]
        if len(spare) < self.groups:
            return
        self.rem_at = spare[:self.groups]
        self.bias_rows = (self.tall + 1) * SUBLANES
        self.per = n_row // n_col
        if n_row % n_col or self.per * self.rows != self.cols:
            return
        self.lk, self.rk = self.rows // self.pack, self.cols // self.pack
        self.hk = self.half // self.pack
        self.ek = self.lk - self.hk
        chunks = max(self.ek + self.per * self.hk, self.hk + self.per * self.ek)
        self.side_rows = -(-chunks * self.own // 16) * 16
        self.cpad = -(-self.cols // 16) * 16
        if self.width % self.n:
            return
        self.ch = self.width // self.n
        if 2 * self.ch != SUBLANES:
            return
        self.q = LANES // self.cols
        self.ig = -(-self.rows // self.q)
        self.ipad = self.ig * self.q
        self.jslot = self.per * self.ipad
        if self.q * self.jslot > LANES:
            return
        self.m = n_row * self.ig
        self.edge_rows = self.ig * SUBLANES
        self.ok = True

    def j_base(self, c):
        return (c // self.q) * LANES + (c % self.q) * self.jslot


def bias_kernel(p, col_ref, pair_hbm, w_hbm, x_hbm, *refs):
    out_hbm, *part_hbm = refs[:p.n_col + 1]
    pair_ref, w_ref, x_ref, piece_ref, sems, out_sems, part_sems = refs[p.n_col + 1:]
    copies = [pltpu.make_async_copy(pair_hbm, pair_ref, sems.at[0]), pltpu.make_async_copy(w_hbm, w_ref, sems.at[1]),
              pltpu.make_async_copy(x_hbm, x_ref, sems.at[2])]
    for copy in copies:
        copy.start()
    for copy in copies:
        copy.wait()
    parts = []
    for shift in range(p.n_col):
        group = over(lax.rem(col_ref[0] + shift, p.n_col), p.split)
        parts.append(pltpu.make_async_copy(x_ref.at[group], part_hbm[shift], part_sems.at[shift]))
        parts[-1].start()
    normed = standardize_features(pair_ref[...]).reshape(p.rows * p.cols, p.width)
    heads = p.heads

    def tile(many):
        spread = modulo(over(lane_iota(heads), many), heads) == row_iota(heads)
        return lax.dot_general(w_ref[...], jnp.where(spread, 1.0, 0.0).astype(BF16), (((0,), (0,)), ((), ())),
                               preferred_element_type=F32)

    main_w, rem_w = tile(p.i_main), tile(p.i_rem)
    main_slot, rem_slot = modulo(lane_iota(p.width), p.i_main), modulo(lane_iota(p.width), p.i_rem)
    at = lane_iota(SUBLANES)
    for h in range(p.split):
        main = jnp.zeros((p.cols, LANES), F32)
        rem = jnp.zeros((p.cols, LANES), F32)
        for m in range(p.half):
            i = h * p.late + m
            block = normed[i * p.cols:(i + 1) * p.cols].astype(BF16)
            if m < p.i_main:
                main += dot(block, jnp.where(main_slot == m, main_w, 0.0).astype(BF16))
            else:
                rem += dot(block, jnp.where(rem_slot == m - p.i_main, rem_w, 0.0).astype(BF16))
        blocks = [jnp.zeros((SUBLANES, LANES), F32) for _ in range(p.tall + 1)]
        for value, places, wide in ((main, p.main_at, p.main), (rem, p.rem_at, p.rem)):
            for g, (b, lane) in enumerate(places):
                here = (at >= lane) & (at < lane + wide)
                blocks[b] = jnp.where(here, value[g * SUBLANES:(g + 1) * SUBLANES], blocks[b])
        piece = jnp.concatenate(blocks, axis=0).astype(BF16)
        for c in range(h, p.n_col, p.split):
            piece_ref[c] = piece
    pieces = [pltpu.make_async_copy(piece_ref, out_hbm.at[pl.ds(r * p.n_col, p.n_col)], out_sems.at[r])
              for r in range(p.n_row)]
    for copy in pieces:
        copy.start()
    for copy in pieces + parts:
        copy.wait()


def pick_half(p, second, rows):
    main, rest = [], []
    for r in range(p.n_row):
        a, b = r * p.rows, r * p.rows + p.late
        main.append(jnp.where(second, rows[b:b + p.i_main], rows[a:a + p.i_main]))
        rest.append(jnp.where(second, rows[b + p.i_main:b + p.half], rows[a + p.i_main:a + p.half]))
    return jnp.concatenate(main + rest, axis=0)


def project_kernel(p, col_ref, *refs):
    x_refs = refs[:p.n_col]
    w_ref, q_ref, k_ref, v_ref, gate_ref, x_out, hold = refs[p.n_col:]
    me = col_ref[0]
    second = lax.rem(me, p.split) == 1
    for shift in range(p.n_col):
        hold[lax.rem(me + (p.n_col - shift), p.n_col)] = x_refs[shift][...].astype(F32)
    f = p.feat
    for s in range(p.own):
        x = jnp.concatenate([hold[c, s] for c in range(p.n_col)], axis=0)
        normed = standardize_features(x)
        x_out[s] = pick_half(p, second, x).astype(BF16)
        lines = dot(normed.astype(BF16), w_ref[:, f:3 * f])
        k_ref[s] = lines[:, :f].astype(BF16)
        v_ref[s] = lines[:, f:].astype(BF16)
        normed = pick_half(p, second, normed).astype(BF16)
        gate_ref[s] = jax.nn.sigmoid(dot(normed, w_ref[:, 3 * f:]))
        q_ref[s] = (dot(normed, w_ref[:, :f]) * p.hd ** (-0.5)).astype(BF16)


def attend_kernel(p, col_ref, q_ref, k_ref, v_ref, gate_ref, x_ref, bias_ref, wf_ref, ws_ref,
                  emb_ref, side_hbm, bias, four, lint, rint, send, side_ref, sems):
    h, t, f, m = p.heads, p.queries, p.feat, p.half
    at = lane_iota(SUBLANES)
    for first, places, wide in ((0, p.main_at, p.main), (p.n_row * p.main, p.rem_at, p.rem)):
        fold = LANES // wide
        slot = over(at, wide)
        for c in range(p.n_col):
            for b in range(p.n_row // fold):
                for g, (block, lane) in enumerate(places):
                    built = None
                    for u in range(fold):
                        piece = bias_ref[(b * fold + u) * p.n_col + c,
                                         block * SUBLANES:(block + 1) * SUBLANES].astype(F32)
                        turn = (u * wide - lane) % LANES
                        piece = pltpu.roll(piece, turn, axis=1) if turn else piece
                        built = piece if u == 0 else jnp.where(slot == u, piece, built)
                    row = c * p.cols + g * SUBLANES
                    bias[row:row + SUBLANES, first + b * LANES:first + (b + 1) * LANES] = built
    step = 2 * LANES
    lane, row = lane_iota(f, step), row_iota(f, step)
    blocks = []
    for many, wide, count in ((p.i_main, p.main, p.n_row * p.main // step), (p.i_rem, p.rem, p.n_row * p.rem // step)):
        own_head = over(row, p.hd) == modulo(over(lane, many), h)
        at = lane_iota(step // h, step)
        pick = jnp.where(row_iota(step // h, step) == over(at, wide) * many + modulo(at, many), 1.0, 0.0).astype(BF16)
        blocks += [(own_head, pick)] * count
    fit = LANES // p.hd
    head_lane, low = over(lane_iota(SUBLANES), p.hd), row_iota(SUBLANES) >= p.i_rem
    own_lane = [jnp.where(head_lane == g % fit, 1.0, 0.0) for g in range(h)]
    own_pair = [jnp.where(low, own_lane[g + 1], own_lane[g]) for g in range(0, h, 2)]
    empty = jnp.zeros((SUBLANES, LANES), F32)

    def only(rows, mask, tile):
        return jnp.concatenate([rows[:, n * LANES:(n + 1) * LANES] * mask if n == tile else empty
                                for n in range(f // LANES)], axis=1)

    new, tall, together = [], step // SUBLANES, 4
    for first in range(0, p.own, together):
        jobs = []
        for s in range(first, min(first + together, p.own)):
            q = q_ref[s].astype(F32)
            spread = []
            for r in range(p.n_row):
                rows = q[r * p.i_main:(r + 1) * p.i_main]
                spread += [only(rows, mask, g // fit) for g, mask in enumerate(own_lane)]
            for r in range(p.n_row):
                start = p.n_row * p.i_main + r * p.i_rem
                rows = jnp.concatenate([q[start:start + p.i_rem]] * 2, axis=0)
                spread += [only(rows, mask, 2 * g // fit) for g, mask in enumerate(own_pair)]
            for n in range(len(blocks)):
                jobs.append((s, n, jnp.concatenate(spread[n * tall:(n + 1) * tall], axis=0).astype(BF16)))
        v_t = {s: jnp.transpose(v_ref[s].astype(F32)).astype(BF16) for s in range(first, first + together)
               if s < p.own}
        scores = [dot_nt(k_ref[s], rows) + bias[:, n * step:(n + 1) * step] for s, n, rows in jobs]
        weights = [jnp.exp(score - jnp.max(score, axis=0, keepdims=True)) for score in scores]
        share = [1.0 / jnp.sum(weight, axis=0, keepdims=True) for weight in weights]
        mixed = [dot(v_t[s], weight.astype(BF16)) for (s, _, _), weight in zip(jobs, weights)]
        mixed = [jnp.where(blocks[n][0], value * part, 0.0).astype(BF16)
                 for (_, n, _), value, part in zip(jobs, mixed, share)]
        attended = [dot_nt(blocks[n][1], value) for (_, n, _), value in zip(jobs, mixed)]
        for i, at in enumerate(range(0, len(jobs), len(blocks))):
            rows = jnp.concatenate(attended[at:at + len(blocks)], axis=0)
            new.append((gate_ref[first + i] * rows).astype(BF16))
    new = dot(jnp.concatenate(new, axis=0), wf_ref[...])
    new = (x_ref[...].astype(F32).reshape(p.own * t, f) + new).astype(BF16).astype(F32)
    a, b = p.per * p.i_main, p.per * p.i_rem
    for s in range(p.own):
        for c in range(p.n_col):
            row, tail = s * t + c * a, s * t + p.n_row * p.i_main + c * b
            emb_ref[c, s] = jnp.concatenate([new[row:row + a], new[tail:tail + b]], axis=0).astype(BF16)
    sides = dot(standardize_features(new).astype(BF16), ws_ref[...])
    four[0] = sides[:, :LANES]
    four[1] = sides[:, LANES:]
    n4 = t // p.pack
    lane = over(lane_iota(n4), p.outer)
    for s in range(p.own):
        for side, woven in enumerate((lint, rint)):
            packed = four[side, pl.ds(s * t, n4, stride=p.pack), :]
            for a in range(1, p.pack):
                packed = jnp.where(lane == a, four[side, pl.ds(s * t + a, n4, stride=p.pack), :], packed)
            woven[pl.ds(s, n4, stride=p.own), :] = packed
    o = p.own

    def place(r, k):
        return (r * p.km + k if k < p.km else p.n_row * p.km + r * (p.hk - p.km) + k - p.km) * o

    def fill(left, right):
        for r in range(p.n_row):
            for c in range(p.n_col):
                d, row = r * p.n_col + c, 0
                spans = [(lint, place(r, k)) for k in left]
                spans += [(rint, place(c * p.per + u, k)) for u in range(p.per) for k in right]
                for source, start in spans:
                    send[d, row:row + o] = source[start:start + o]
                    row += o
                if row < p.side_rows:
                    send[d, row:p.side_rows] = jnp.zeros((p.side_rows - row, LANES), F32)
            block = slice(r * p.n_col, (r + 1) * p.n_col)
            side_ref[block] = send[block].astype(BF16)
            leave(r).start()

    def leave(r):
        block = pl.ds(r * p.n_col, p.n_col)
        return pltpu.make_async_copy(side_ref.at[block], side_hbm.at[block], sems.at[r])

    second = lax.rem(col_ref[0], p.split) == 1

    @pl.when(jnp.logical_not(second))
    def _():
        fill(range(p.ek), range(p.hk))

    @pl.when(second)
    def _():
        fill(range(p.hk), range(p.hk - p.ek, p.hk))

    for r in range(p.n_row):
        leave(r).wait()


def home_kernel(p, col_ref, *refs):
    part_refs = refs[:p.n_col]
    out_ref, hold = refs[p.n_col:]
    me = col_ref[0]
    for shift in range(p.n_col):
        hold[lax.rem(me + (p.n_col - shift), p.n_col)] = part_refs[shift][...].astype(F32)
    both = 2 * p.half - p.rows
    tail = p.per * p.i_main
    for g in range(p.n_group):
        for s in range(p.own):
            rows = []
            for u in range(p.per):
                for skip, half in ((0, hold[g * p.split, s]), (both, hold[g * p.split + 1, s])):
                    rows.append(half[u * p.i_main + min(skip, p.i_main):(u + 1) * p.i_main])
                    rows.append(half[tail + u * p.i_rem + max(skip - p.i_main, 0):tail + (u + 1) * p.i_rem])
            rows = [value for value in rows if value.shape[0]]
            out_ref[g * p.own + s] = jnp.concatenate(rows, axis=0).astype(BF16)


def outer_kernel(p, recv_ref, pair_ref, w_ref, wv_ref, wg_ref, wo_ref, mid_ref, edge_ref, gate_ref,
                 flat, rt, lhs, mid):
    flat[...] = recv_ref[...].reshape(p.n * p.side_rows, LANES).astype(F32)

    def chunk(h, k):
        return jnp.concatenate(
            [flat[pl.ds(h * p.side_rows + k * p.own + s, p.n // p.split, stride=p.split * p.side_rows), :]
             for s in range(p.own)], axis=0)

    hk, ek = p.hk, p.ek
    for u in range(p.per):
        for k in range(p.lk):
            value = chunk(0, ek + u * hk + k) if k < hk else chunk(1, hk + u * ek + k - hk)
            row = (u * p.lk + k) * LANES
            rt[row:row + LANES, :] = jnp.transpose(value)
    right = []
    for first in range(0, p.outer, p.pack):
        right.append(jnp.concatenate(
            [rt[pl.ds(first + d, p.cols, stride=p.outer), :] for d in range(p.pack)], axis=1))
    right = jnp.concatenate(right, axis=0).astype(BF16)
    at = over(lane_iota(p.seq_total), p.outer)
    left = []
    for g in range(p.lk):
        base = chunk(0, g) if g < ek else chunk(1, g - ek)
        turned = [base] + [pltpu.roll(base, t * p.outer, axis=1) for t in range(1, p.pack)]
        for a in range(p.pack):
            left.append(jnp.concatenate(
                [jnp.where(at == d, turned[(d - a) % p.pack], 0.0) for d in range(p.pack)], axis=0).astype(BF16))
    products = dot(right, jnp.concatenate(left, axis=1)) * (1.0 / p.seq_total)
    for i in range(p.rows):
        for g in range(p.outer // p.pack):
            lhs[i * p.cpad:i * p.cpad + p.cols, g * LANES:(g + 1) * LANES] = products[
                g * p.cols:(g + 1) * p.cols, i * LANES:(i + 1) * LANES].astype(BF16)
        if p.cpad > p.cols:
            lhs[i * p.cpad + p.cols:(i + 1) * p.cpad, :] = jnp.zeros((p.cpad - p.cols, lhs.shape[1]), BF16)
    update = dot(lhs[...], w_ref[...])
    for i in range(p.rows):
        fresh = (pair_ref[i].astype(F32) + update[i * p.cpad:i * p.cpad + p.cols]).astype(BF16)
        mid_ref[i] = fresh
        mid[i * p.cols:(i + 1) * p.cols, :] = fresh.astype(F32)
    tail = mid.shape[0] - p.rows * p.cols
    mid[p.rows * p.cols:, :] = jnp.zeros((tail, LANES), F32)
    step = p.q * p.cols
    for k in range(p.ig):
        normed = standardize_features(mid[k * step:k * step + LANES, :]).astype(BF16)
        value = dot_nt(wv_ref[...], normed)
        gate = jax.nn.sigmoid(dot_nt(wg_ref[...], normed))
        edge_ref[:, k * SUBLANES:(k + 1) * SUBLANES, :] = (gate * value).reshape(
            p.n, SUBLANES, LANES).astype(BF16)
        many = min(step, p.rows * p.cols - k * step)
        gate_ref[k * step:k * step + many, :] = jax.nn.sigmoid(dot(normed, wo_ref[...]))[:many]


def triangle_kernel(p, recv_ref, out_ref, flat, ls, rs, os, sb):
    for r in range(p.n_row):
        for c in range(p.n_col):
            flat[c, r * p.edge_rows:(r + 1) * p.edge_rows, :] = recv_ref[r * p.n_col + c].astype(F32)
    lane = lane_iota(p.m)
    part_of = jnp.broadcast_to(lane_iota(1) // p.jslot, (p.m, LANES))
    blocks = p.per * p.ig
    rs[...] = jnp.zeros_like(rs)
    for ch in range(p.ch):
        for c in range(p.n_col):
            left = flat[c, pl.ds(ch, p.m, stride=SUBLANES), :]
            right = flat[c, pl.ds(p.ch + ch, p.m, stride=SUBLANES), :]
            both = jnp.concatenate([left, right], axis=0).astype(BF16)
            for a in range(p.q):
                turn = (-a * p.cols) % LANES
                turned = pltpu.roll(both, turn, axis=1).astype(F32) if turn else None
                lt = turned[:p.m] if turn else left
                rt = turned[p.m:] if turn else right
                ls[ch, c, pl.ds(a, p.m, stride=p.q), :] = jnp.where(lane < p.cols, lt, 0.0)
                for first in range(0, p.n_col, p.q):
                    many = min(p.q, p.n_col - first) * blocks
                    rs[ch, c, pl.ds(p.j_base(first) + a, many, stride=p.q), :] = rt[
                        first * blocks:first * blocks + many]
    for ch in range(p.ch):
        lfull = jnp.concatenate([ls[ch, c] for c in range(p.n_col)], axis=1).astype(BF16)
        rfull = jnp.concatenate([rs[ch, c] for c in range(p.n_col)], axis=1).astype(BF16)
        summed = dot_nt(lfull, rfull)
        for b in range(summed.shape[1] // LANES):
            os[ch, b] = summed[:, b * LANES:(b + 1) * LANES]
        rows = [[os[ch, b, pl.ds(a, p.m, stride=p.q), :] for a in range(p.q)]
                for b in range(summed.shape[1] // LANES)]
        for c in range(p.n_col):
            b, part = c // p.q, c % p.q
            packed = None
            for a in range(p.q):
                turn = ((a - part) * p.jslot) % LANES
                piece = pltpu.roll(rows[b][a].astype(BF16), turn, axis=1).astype(F32) if turn else rows[b][a]
                packed = piece if packed is None else jnp.where(part_of == a, piece, packed)
            sb[c, pl.ds(ch, p.m, stride=p.ch), :] = packed
    for r in range(p.n_row):
        for c in range(p.n_col):
            for k in range(p.ig):
                row = (r * p.ig + k) * p.ch
                out_ref[r * p.n_col + c, k] = sb[c, row:row + p.ch, :].astype(BF16)


def final_kernel(p, recv_ref, mid_ref, gate_ref, w_ref, out_hbm, flat, hold, update, out_ref, sems):
    copies = []
    for k in range(p.ig):
        for d in range(p.n):
            flat[k, d * p.ch:(d + 1) * p.ch, :] = recv_ref[d, k].astype(F32)
    for k in range(p.ig):
        normed = jnp.transpose(standardize_features(flat[k], axis=0)).astype(BF16)
        hold[k] = dot(normed, w_ref[...])
        first, last = k * p.q, min((k + 1) * p.q, p.rows)
        for i in range(first, last):
            for u in range(p.per):
                row = (i - first) * p.jslot + u * p.ipad
                update[i * p.cols + u * p.rows:i * p.cols + (u + 1) * p.rows, :] = hold[k, row:row + p.rows, :]
        span = slice(first * p.cols, last * p.cols)
        fresh = mid_ref[first:last].astype(F32) + (gate_ref[span] * update[span]).reshape(
            last - first, p.cols, p.width)
        out_ref[first:last] = fresh.astype(BF16)
        rows = pl.ds(first, last - first)
        copies.append(pltpu.make_async_copy(out_ref.at[rows], out_hbm.at[rows], sems.at[k]))
        copies[-1].start()
    for copy in copies:
        copy.wait()


def fast(p, x, pair, w_in, w_out, w_bias, w_side, w_outer, w_tri, w_last):
    col = lax.axis_index("col")
    n, ch, width = p.n, p.ch, p.width
    sds = jax.ShapeDtypeStruct

    side_w = jnp.concatenate([w_side[:, :p.outer]] * p.pack + [w_side[:, p.outer:]] * p.pack, axis=1)
    by_d = jnp.transpose(w_outer.reshape(p.outer, p.outer, width), (1, 0, 2)).reshape(w_outer.shape)
    blocks = jnp.transpose(w_tri.reshape(width, 5, width), (1, 2, 0)).reshape(5, n, ch, width)
    value_w = jnp.concatenate([blocks[0], blocks[2]], axis=1).reshape(n * 2 * ch, width)
    gate_w = jnp.concatenate([blocks[1], blocks[3]], axis=1).reshape(n * 2 * ch, width)
    own_gate_w = w_tri[:, 4 * width:]

    at = col.reshape(1)
    chunks = (p.own, p.res, p.feat)
    piece, *parts = call(
        functools.partial(bias_kernel, p), (sds((n, p.bias_rows, LANES), BF16),) + (sds(chunks, BF16),) * p.n_col,
        [pltpu.VMEM(pair.shape, BF16), pltpu.VMEM((p.heads, width), BF16), pltpu.VMEM((p.n_group,) + chunks, BF16),
         pltpu.VMEM((p.n_col, p.bias_rows, LANES), BF16), pltpu.SemaphoreType.DMA((3,)),
         pltpu.SemaphoreType.DMA((p.n_row,)), pltpu.SemaphoreType.DMA((p.n_col,))],
        [SMEM] + [HBM] * 3, "bias", limit=64, out_spec=HBM)(at, pair, w_bias.T, x.reshape((p.n_group,) + chunks))
    bias = lax.all_to_all(piece, ALL, 0, 0, tiled=True)

    def ring(parts):
        return [parts[0]] + [
            lax.ppermute(parts[shift], "col", [(c, (c + shift) % p.n_col) for c in range(p.n_col)])
            for shift in range(1, p.n_col)]

    parts = ring(parts)
    mine, every = (p.own, p.queries, p.feat), (p.own, p.total, p.feat)
    q, k, v, gate, rest = call(
        functools.partial(project_kernel, p),
        (sds(mine, BF16), sds(every, BF16), sds(every, BF16), sds(mine, F32), sds(mine, BF16)),
        [pltpu.VMEM((p.n_col, p.own, p.res, p.feat), F32)],
        [SMEM] + [VMEM] * (p.n_col + 1), "project")(at, *parts, w_in)
    emb, sides = call(
        functools.partial(attend_kernel, p),
        (sds((p.n_col, p.own, p.per * p.half, p.feat), BF16), sds((n, p.side_rows, LANES), BF16)),
        [pltpu.VMEM((p.total, p.queries * p.heads), F32), pltpu.VMEM((2, p.own * p.queries, LANES), F32)]
        + [pltpu.VMEM((p.queries // p.pack * p.own, LANES), F32)] * 2
        + [pltpu.VMEM((n, p.side_rows, LANES), F32), pltpu.VMEM((n, p.side_rows, LANES), BF16),
           pltpu.SemaphoreType.DMA((p.n_row,))],
        [SMEM] + [VMEM] * 8, "attend", out_spec=(VMEM, HBM))(at, q, k, v, gate, rest, bias, w_out, side_w)

    sides = lax.all_to_all(sides, ALL, 0, 0, tiled=True)

    parts = ring([lax.dynamic_index_in_dim(emb, lax.rem(col + shift, p.n_col), 0, keepdims=False)
                  for shift in range(p.n_col)])
    home = call(functools.partial(home_kernel, p), sds(x.shape, BF16),
                [pltpu.VMEM((p.n_col, p.own, p.per * p.half, p.feat), F32)],
                [SMEM] + [VMEM] * p.n_col, "home")(at, *parts)

    mid, edges, out_gate = call(
        functools.partial(outer_kernel, p),
        (sds((p.rows, p.cols, width), BF16), sds((n, p.edge_rows, LANES), BF16),
         sds((p.rows * p.cols, width), F32)),
        [pltpu.VMEM((n * p.side_rows, LANES), F32),
         pltpu.VMEM((p.rk * LANES, p.seq_total), F32),
         pltpu.VMEM((p.rows * p.cpad, p.outer * p.outer), BF16),
         pltpu.VMEM(((p.ig - 1) * p.q * p.cols + LANES, LANES), F32)],
        [VMEM] * 6, "outer")(sides, pair, by_d, value_w, gate_w, own_gate_w)

    edges, home = lax.optimization_barrier((edges, home))
    edges = lax.all_to_all(edges, ALL, 0, 0, tiled=True)
    n_lane = p.j_base(p.n_col - 1) // LANES + 1
    back = call(
        functools.partial(triangle_kernel, p), sds((n, p.ig, ch, LANES), BF16),
        [pltpu.VMEM((p.n_col, p.n_row * p.edge_rows, LANES), F32),
         pltpu.VMEM((ch, p.n_col, p.m * p.q, LANES), F32),
         pltpu.VMEM((ch, p.n_col, n_lane * LANES, LANES), F32),
         pltpu.VMEM((ch, n_lane, p.m * p.q, LANES), F32),
         pltpu.VMEM((p.n_col, p.m * ch, LANES), F32)],
        [VMEM], "triangle")(edges)

    back = lax.all_to_all(back, ALL, 0, 0, tiled=True)
    state = call(
        functools.partial(final_kernel, p), sds((p.rows, p.cols, width), BF16),
        [pltpu.VMEM((p.ig, width, LANES), F32), pltpu.VMEM((p.ig, LANES, LANES), F32),
         pltpu.VMEM((p.rows * p.cols, LANES), F32), pltpu.VMEM((p.rows, p.cols, width), BF16),
         pltpu.SemaphoreType.DMA((p.ig,))],
        [VMEM] * 4, "final", out_spec=HBM)(back, mid, out_gate, w_last)
    return home, state


def general(
    stack_embedding,
    pair_representation,
    mixing_entry_coefficients,
    mixing_final_coefficients,
    pair_bias_matrix,
    tensor_side_coefficients,
    outer_output_weight,
    triangle_projection_weight,
    triangle_output_weight,
):
    sequences_per_device, residues_per_device, alignment_channels = stack_embedding.shape
    rows_dev = pair_representation.shape[0]
    pair_width = pair_representation.shape[2]
    number_heads = pair_bias_matrix.shape[1]
    head_channels = alignment_channels // number_heads
    outer_width = tensor_side_coefficients.shape[1] // 2
    row_count = lax.axis_size("row")
    seq_total = sequences_per_device * row_count
    row_index = lax.axis_index("row")
    normalized_input = (
        standardize_features(stack_embedding).astype(jnp.bfloat16).reshape(-1, alignment_channels)
    )
    mapped_lines = jnp.dot(
        normalized_input, mixing_entry_coefficients, preferred_element_type=jnp.float32
    )
    stack_probe_vectors = (
        (mapped_lines[:, :alignment_channels] * head_channels ** (-0.5))
        .astype(jnp.bfloat16)
        .reshape(sequences_per_device, residues_per_device, number_heads, head_channels)
    )
    stack_lookup_vectors = (
        mapped_lines[:, alignment_channels : 2 * alignment_channels]
        .astype(jnp.bfloat16)
        .reshape(sequences_per_device, residues_per_device, alignment_channels)
    )
    stack_content_vectors = (
        mapped_lines[:, 2 * alignment_channels : 3 * alignment_channels]
        .astype(jnp.bfloat16)
        .reshape(sequences_per_device, residues_per_device, alignment_channels)
    )
    sigmoid_factors = jax.nn.sigmoid(mapped_lines[:, 3 * alignment_channels :]).reshape(
        sequences_per_device, residues_per_device, alignment_channels
    )
    pair_normed = standardize_features(pair_representation).astype(jnp.bfloat16)
    bias_local = jnp.einsum(
        "ijc,ch->hij", pair_normed, pair_bias_matrix, preferred_element_type=jnp.float32
    ).astype(jnp.bfloat16)
    bias_all = lax.all_gather(bias_local, "row", axis=1, tiled=True)
    bias_query = lax.all_to_all(bias_all, "col", split_axis=1, concat_axis=2, tiled=True)
    best_score = jnp.full(
        (sequences_per_device, number_heads, residues_per_device), -1e30, jnp.float32
    )
    received_keys = lax.all_gather(stack_lookup_vectors, "col", axis=1, tiled=True)
    received_values = lax.all_gather(stack_content_vectors, "col", axis=1, tiled=True)
    key_count = received_keys.shape[1]
    received_keys = received_keys.reshape(
        sequences_per_device, key_count, number_heads, head_channels
    )
    received_values = received_values.reshape(
        sequences_per_device, key_count, number_heads, head_channels
    )
    bias_piece = bias_query.astype(jnp.float32)
    scores = (
        jnp.einsum(
            "yeca,yica->ycei",
            stack_probe_vectors,
            received_keys,
            preferred_element_type=jnp.float32,
        )
        + bias_piece[None]
    )
    next_best = jnp.maximum(best_score, jnp.max(scores, axis=-1))
    weights = jnp.exp(scores - next_best[..., None])
    next_sum = jnp.sum(weights, axis=-1)
    update = jnp.einsum(
        "shqk,skhd->sqhd",
        weights.astype(jnp.bfloat16),
        received_values,
        preferred_element_type=jnp.float32,
    )
    weighted_mixture = (update / jnp.transpose(next_sum, (0, 2, 1))[..., None]).reshape(
        sequences_per_device, residues_per_device, alignment_channels
    )
    scaled_mixture = (sigmoid_factors * weighted_mixture).astype(jnp.bfloat16)
    stack_increment = jnp.dot(
        scaled_mixture.reshape(-1, alignment_channels),
        mixing_final_coefficients,
        preferred_element_type=jnp.float32,
    ).reshape(sequences_per_device, residues_per_device, alignment_channels)
    stack_embedding_updated = (stack_embedding.astype(jnp.float32) + stack_increment).astype(
        jnp.bfloat16
    )
    tensor_standardized = (
        standardize_features(stack_embedding_updated)
        .astype(jnp.bfloat16)
        .reshape(-1, alignment_channels)
    )
    sides = jnp.dot(
        tensor_standardized, tensor_side_coefficients, preferred_element_type=jnp.float32
    ).astype(jnp.bfloat16)
    sides = sides.reshape(sequences_per_device, residues_per_device, 2 * outer_width)
    left_side = sides[..., :outer_width]
    right_side = sides[..., outer_width:]
    left_wide = lax.all_gather(left_side, "col", axis=1, tiled=True)
    left_every, right_all = (
        lax.all_gather(left_wide, "row", axis=0, tiled=True),
        lax.all_gather(right_side, "row", axis=0, tiled=True),
    )
    left_all = lax.dynamic_slice_in_dim(left_every, row_index * rows_dev, rows_dev, 1)
    products = jnp.einsum("sic,sjd->ijcd", left_all, right_all, preferred_element_type=jnp.float32)
    averaged = (products * (1.0 / seq_total)).astype(jnp.bfloat16)
    outer_update = jnp.dot(
        averaged.reshape(-1, outer_width * outer_width),
        outer_output_weight,
        preferred_element_type=jnp.float32,
    )
    pair_mid = (
        pair_representation.astype(jnp.float32)
        + outer_update.reshape(rows_dev, residues_per_device, pair_width)
    ).astype(jnp.bfloat16)
    tri_normed = standardize_features(pair_mid).astype(jnp.bfloat16).reshape(-1, pair_width)
    tri_parts = jnp.dot(
        tri_normed, triangle_projection_weight, preferred_element_type=jnp.float32
    ).reshape(rows_dev, residues_per_device, 5 * pair_width)
    left_edge = (
        jax.nn.sigmoid(tri_parts[..., pair_width : 2 * pair_width]) * tri_parts[..., :pair_width]
    ).astype(jnp.bfloat16)
    right_edge = (
        jax.nn.sigmoid(tri_parts[..., 3 * pair_width : 4 * pair_width])
        * tri_parts[..., 2 * pair_width : 3 * pair_width]
    ).astype(jnp.bfloat16)
    out_gate = jax.nn.sigmoid(tri_parts[..., 4 * pair_width :])
    right_rows = lax.all_gather(right_edge, "row", axis=0, tiled=True)
    right_query = lax.all_to_all(right_rows, "col", split_axis=0, concat_axis=1, tiled=True)
    arrived = lax.all_gather(left_edge, "col", axis=1, tiled=True)
    summed = jnp.einsum("ikc,jkc->ijc", arrived, right_query, preferred_element_type=jnp.float32)
    tri_ln = standardize_features(summed).astype(jnp.bfloat16)
    tri_update = jnp.dot(
        tri_ln.reshape(-1, pair_width), triangle_output_weight, preferred_element_type=jnp.float32
    ).reshape(rows_dev, residues_per_device, pair_width)
    pair_state_next = (pair_mid.astype(jnp.float32) + out_gate * tri_update).astype(jnp.bfloat16)
    return (stack_embedding_updated, pair_state_next)


def shards(x, pair, w_in, w_out, w_bias, w_side, w_outer, w_tri, w_last):
    p = Plan(lax.axis_size("row"), lax.axis_size("col"), x.shape, pair.shape, w_bias.shape[1],
             w_side.shape[1] // 2, w_last.shape[1])
    path = functools.partial(fast, p) if p.ok else general
    return path(x, pair, w_in, w_out, w_bias, w_side, w_outer, w_tri, w_last)


def solution(mesh):
    return jax.shard_map(
        shards,
        mesh=mesh,
        in_specs=(P("row", "col", None), P("row", "col", None), P(), P(), P(), P(), P(), P(), P()),
        out_specs=(P("row", "col", None), P("row", "col", None)),
        check_vma=False,
    )
```

```python
import functools

import jax
import jax.numpy as jnp
from jax import lax
from jax.experimental import pallas as pl
from jax.experimental.pallas import tpu as pltpu
from jax.sharding import PartitionSpec as P

epsilon = 1e-05
LANES = 128
MOST_VMEM = 67_043_328
SUBLANES = 8
F32 = jnp.float32
BF16 = jnp.bfloat16
ALL = ("row", "col")
NT = (((1,), (1,)), ((), ()))
VMEM = pl.BlockSpec(memory_space=pltpu.VMEM)
SMEM = pl.BlockSpec(memory_space=pltpu.SMEM)
HBM = pl.BlockSpec(memory_space=pltpu.HBM)


def standardize_features(inputs, axis=-1):
    inputs = inputs.astype(jnp.float32)
    center = inputs - jnp.mean(inputs, axis=axis, keepdims=True)
    spread = jnp.mean(center * center, axis=axis, keepdims=True)
    return center * lax.rsqrt(spread + epsilon)


def dot(a, b):
    return jnp.dot(a, b, preferred_element_type=F32)


def dot_nt(a, b):
    return lax.dot_general(a, b, NT, preferred_element_type=F32)


def lane_iota(rows, width=LANES):
    return lax.broadcasted_iota(jnp.int32, (rows, width), 1)


def row_iota(rows, width=LANES):
    return lax.broadcasted_iota(jnp.int32, (rows, width), 0)


def over(index, size):
    return lax.shift_right_logical(index, jnp.int32(size.bit_length() - 1))


def modulo(index, size):
    return lax.bitwise_and(index, jnp.int32(size - 1))


def call(body, out_shape, scratch, in_specs, name, limit=24, out_spec=VMEM):
    return pl.pallas_call(
        body,
        out_shape=out_shape,
        in_specs=in_specs,
        out_specs=out_spec if isinstance(out_spec, tuple) else jax.tree.map(lambda _: out_spec, out_shape),
        scratch_shapes=scratch,
        name=name,
        cost_estimate=pl.CostEstimate(flops=400_000_000, bytes_accessed=4_000_000, transcendentals=0),
        compiler_params=pltpu.CompilerParams(vmem_limit_bytes=min(limit * 1024 * 1024, MOST_VMEM)),
    )


class Plan:
    def __init__(self, n_row, n_col, x, pair, heads, outer, channels_out):
        self.n_row, self.n_col, self.n = n_row, n_col, n_row * n_col
        self.seqs, self.res, self.feat = x
        self.rows, self.cols, self.width = pair
        self.heads, self.outer = heads, outer
        self.hd = self.feat // heads
        self.total = self.res * n_col
        self.ok = False
        if any(size & (size - 1) for size in (heads, outer, self.hd, n_row, n_col)) or self.hd * 2 > LANES:
            return
        if self.seqs % n_col or self.width != LANES or heads != SUBLANES or self.cols != self.res:
            return
        if self.rows * n_row != self.total or self.feat % LANES:
            return
        self.split = 2
        if n_col % self.split:
            return
        self.n_group = n_col // self.split
        self.own = self.seqs // self.n_group
        self.seq_total = self.own * self.n_group * n_row
        if LANES % outer or outer % (LANES // outer):
            return
        self.pack = LANES // outer
        if self.rows % self.pack or self.cols % self.pack:
            return
        self.half = -(-self.rows // (self.split * self.pack)) * self.pack
        self.late = self.rows - self.half
        self.queries = n_row * self.half
        self.i_main = LANES // heads // 2
        self.i_rem = self.half - self.i_main
        if self.i_main != SUBLANES or 2 * self.i_rem != SUBLANES or self.i_main % self.pack or self.i_rem % self.pack or LANES % (self.i_rem * heads) or self.cols % SUBLANES:
            return
        self.km = self.i_main // self.pack
        self.main, self.rem = self.i_main * heads, self.i_rem * heads
        self.groups = self.cols // SUBLANES
        self.tall = -(-self.groups // 2)
        self.fold = LANES // self.rem
        if n_row % 2 or n_row % self.fold or n_row * self.main % (2 * LANES) or n_row * self.rem % (2 * LANES):
            return
        self.main_at = [(g % self.tall, g // self.tall * self.main) for g in range(self.groups)]
        spare = [(self.tall, f * self.rem) for f in range(self.fold)]
        if self.groups % 2:
            spare += [(self.tall - 1, self.main + f * self.rem) for f in range(self.main // self.rem)]
        if len(spare) < self.groups:
            return
        self.rem_at = spare[:self.groups]
        self.bias_rows = (self.tall + 1) * SUBLANES
        self.per = n_row // n_col
        if n_row % n_col or self.per * self.rows != self.cols:
            return
        self.lk, self.rk = self.rows // self.pack, self.cols // self.pack
        self.hk = self.half // self.pack
        self.ek = self.lk - self.hk
        chunks = max(self.ek + self.per * self.hk, self.hk + self.per * self.ek)
        self.side_rows = -(-chunks * self.own // 16) * 16
        self.cpad = -(-self.cols // 16) * 16
        if self.width % self.n:
            return
        self.ch = self.width // self.n
        if 2 * self.ch != SUBLANES:
            return
        self.q = LANES // self.cols
        self.ig = -(-self.rows // self.q)
        self.ipad = self.ig * self.q
        self.jslot = self.per * self.ipad
        if self.q * self.jslot > LANES:
            return
        self.m = n_row * self.ig
        self.edge_rows = self.ig * SUBLANES
        self.ok = True

    def j_base(self, c):
        return (c // self.q) * LANES + (c % self.q) * self.jslot


def bias_kernel(p, col_ref, pair_hbm, w_hbm, x_hbm, *refs):
    out_hbm, *part_hbm = refs[:p.n_col + 1]
    pair_ref, w_ref, x_ref, piece_ref, sems, out_sems, part_sems = refs[p.n_col + 1:]
    copies = [pltpu.make_async_copy(pair_hbm, pair_ref, sems.at[0]), pltpu.make_async_copy(w_hbm, w_ref, sems.at[1]),
              pltpu.make_async_copy(x_hbm, x_ref, sems.at[2])]
    for copy in copies:
        copy.start()
    for copy in copies:
        copy.wait()
    parts = []
    for shift in range(p.n_col):
        group = over(lax.rem(col_ref[0] + shift, p.n_col), p.split)
        parts.append(pltpu.make_async_copy(x_ref.at[group], part_hbm[shift], part_sems.at[shift]))
        parts[-1].start()
    normed = standardize_features(pair_ref[...]).reshape(p.rows * p.cols, p.width)
    heads = p.heads

    def tile(many):
        spread = modulo(over(lane_iota(heads), many), heads) == row_iota(heads)
        return lax.dot_general(w_ref[...], jnp.where(spread, 1.0, 0.0).astype(BF16), (((0,), (0,)), ((), ())),
                               preferred_element_type=F32)

    main_w, rem_w = tile(p.i_main), tile(p.i_rem)
    main_slot, rem_slot = modulo(lane_iota(p.width), p.i_main), modulo(lane_iota(p.width), p.i_rem)
    at = lane_iota(SUBLANES)
    for h in range(p.split):
        main = jnp.zeros((p.cols, LANES), F32)
        rem = jnp.zeros((p.cols, LANES), F32)
        for m in range(p.half):
            i = h * p.late + m
            block = normed[i * p.cols:(i + 1) * p.cols].astype(BF16)
            if m < p.i_main:
                main += dot(block, jnp.where(main_slot == m, main_w, 0.0).astype(BF16))
            else:
                rem += dot(block, jnp.where(rem_slot == m - p.i_main, rem_w, 0.0).astype(BF16))
        blocks = [jnp.zeros((SUBLANES, LANES), F32) for _ in range(p.tall + 1)]
        for value, places, wide in ((main, p.main_at, p.main), (rem, p.rem_at, p.rem)):
            for g, (b, lane) in enumerate(places):
                here = (at >= lane) & (at < lane + wide)
                blocks[b] = jnp.where(here, value[g * SUBLANES:(g + 1) * SUBLANES], blocks[b])
        piece = jnp.concatenate(blocks, axis=0).astype(BF16)
        for c in range(h, p.n_col, p.split):
            piece_ref[c] = piece
    pieces = [pltpu.make_async_copy(piece_ref, out_hbm.at[pl.ds(r * p.n_col, p.n_col)], out_sems.at[r])
              for r in range(p.n_row)]
    for copy in pieces:
        copy.start()
    for copy in pieces + parts:
        copy.wait()


def pick_half(p, second, rows):
    main, rest = [], []
    for r in range(p.n_row):
        a, b = r * p.rows, r * p.rows + p.late
        main.append(jnp.where(second, rows[b:b + p.i_main], rows[a:a + p.i_main]))
        rest.append(jnp.where(second, rows[b + p.i_main:b + p.half], rows[a + p.i_main:a + p.half]))
    return jnp.concatenate(main + rest, axis=0)


def project_kernel(p, col_ref, *refs):
    x_refs = refs[:p.n_col]
    w_ref, q_ref, k_ref, v_ref, gate_ref, x_out, hold = refs[p.n_col:]
    me = col_ref[0]
    second = lax.rem(me, p.split) == 1
    for shift in range(p.n_col):
        hold[lax.rem(me + (p.n_col - shift), p.n_col)] = x_refs[shift][...].astype(F32)
    f = p.feat
    for s in range(p.own):
        x = jnp.concatenate([hold[c, s] for c in range(p.n_col)], axis=0)
        normed = standardize_features(x)
        x_out[s] = pick_half(p, second, x).astype(BF16)
        lines = dot(normed.astype(BF16), w_ref[:, f:3 * f])
        k_ref[s] = lines[:, :f].astype(BF16)
        v_ref[s] = lines[:, f:].astype(BF16)
        normed = pick_half(p, second, normed).astype(BF16)
        gate_ref[s] = jax.nn.sigmoid(dot(normed, w_ref[:, 3 * f:]))
        q_ref[s] = (dot(normed, w_ref[:, :f]) * p.hd ** (-0.5)).astype(BF16)


def attend_kernel(p, col_ref, q_ref, k_ref, v_ref, gate_ref, x_ref, bias_ref, wf_ref, ws_ref,
                  emb_ref, side_hbm, bias, four, lint, rint, send, side_ref, sems):
    h, t, f, m = p.heads, p.queries, p.feat, p.half
    at = lane_iota(SUBLANES)
    for first, places, wide in ((0, p.main_at, p.main), (p.n_row * p.main, p.rem_at, p.rem)):
        fold = LANES // wide
        slot = over(at, wide)
        for c in range(p.n_col):
            for b in range(p.n_row // fold):
                for g, (block, lane) in enumerate(places):
                    built = None
                    for u in range(fold):
                        piece = bias_ref[(b * fold + u) * p.n_col + c,
                                         block * SUBLANES:(block + 1) * SUBLANES].astype(F32)
                        turn = (u * wide - lane) % LANES
                        piece = pltpu.roll(piece, turn, axis=1) if turn else piece
                        built = piece if u == 0 else jnp.where(slot == u, piece, built)
                    row = c * p.cols + g * SUBLANES
                    bias[row:row + SUBLANES, first + b * LANES:first + (b + 1) * LANES] = built
    step = 2 * LANES
    lane, row = lane_iota(f, step), row_iota(f, step)
    blocks = []
    for many, wide, count in ((p.i_main, p.main, p.n_row * p.main // step), (p.i_rem, p.rem, p.n_row * p.rem // step)):
        own_head = over(row, p.hd) == modulo(over(lane, many), h)
        at = lane_iota(step // h, step)
        pick = jnp.where(row_iota(step // h, step) == over(at, wide) * many + modulo(at, many), 1.0, 0.0).astype(BF16)
        blocks += [(own_head, pick)] * count
    fit = LANES // p.hd
    head_lane, low = over(lane_iota(SUBLANES), p.hd), row_iota(SUBLANES) >= p.i_rem
    own_lane = [jnp.where(head_lane == g % fit, 1.0, 0.0) for g in range(h)]
    own_pair = [jnp.where(low, own_lane[g + 1], own_lane[g]) for g in range(0, h, 2)]
    empty = jnp.zeros((SUBLANES, LANES), F32)

    def only(rows, mask, tile):
        return jnp.concatenate([rows[:, n * LANES:(n + 1) * LANES] * mask if n == tile else empty
                                for n in range(f // LANES)], axis=1)

    new, tall, together = [], step // SUBLANES, 4
    for first in range(0, p.own, together):
        jobs = []
        for s in range(first, min(first + together, p.own)):
            q = q_ref[s].astype(F32)
            spread = []
            for r in range(p.n_row):
                rows = q[r * p.i_main:(r + 1) * p.i_main]
                spread += [only(rows, mask, g // fit) for g, mask in enumerate(own_lane)]
            for r in range(p.n_row):
                start = p.n_row * p.i_main + r * p.i_rem
                rows = jnp.concatenate([q[start:start + p.i_rem]] * 2, axis=0)
                spread += [only(rows, mask, 2 * g // fit) for g, mask in enumerate(own_pair)]
            for n in range(len(blocks)):
                jobs.append((s, n, jnp.concatenate(spread[n * tall:(n + 1) * tall], axis=0).astype(BF16)))
        v_t = {s: jnp.transpose(v_ref[s].astype(F32)).astype(BF16) for s in range(first, first + together)
               if s < p.own}
        scores = [dot_nt(k_ref[s], rows) + bias[:, n * step:(n + 1) * step] for s, n, rows in jobs]
        weights = [jnp.exp(score - jnp.max(score, axis=0, keepdims=True)) for score in scores]
        share = [1.0 / jnp.sum(weight, axis=0, keepdims=True) for weight in weights]
        mixed = [dot(v_t[s], weight.astype(BF16)) for (s, _, _), weight in zip(jobs, weights)]
        mixed = [jnp.where(blocks[n][0], value * part, 0.0).astype(BF16)
                 for (_, n, _), value, part in zip(jobs, mixed, share)]
        attended = [dot_nt(blocks[n][1], value) for (_, n, _), value in zip(jobs, mixed)]
        for i, at in enumerate(range(0, len(jobs), len(blocks))):
            rows = jnp.concatenate(attended[at:at + len(blocks)], axis=0)
            new.append((gate_ref[first + i] * rows).astype(BF16))
    new = dot(jnp.concatenate(new, axis=0), wf_ref[...])
    new = (x_ref[...].astype(F32).reshape(p.own * t, f) + new).astype(BF16).astype(F32)
    a, b = p.per * p.i_main, p.per * p.i_rem
    for s in range(p.own):
        for c in range(p.n_col):
            row, tail = s * t + c * a, s * t + p.n_row * p.i_main + c * b
            emb_ref[c, s] = jnp.concatenate([new[row:row + a], new[tail:tail + b]], axis=0).astype(BF16)
    sides = dot(standardize_features(new).astype(BF16), ws_ref[...])
    four[0] = sides[:, :LANES]
    four[1] = sides[:, LANES:]
    n4 = t // p.pack
    lane = over(lane_iota(n4), p.outer)
    for s in range(p.own):
        for side, woven in enumerate((lint, rint)):
            packed = four[side, pl.ds(s * t, n4, stride=p.pack), :]
            for a in range(1, p.pack):
                packed = jnp.where(lane == a, four[side, pl.ds(s * t + a, n4, stride=p.pack), :], packed)
            woven[pl.ds(s, n4, stride=p.own), :] = packed
    o = p.own

    def place(r, k):
        return (r * p.km + k if k < p.km else p.n_row * p.km + r * (p.hk - p.km) + k - p.km) * o

    def fill(left, right):
        for r in range(p.n_row):
            for c in range(p.n_col):
                d, row = r * p.n_col + c, 0
                spans = [(lint, place(r, k)) for k in left]
                spans += [(rint, place(c * p.per + u, k)) for u in range(p.per) for k in right]
                for source, start in spans:
                    send[d, row:row + o] = source[start:start + o]
                    row += o
                if row < p.side_rows:
                    send[d, row:p.side_rows] = jnp.zeros((p.side_rows - row, LANES), F32)
            block = slice(r * p.n_col, (r + 1) * p.n_col)
            side_ref[block] = send[block].astype(BF16)
            leave(r).start()

    def leave(r):
        block = pl.ds(r * p.n_col, p.n_col)
        return pltpu.make_async_copy(side_ref.at[block], side_hbm.at[block], sems.at[r])

    second = lax.rem(col_ref[0], p.split) == 1

    @pl.when(jnp.logical_not(second))
    def _():
        fill(range(p.ek), range(p.hk))

    @pl.when(second)
    def _():
        fill(range(p.hk), range(p.hk - p.ek, p.hk))

    for r in range(p.n_row):
        leave(r).wait()


def home_kernel(p, col_ref, *refs):
    part_refs = refs[:p.n_col]
    out_ref, hold = refs[p.n_col:]
    me = col_ref[0]
    for shift in range(p.n_col):
        hold[lax.rem(me + (p.n_col - shift), p.n_col)] = part_refs[shift][...].astype(F32)
    both = 2 * p.half - p.rows
    tail = p.per * p.i_main
    for g in range(p.n_group):
        for s in range(p.own):
            rows = []
            for u in range(p.per):
                for skip, half in ((0, hold[g * p.split, s]), (both, hold[g * p.split + 1, s])):
                    rows.append(half[u * p.i_main + min(skip, p.i_main):(u + 1) * p.i_main])
                    rows.append(half[tail + u * p.i_rem + max(skip - p.i_main, 0):tail + (u + 1) * p.i_rem])
            rows = [value for value in rows if value.shape[0]]
            out_ref[g * p.own + s] = jnp.concatenate(rows, axis=0).astype(BF16)


def outer_kernel(p, recv_ref, pair_ref, w_ref, wv_ref, wg_ref, wo_ref, mid_ref, edge_ref, gate_ref,
                 flat, rt, lhs, mid):
    flat[...] = recv_ref[...].reshape(p.n * p.side_rows, LANES).astype(F32)

    def chunk(h, k):
        return jnp.concatenate(
            [flat[pl.ds(h * p.side_rows + k * p.own + s, p.n // p.split, stride=p.split * p.side_rows), :]
             for s in range(p.own)], axis=0)

    hk, ek = p.hk, p.ek
    for u in range(p.per):
        for k in range(p.lk):
            value = chunk(0, ek + u * hk + k) if k < hk else chunk(1, hk + u * ek + k - hk)
            row = (u * p.lk + k) * LANES
            rt[row:row + LANES, :] = jnp.transpose(value)
    right = []
    for first in range(0, p.outer, p.pack):
        right.append(jnp.concatenate(
            [rt[pl.ds(first + d, p.cols, stride=p.outer), :] for d in range(p.pack)], axis=1))
    right = jnp.concatenate(right, axis=0).astype(BF16)
    at = over(lane_iota(p.seq_total), p.outer)
    left = []
    for g in range(p.lk):
        base = chunk(0, g) if g < ek else chunk(1, g - ek)
        turned = [base] + [pltpu.roll(base, t * p.outer, axis=1) for t in range(1, p.pack)]
        for a in range(p.pack):
            left.append(jnp.concatenate(
                [jnp.where(at == d, turned[(d - a) % p.pack], 0.0) for d in range(p.pack)], axis=0).astype(BF16))
    products = dot(right, jnp.concatenate(left, axis=1)) * (1.0 / p.seq_total)
    for i in range(p.rows):
        for g in range(p.outer // p.pack):
            lhs[i * p.cpad:i * p.cpad + p.cols, g * LANES:(g + 1) * LANES] = products[
                g * p.cols:(g + 1) * p.cols, i * LANES:(i + 1) * LANES].astype(BF16)
        if p.cpad > p.cols:
            lhs[i * p.cpad + p.cols:(i + 1) * p.cpad, :] = jnp.zeros((p.cpad - p.cols, lhs.shape[1]), BF16)
    update = dot(lhs[...], w_ref[...])
    for i in range(p.rows):
        fresh = (pair_ref[i].astype(F32) + update[i * p.cpad:i * p.cpad + p.cols]).astype(BF16)
        mid_ref[i] = fresh
        mid[i * p.cols:(i + 1) * p.cols, :] = fresh.astype(F32)
    tail = mid.shape[0] - p.rows * p.cols
    mid[p.rows * p.cols:, :] = jnp.zeros((tail, LANES), F32)
    step = p.q * p.cols
    for k in range(p.ig):
        normed = standardize_features(mid[k * step:k * step + LANES, :]).astype(BF16)
        value = dot_nt(wv_ref[...], normed)
        gate = jax.nn.sigmoid(dot_nt(wg_ref[...], normed))
        edge_ref[:, k * SUBLANES:(k + 1) * SUBLANES, :] = (gate * value).reshape(
            p.n, SUBLANES, LANES).astype(BF16)
        many = min(step, p.rows * p.cols - k * step)
        gate_ref[k * step:k * step + many, :] = jax.nn.sigmoid(dot(normed, wo_ref[...]))[:many]


def triangle_kernel(p, recv_ref, out_ref, flat, ls, rs, os, sb):
    for r in range(p.n_row):
        for c in range(p.n_col):
            flat[c, r * p.edge_rows:(r + 1) * p.edge_rows, :] = recv_ref[r * p.n_col + c].astype(F32)
    lane = lane_iota(p.m)
    part_of = jnp.broadcast_to(lane_iota(1) // p.jslot, (p.m, LANES))
    blocks = p.per * p.ig
    for ch in range(p.ch):
        for c in range(p.n_col):
            for first in range(0, p.n_col, p.q):
                many = min(p.q, p.n_col - first) * blocks * p.q
                start, end = p.j_base(first) + many // SUBLANES * SUBLANES, p.j_base(first) + LANES
                if start < end:
                    rs[ch, c, start:end, :] = jnp.zeros((end - start, LANES), F32)
    for ch in range(p.ch):
        for c in range(p.n_col):
            left = flat[c, pl.ds(ch, p.m, stride=SUBLANES), :]
            right = flat[c, pl.ds(p.ch + ch, p.m, stride=SUBLANES), :]
            both = jnp.concatenate([left, right], axis=0).astype(BF16)
            for a in range(p.q):
                turn = (-a * p.cols) % LANES
                turned = pltpu.roll(both, turn, axis=1).astype(F32) if turn else None
                lt = turned[:p.m] if turn else left
                rt = turned[p.m:] if turn else right
                ls[ch, c, pl.ds(a, p.m, stride=p.q), :] = jnp.where(lane < p.cols, lt, 0.0)
                for first in range(0, p.n_col, p.q):
                    many = min(p.q, p.n_col - first) * blocks
                    rs[ch, c, pl.ds(p.j_base(first) + a, many, stride=p.q), :] = rt[
                        first * blocks:first * blocks + many]
    for ch in range(p.ch):
        lfull = jnp.concatenate([ls[ch, c] for c in range(p.n_col)], axis=1).astype(BF16)
        rfull = jnp.concatenate([rs[ch, c] for c in range(p.n_col)], axis=1).astype(BF16)
        summed = dot_nt(lfull, rfull)
        for b in range(summed.shape[1] // LANES):
            os[ch, b] = summed[:, b * LANES:(b + 1) * LANES]
        rows = [[os[ch, b, pl.ds(a, p.m, stride=p.q), :] for a in range(p.q)]
                for b in range(summed.shape[1] // LANES)]
        for c in range(p.n_col):
            b, part = c // p.q, c % p.q
            packed = None
            for a in range(p.q):
                turn = ((a - part) * p.jslot) % LANES
                piece = pltpu.roll(rows[b][a].astype(BF16), turn, axis=1).astype(F32) if turn else rows[b][a]
                packed = piece if packed is None else jnp.where(part_of == a, piece, packed)
            sb[c, pl.ds(ch, p.m, stride=p.ch), :] = packed
    for r in range(p.n_row):
        for c in range(p.n_col):
            for k in range(p.ig):
                row = (r * p.ig + k) * p.ch
                out_ref[r * p.n_col + c, k] = sb[c, row:row + p.ch, :].astype(BF16)


def final_kernel(p, recv_ref, mid_ref, gate_ref, w_ref, out_hbm, flat, hold, update, out_ref, sems):
    copies = []
    for k in range(p.ig):
        for d in range(p.n):
            flat[k, d * p.ch:(d + 1) * p.ch, :] = recv_ref[d, k].astype(F32)
    for k in range(p.ig):
        normed = jnp.transpose(standardize_features(flat[k], axis=0)).astype(BF16)
        hold[k] = dot(normed, w_ref[...])
        first, last = k * p.q, min((k + 1) * p.q, p.rows)
        for i in range(first, last):
            for u in range(p.per):
                row = (i - first) * p.jslot + u * p.ipad
                update[i * p.cols + u * p.rows:i * p.cols + (u + 1) * p.rows, :] = hold[k, row:row + p.rows, :]
        span = slice(first * p.cols, last * p.cols)
        fresh = mid_ref[first:last].astype(F32) + (gate_ref[span] * update[span]).reshape(
            last - first, p.cols, p.width)
        out_ref[first:last] = fresh.astype(BF16)
        rows = pl.ds(first, last - first)
        copies.append(pltpu.make_async_copy(out_ref.at[rows], out_hbm.at[rows], sems.at[k]))
        copies[-1].start()
    for copy in copies:
        copy.wait()


def fast(p, x, pair, w_in, w_out, w_bias, w_side, w_outer, w_tri, w_last):
    col = lax.axis_index("col")
    n, ch, width = p.n, p.ch, p.width
    sds = jax.ShapeDtypeStruct

    side_w = jnp.concatenate([w_side[:, :p.outer]] * p.pack + [w_side[:, p.outer:]] * p.pack, axis=1)
    by_d = jnp.transpose(w_outer.reshape(p.outer, p.outer, width), (1, 0, 2)).reshape(w_outer.shape)
    blocks = jnp.transpose(w_tri.reshape(width, 5, width), (1, 2, 0)).reshape(5, n, ch, width)
    value_w = jnp.concatenate([blocks[0], blocks[2]], axis=1).reshape(n * 2 * ch, width)
    gate_w = jnp.concatenate([blocks[1], blocks[3]], axis=1).reshape(n * 2 * ch, width)
    own_gate_w = w_tri[:, 4 * width:]

    at = col.reshape(1)
    chunks = (p.own, p.res, p.feat)
    piece, *parts = call(
        functools.partial(bias_kernel, p), (sds((n, p.bias_rows, LANES), BF16),) + (sds(chunks, BF16),) * p.n_col,
        [pltpu.VMEM(pair.shape, BF16), pltpu.VMEM((p.heads, width), BF16), pltpu.VMEM((p.n_group,) + chunks, BF16),
         pltpu.VMEM((p.n_col, p.bias_rows, LANES), BF16), pltpu.SemaphoreType.DMA((3,)),
         pltpu.SemaphoreType.DMA((p.n_row,)), pltpu.SemaphoreType.DMA((p.n_col,))],
        [SMEM] + [HBM] * 3, "bias", limit=64, out_spec=HBM)(at, pair, w_bias.T, x.reshape((p.n_group,) + chunks))
    bias = lax.all_to_all(piece, ALL, 0, 0, tiled=True)

    def ring(parts):
        return [parts[0]] + [
            lax.ppermute(parts[shift], "col", [(c, (c + shift) % p.n_col) for c in range(p.n_col)])
            for shift in range(1, p.n_col)]

    parts = ring(parts)
    mine, every = (p.own, p.queries, p.feat), (p.own, p.total, p.feat)
    q, k, v, gate, rest = call(
        functools.partial(project_kernel, p),
        (sds(mine, BF16), sds(every, BF16), sds(every, BF16), sds(mine, F32), sds(mine, BF16)),
        [pltpu.VMEM((p.n_col, p.own, p.res, p.feat), F32)],
        [SMEM] + [VMEM] * (p.n_col + 1), "project")(at, *parts, w_in)
    emb, sides = call(
        functools.partial(attend_kernel, p),
        (sds((p.n_col, p.own, p.per * p.half, p.feat), BF16), sds((n, p.side_rows, LANES), BF16)),
        [pltpu.VMEM((p.total, p.queries * p.heads), F32), pltpu.VMEM((2, p.own * p.queries, LANES), F32)]
        + [pltpu.VMEM((p.queries // p.pack * p.own, LANES), F32)] * 2
        + [pltpu.VMEM((n, p.side_rows, LANES), F32), pltpu.VMEM((n, p.side_rows, LANES), BF16),
           pltpu.SemaphoreType.DMA((p.n_row,))],
        [SMEM] + [VMEM] * 8, "attend", out_spec=(VMEM, HBM))(at, q, k, v, gate, rest, bias, w_out, side_w)

    sides = lax.all_to_all(sides, ALL, 0, 0, tiled=True)

    parts = ring([lax.dynamic_index_in_dim(emb, lax.rem(col + shift, p.n_col), 0, keepdims=False)
                  for shift in range(p.n_col)])
    home = call(functools.partial(home_kernel, p), sds(x.shape, BF16),
                [pltpu.VMEM((p.n_col, p.own, p.per * p.half, p.feat), F32)],
                [SMEM] + [VMEM] * p.n_col, "home")(at, *parts)

    mid, edges, out_gate = call(
        functools.partial(outer_kernel, p),
        (sds((p.rows, p.cols, width), BF16), sds((n, p.edge_rows, LANES), BF16),
         sds((p.rows * p.cols, width), F32)),
        [pltpu.VMEM((n * p.side_rows, LANES), F32),
         pltpu.VMEM((p.rk * LANES, p.seq_total), F32),
         pltpu.VMEM((p.rows * p.cpad, p.outer * p.outer), BF16),
         pltpu.VMEM(((p.ig - 1) * p.q * p.cols + LANES, LANES), F32)],
        [VMEM] * 6, "outer")(sides, pair, by_d, value_w, gate_w, own_gate_w)

    edges, home = lax.optimization_barrier((edges, home))
    edges = lax.all_to_all(edges, ALL, 0, 0, tiled=True)
    n_lane = p.j_base(p.n_col - 1) // LANES + 1
    back = call(
        functools.partial(triangle_kernel, p), sds((n, p.ig, ch, LANES), BF16),
        [pltpu.VMEM((p.n_col, p.n_row * p.edge_rows, LANES), F32),
         pltpu.VMEM((ch, p.n_col, p.m * p.q, LANES), F32),
         pltpu.VMEM((ch, p.n_col, n_lane * LANES, LANES), F32),
         pltpu.VMEM((ch, n_lane, p.m * p.q, LANES), F32),
         pltpu.VMEM((p.n_col, p.m * ch, LANES), F32)],
        [VMEM], "triangle")(edges)

    back = lax.all_to_all(back, ALL, 0, 0, tiled=True)
    state = call(
        functools.partial(final_kernel, p), sds((p.rows, p.cols, width), BF16),
        [pltpu.VMEM((p.ig, width, LANES), F32), pltpu.VMEM((p.ig, LANES, LANES), F32),
         pltpu.VMEM((p.rows * p.cols, LANES), F32), pltpu.VMEM((p.rows, p.cols, width), BF16),
         pltpu.SemaphoreType.DMA((p.ig,))],
        [VMEM] * 4, "final", out_spec=HBM)(back, mid, out_gate, w_last)
    return home, state


def general(
    stack_embedding,
    pair_representation,
    mixing_entry_coefficients,
    mixing_final_coefficients,
    pair_bias_matrix,
    tensor_side_coefficients,
    outer_output_weight,
    triangle_projection_weight,
    triangle_output_weight,
):
    sequences_per_device, residues_per_device, alignment_channels = stack_embedding.shape
    rows_dev = pair_representation.shape[0]
    pair_width = pair_representation.shape[2]
    number_heads = pair_bias_matrix.shape[1]
    head_channels = alignment_channels // number_heads
    outer_width = tensor_side_coefficients.shape[1] // 2
    row_count = lax.axis_size("row")
    seq_total = sequences_per_device * row_count
    row_index = lax.axis_index("row")
    normalized_input = (
        standardize_features(stack_embedding).astype(jnp.bfloat16).reshape(-1, alignment_channels)
    )
    mapped_lines = jnp.dot(
        normalized_input, mixing_entry_coefficients, preferred_element_type=jnp.float32
    )
    stack_probe_vectors = (
        (mapped_lines[:, :alignment_channels] * head_channels ** (-0.5))
        .astype(jnp.bfloat16)
        .reshape(sequences_per_device, residues_per_device, number_heads, head_channels)
    )
    stack_lookup_vectors = (
        mapped_lines[:, alignment_channels : 2 * alignment_channels]
        .astype(jnp.bfloat16)
        .reshape(sequences_per_device, residues_per_device, alignment_channels)
    )
    stack_content_vectors = (
        mapped_lines[:, 2 * alignment_channels : 3 * alignment_channels]
        .astype(jnp.bfloat16)
        .reshape(sequences_per_device, residues_per_device, alignment_channels)
    )
    sigmoid_factors = jax.nn.sigmoid(mapped_lines[:, 3 * alignment_channels :]).reshape(
        sequences_per_device, residues_per_device, alignment_channels
    )
    pair_normed = standardize_features(pair_representation).astype(jnp.bfloat16)
    bias_local = jnp.einsum(
        "ijc,ch->hij", pair_normed, pair_bias_matrix, preferred_element_type=jnp.float32
    ).astype(jnp.bfloat16)
    bias_all = lax.all_gather(bias_local, "row", axis=1, tiled=True)
    bias_query = lax.all_to_all(bias_all, "col", split_axis=1, concat_axis=2, tiled=True)
    best_score = jnp.full(
        (sequences_per_device, number_heads, residues_per_device), -1e30, jnp.float32
    )
    received_keys = lax.all_gather(stack_lookup_vectors, "col", axis=1, tiled=True)
    received_values = lax.all_gather(stack_content_vectors, "col", axis=1, tiled=True)
    key_count = received_keys.shape[1]
    received_keys = received_keys.reshape(
        sequences_per_device, key_count, number_heads, head_channels
    )
    received_values = received_values.reshape(
        sequences_per_device, key_count, number_heads, head_channels
    )
    bias_piece = bias_query.astype(jnp.float32)
    scores = (
        jnp.einsum(
            "yeca,yica->ycei",
            stack_probe_vectors,
            received_keys,
            preferred_element_type=jnp.float32,
        )
        + bias_piece[None]
    )
    next_best = jnp.maximum(best_score, jnp.max(scores, axis=-1))
    weights = jnp.exp(scores - next_best[..., None])
    next_sum = jnp.sum(weights, axis=-1)
    update = jnp.einsum(
        "shqk,skhd->sqhd",
        weights.astype(jnp.bfloat16),
        received_values,
        preferred_element_type=jnp.float32,
    )
    weighted_mixture = (update / jnp.transpose(next_sum, (0, 2, 1))[..., None]).reshape(
        sequences_per_device, residues_per_device, alignment_channels
    )
    scaled_mixture = (sigmoid_factors * weighted_mixture).astype(jnp.bfloat16)
    stack_increment = jnp.dot(
        scaled_mixture.reshape(-1, alignment_channels),
        mixing_final_coefficients,
        preferred_element_type=jnp.float32,
    ).reshape(sequences_per_device, residues_per_device, alignment_channels)
    stack_embedding_updated = (stack_embedding.astype(jnp.float32) + stack_increment).astype(
        jnp.bfloat16
    )
    tensor_standardized = (
        standardize_features(stack_embedding_updated)
        .astype(jnp.bfloat16)
        .reshape(-1, alignment_channels)
    )
    sides = jnp.dot(
        tensor_standardized, tensor_side_coefficients, preferred_element_type=jnp.float32
    ).astype(jnp.bfloat16)
    sides = sides.reshape(sequences_per_device, residues_per_device, 2 * outer_width)
    left_side = sides[..., :outer_width]
    right_side = sides[..., outer_width:]
    left_wide = lax.all_gather(left_side, "col", axis=1, tiled=True)
    left_every, right_all = (
        lax.all_gather(left_wide, "row", axis=0, tiled=True),
        lax.all_gather(right_side, "row", axis=0, tiled=True),
    )
    left_all = lax.dynamic_slice_in_dim(left_every, row_index * rows_dev, rows_dev, 1)
    products = jnp.einsum("sic,sjd->ijcd", left_all, right_all, preferred_element_type=jnp.float32)
    averaged = (products * (1.0 / seq_total)).astype(jnp.bfloat16)
    outer_update = jnp.dot(
        averaged.reshape(-1, outer_width * outer_width),
        outer_output_weight,
        preferred_element_type=jnp.float32,
    )
    pair_mid = (
        pair_representation.astype(jnp.float32)
        + outer_update.reshape(rows_dev, residues_per_device, pair_width)
    ).astype(jnp.bfloat16)
    tri_normed = standardize_features(pair_mid).astype(jnp.bfloat16).reshape(-1, pair_width)
    tri_parts = jnp.dot(
        tri_normed, triangle_projection_weight, preferred_element_type=jnp.float32
    ).reshape(rows_dev, residues_per_device, 5 * pair_width)
    left_edge = (
        jax.nn.sigmoid(tri_parts[..., pair_width : 2 * pair_width]) * tri_parts[..., :pair_width]
    ).astype(jnp.bfloat16)
    right_edge = (
        jax.nn.sigmoid(tri_parts[..., 3 * pair_width : 4 * pair_width])
        * tri_parts[..., 2 * pair_width : 3 * pair_width]
    ).astype(jnp.bfloat16)
    out_gate = jax.nn.sigmoid(tri_parts[..., 4 * pair_width :])
    right_rows = lax.all_gather(right_edge, "row", axis=0, tiled=True)
    right_query = lax.all_to_all(right_rows, "col", split_axis=0, concat_axis=1, tiled=True)
    arrived = lax.all_gather(left_edge, "col", axis=1, tiled=True)
    summed = jnp.einsum("ikc,jkc->ijc", arrived, right_query, preferred_element_type=jnp.float32)
    tri_ln = standardize_features(summed).astype(jnp.bfloat16)
    tri_update = jnp.dot(
        tri_ln.reshape(-1, pair_width), triangle_output_weight, preferred_element_type=jnp.float32
    ).reshape(rows_dev, residues_per_device, pair_width)
    pair_state_next = (pair_mid.astype(jnp.float32) + out_gate * tri_update).astype(jnp.bfloat16)
    return (stack_embedding_updated, pair_state_next)


def shards(x, pair, w_in, w_out, w_bias, w_side, w_outer, w_tri, w_last):
    p = Plan(lax.axis_size("row"), lax.axis_size("col"), x.shape, pair.shape, w_bias.shape[1],
             w_side.shape[1] // 2, w_last.shape[1])
    path = functools.partial(fast, p) if p.ok else general
    return path(x, pair, w_in, w_out, w_bias, w_side, w_outer, w_tri, w_last)


def solution(mesh):
    return jax.shard_map(
        shards,
        mesh=mesh,
        in_specs=(P("row", "col", None), P("row", "col", None), P(), P(), P(), P(), P(), P(), P()),
        out_specs=(P("row", "col", None), P("row", "col", None)),
        check_vma=False,
    )
```

```python
import functools

import jax
import jax.numpy as jnp
from jax import lax
from jax.experimental import pallas as pl
from jax.experimental.pallas import tpu as pltpu
from jax.sharding import PartitionSpec as P

epsilon = 1e-05
LANES = 128
MOST_VMEM = 67_043_328
SUBLANES = 8
F32 = jnp.float32
BF16 = jnp.bfloat16
ALL = ("row", "col")
NT = (((1,), (1,)), ((), ()))
VMEM = pl.BlockSpec(memory_space=pltpu.VMEM)
SMEM = pl.BlockSpec(memory_space=pltpu.SMEM)
HBM = pl.BlockSpec(memory_space=pltpu.HBM)


def standardize_features(inputs, axis=-1):
    inputs = inputs.astype(jnp.float32)
    center = inputs - jnp.mean(inputs, axis=axis, keepdims=True)
    spread = jnp.mean(center * center, axis=axis, keepdims=True)
    return center * lax.rsqrt(spread + epsilon)


def dot(a, b):
    return jnp.dot(a, b, preferred_element_type=F32)


def dot_nt(a, b):
    return lax.dot_general(a, b, NT, preferred_element_type=F32)


def lane_iota(rows, width=LANES):
    return lax.broadcasted_iota(jnp.int32, (rows, width), 1)


def row_iota(rows, width=LANES):
    return lax.broadcasted_iota(jnp.int32, (rows, width), 0)


def over(index, size):
    return lax.shift_right_logical(index, jnp.int32(size.bit_length() - 1))


def modulo(index, size):
    return lax.bitwise_and(index, jnp.int32(size - 1))


def call(body, out_shape, scratch, in_specs, name, limit=24, out_spec=VMEM, flags=None):
    return pl.pallas_call(
        body,
        out_shape=out_shape,
        in_specs=in_specs,
        out_specs=out_spec if isinstance(out_spec, tuple) else jax.tree.map(lambda _: out_spec, out_shape),
        scratch_shapes=scratch,
        name=name,
        cost_estimate=pl.CostEstimate(flops=400_000_000, bytes_accessed=4_000_000, transcendentals=0),
        compiler_params=pltpu.CompilerParams(vmem_limit_bytes=min(limit * 1024 * 1024, MOST_VMEM), flags=flags),
    )


class Plan:
    def __init__(self, n_row, n_col, x, pair, heads, outer, channels_out):
        self.n_row, self.n_col, self.n = n_row, n_col, n_row * n_col
        self.seqs, self.res, self.feat = x
        self.rows, self.cols, self.width = pair
        self.heads, self.outer = heads, outer
        self.hd = self.feat // heads
        self.total = self.res * n_col
        self.ok = False
        if any(size & (size - 1) for size in (heads, outer, self.hd, n_row, n_col)) or self.hd * 2 > LANES:
            return
        if self.seqs % n_col or self.width != LANES or heads != SUBLANES or self.cols != self.res:
            return
        if self.rows * n_row != self.total or self.feat % LANES:
            return
        self.split = 2
        if n_col % self.split:
            return
        self.n_group = n_col // self.split
        self.own = self.seqs // self.n_group
        self.seq_total = self.own * self.n_group * n_row
        if LANES % outer or outer % (LANES // outer):
            return
        self.pack = LANES // outer
        if self.rows % self.pack or self.cols % self.pack:
            return
        self.half = -(-self.rows // (self.split * self.pack)) * self.pack
        self.late = self.rows - self.half
        self.queries = n_row * self.half
        self.i_main = LANES // heads // 2
        self.i_rem = self.half - self.i_main
        if self.i_main != SUBLANES or 2 * self.i_rem != SUBLANES or self.i_main % self.pack or self.i_rem % self.pack or LANES % (self.i_rem * heads) or self.cols % SUBLANES:
            return
        self.km = self.i_main // self.pack
        self.main, self.rem = self.i_main * heads, self.i_rem * heads
        self.groups = self.cols // SUBLANES
        self.tall = -(-self.groups // 2)
        self.fold = LANES // self.rem
        if n_row % 2 or n_row % self.fold or n_row * self.main % (2 * LANES) or n_row * self.rem % (2 * LANES):
            return
        self.main_at = [(g % self.tall, g // self.tall * self.main) for g in range(self.groups)]
        spare = [(self.tall, f * self.rem) for f in range(self.fold)]
        if self.groups % 2:
            spare += [(self.tall - 1, self.main + f * self.rem) for f in range(self.main // self.rem)]
        if len(spare) < self.groups:
            return
        self.rem_at = spare[:self.groups]
        self.bias_rows = (self.tall + 1) * SUBLANES
        self.per = n_row // n_col
        if n_row % n_col or self.per * self.rows != self.cols:
            return
        self.lk, self.rk = self.rows // self.pack, self.cols // self.pack
        self.hk = self.half // self.pack
        self.ek = self.lk - self.hk
        chunks = max(self.ek + self.per * self.hk, self.hk + self.per * self.ek)
        self.side_rows = -(-chunks * self.own // 16) * 16
        self.cpad = -(-self.cols // 16) * 16
        if self.width % self.n:
            return
        self.ch = self.width // self.n
        if 2 * self.ch != SUBLANES:
            return
        self.q = LANES // self.cols
        self.ig = -(-self.rows // self.q)
        self.ipad = self.ig * self.q
        self.jslot = self.per * self.ipad
        if self.q * self.jslot > LANES:
            return
        self.m = n_row * self.ig
        self.edge_rows = self.ig * SUBLANES
        self.ok = True

    def j_base(self, c):
        return (c // self.q) * LANES + (c % self.q) * self.jslot


def bias_kernel(p, col_ref, pair_hbm, w_hbm, x_hbm, *refs):
    out_hbm, *part_hbm = refs[:p.n_col + 1]
    pair_ref, w_ref, x_ref, piece_ref, sems, out_sems, part_sems = refs[p.n_col + 1:]
    copies = [pltpu.make_async_copy(pair_hbm, pair_ref, sems.at[0]), pltpu.make_async_copy(w_hbm, w_ref, sems.at[1]),
              pltpu.make_async_copy(x_hbm, x_ref, sems.at[2])]
    for copy in copies:
        copy.start()
    for copy in copies:
        copy.wait()
    parts = []
    for shift in range(p.n_col):
        group = over(lax.rem(col_ref[0] + shift, p.n_col), p.split)
        parts.append(pltpu.make_async_copy(x_ref.at[group], part_hbm[shift], part_sems.at[shift]))
        parts[-1].start()
    normed = standardize_features(pair_ref[...]).reshape(p.rows * p.cols, p.width)
    heads = p.heads

    def tile(many):
        spread = modulo(over(lane_iota(heads), many), heads) == row_iota(heads)
        return lax.dot_general(w_ref[...], jnp.where(spread, 1.0, 0.0).astype(BF16), (((0,), (0,)), ((), ())),
                               preferred_element_type=F32)

    main_w, rem_w = tile(p.i_main), tile(p.i_rem)
    main_slot, rem_slot = modulo(lane_iota(p.width), p.i_main), modulo(lane_iota(p.width), p.i_rem)
    at = lane_iota(SUBLANES)
    for h in range(p.split):
        main = jnp.zeros((p.cols, LANES), F32)
        rem = jnp.zeros((p.cols, LANES), F32)
        for m in range(p.half):
            i = h * p.late + m
            block = normed[i * p.cols:(i + 1) * p.cols].astype(BF16)
            if m < p.i_main:
                main += dot(block, jnp.where(main_slot == m, main_w, 0.0).astype(BF16))
            else:
                rem += dot(block, jnp.where(rem_slot == m - p.i_main, rem_w, 0.0).astype(BF16))
        blocks = [jnp.zeros((SUBLANES, LANES), F32) for _ in range(p.tall + 1)]
        for value, places, wide in ((main, p.main_at, p.main), (rem, p.rem_at, p.rem)):
            for g, (b, lane) in enumerate(places):
                here = (at >= lane) & (at < lane + wide)
                blocks[b] = jnp.where(here, value[g * SUBLANES:(g + 1) * SUBLANES], blocks[b])
        piece = jnp.concatenate(blocks, axis=0).astype(BF16)
        for c in range(h, p.n_col, p.split):
            piece_ref[c] = piece
    pieces = [pltpu.make_async_copy(piece_ref, out_hbm.at[pl.ds(r * p.n_col, p.n_col)], out_sems.at[r])
              for r in range(p.n_row)]
    for copy in pieces:
        copy.start()
    for copy in pieces + parts:
        copy.wait()


def pick_half(p, second, rows):
    main, rest = [], []
    for r in range(p.n_row):
        a, b = r * p.rows, r * p.rows + p.late
        main.append(jnp.where(second, rows[b:b + p.i_main], rows[a:a + p.i_main]))
        rest.append(jnp.where(second, rows[b + p.i_main:b + p.half], rows[a + p.i_main:a + p.half]))
    return jnp.concatenate(main + rest, axis=0)


def project_kernel(p, col_ref, *refs):
    x_refs = refs[:p.n_col]
    w_ref, q_ref, k_ref, v_ref, gate_ref, x_out, hold = refs[p.n_col:]
    me = col_ref[0]
    second = lax.rem(me, p.split) == 1
    for shift in range(p.n_col):
        hold[lax.rem(me + (p.n_col - shift), p.n_col)] = x_refs[shift][...].astype(F32)
    f = p.feat
    for s in range(p.own):
        x = jnp.concatenate([hold[c, s] for c in range(p.n_col)], axis=0)
        normed = standardize_features(x)
        x_out[s] = pick_half(p, second, x).astype(BF16)
        lines = dot(normed.astype(BF16), w_ref[:, f:3 * f])
        k_ref[s] = lines[:, :f].astype(BF16)
        v_ref[s] = lines[:, f:].astype(BF16)
        normed = pick_half(p, second, normed).astype(BF16)
        gate_ref[s] = jax.nn.sigmoid(dot(normed, w_ref[:, 3 * f:]))
        q_ref[s] = (dot(normed, w_ref[:, :f]) * p.hd ** (-0.5)).astype(BF16)


def attend_kernel(p, col_ref, q_ref, k_ref, v_ref, gate_ref, x_ref, bias_ref, wf_ref, ws_ref,
                  emb_ref, side_hbm, bias, four, lint, rint, send, side_ref, sems):
    h, t, f, m = p.heads, p.queries, p.feat, p.half
    at = lane_iota(SUBLANES)
    for first, places, wide in ((0, p.main_at, p.main), (p.n_row * p.main, p.rem_at, p.rem)):
        fold = LANES // wide
        slot = over(at, wide)
        for c in range(p.n_col):
            for b in range(p.n_row // fold):
                for g, (block, lane) in enumerate(places):
                    built = None
                    for u in range(fold):
                        piece = bias_ref[(b * fold + u) * p.n_col + c,
                                         block * SUBLANES:(block + 1) * SUBLANES].astype(F32)
                        turn = (u * wide - lane) % LANES
                        piece = pltpu.roll(piece, turn, axis=1) if turn else piece
                        built = piece if u == 0 else jnp.where(slot == u, piece, built)
                    row = c * p.cols + g * SUBLANES
                    bias[row:row + SUBLANES, first + b * LANES:first + (b + 1) * LANES] = built
    step = 2 * LANES
    lane, row = lane_iota(f, step), row_iota(f, step)
    blocks = []
    for many, wide, count in ((p.i_main, p.main, p.n_row * p.main // step), (p.i_rem, p.rem, p.n_row * p.rem // step)):
        own_head = over(row, p.hd) == modulo(over(lane, many), h)
        at = lane_iota(step // h, step)
        pick = jnp.where(row_iota(step // h, step) == over(at, wide) * many + modulo(at, many), 1.0, 0.0).astype(BF16)
        blocks += [(own_head, pick)] * count
    fit = LANES // p.hd
    head_lane, low = over(lane_iota(SUBLANES), p.hd), row_iota(SUBLANES) >= p.i_rem
    own_lane = [jnp.where(head_lane == g % fit, 1.0, 0.0) for g in range(h)]
    own_pair = [jnp.where(low, own_lane[g + 1], own_lane[g]) for g in range(0, h, 2)]
    empty = jnp.zeros((SUBLANES, LANES), F32)

    def only(rows, mask, tile):
        return jnp.concatenate([rows[:, n * LANES:(n + 1) * LANES] * mask if n == tile else empty
                                for n in range(f // LANES)], axis=1)

    new, tall, together = [], step // SUBLANES, 4
    for first in range(0, p.own, together):
        jobs = []
        for s in range(first, min(first + together, p.own)):
            q = q_ref[s].astype(F32)
            spread = []
            for r in range(p.n_row):
                rows = q[r * p.i_main:(r + 1) * p.i_main]
                spread += [only(rows, mask, g // fit) for g, mask in enumerate(own_lane)]
            for r in range(p.n_row):
                start = p.n_row * p.i_main + r * p.i_rem
                rows = jnp.concatenate([q[start:start + p.i_rem]] * 2, axis=0)
                spread += [only(rows, mask, 2 * g // fit) for g, mask in enumerate(own_pair)]
            for n in range(len(blocks)):
                jobs.append((s, n, jnp.concatenate(spread[n * tall:(n + 1) * tall], axis=0).astype(BF16)))
        v_t = {s: jnp.transpose(v_ref[s].astype(F32)).astype(BF16) for s in range(first, first + together)
               if s < p.own}
        scores = [dot_nt(k_ref[s], rows) + bias[:, n * step:(n + 1) * step] for s, n, rows in jobs]
        weights = [jnp.exp(score - jnp.max(score, axis=0, keepdims=True)) for score in scores]
        share = [1.0 / jnp.sum(weight, axis=0, keepdims=True) for weight in weights]
        mixed = [dot(v_t[s], weight.astype(BF16)) for (s, _, _), weight in zip(jobs, weights)]
        mixed = [jnp.where(blocks[n][0], value * part, 0.0).astype(BF16)
                 for (_, n, _), value, part in zip(jobs, mixed, share)]
        attended = [dot_nt(blocks[n][1], value) for (_, n, _), value in zip(jobs, mixed)]
        for i, at in enumerate(range(0, len(jobs), len(blocks))):
            rows = jnp.concatenate(attended[at:at + len(blocks)], axis=0)
            new.append((gate_ref[first + i] * rows).astype(BF16))
    new = dot(jnp.concatenate(new, axis=0), wf_ref[...])
    new = (x_ref[...].astype(F32).reshape(p.own * t, f) + new).astype(BF16).astype(F32)
    a, b = p.per * p.i_main, p.per * p.i_rem
    for s in range(p.own):
        for c in range(p.n_col):
            row, tail = s * t + c * a, s * t + p.n_row * p.i_main + c * b
            emb_ref[c, s] = jnp.concatenate([new[row:row + a], new[tail:tail + b]], axis=0).astype(BF16)
    sides = dot(standardize_features(new).astype(BF16), ws_ref[...])
    four[0] = sides[:, :LANES]
    four[1] = sides[:, LANES:]
    n4 = t // p.pack
    lane = over(lane_iota(n4), p.outer)
    for s in range(p.own):
        for side, woven in enumerate((lint, rint)):
            packed = four[side, pl.ds(s * t, n4, stride=p.pack), :]
            for a in range(1, p.pack):
                packed = jnp.where(lane == a, four[side, pl.ds(s * t + a, n4, stride=p.pack), :], packed)
            woven[pl.ds(s, n4, stride=p.own), :] = packed
    o = p.own

    def place(r, k):
        return (r * p.km + k if k < p.km else p.n_row * p.km + r * (p.hk - p.km) + k - p.km) * o

    def fill(left, right):
        for r in range(p.n_row):
            for c in range(p.n_col):
                d, row = r * p.n_col + c, 0
                spans = [(lint, place(r, k)) for k in left]
                spans += [(rint, place(c * p.per + u, k)) for u in range(p.per) for k in right]
                for source, start in spans:
                    send[d, row:row + o] = source[start:start + o]
                    row += o
                if row < p.side_rows:
                    send[d, row:p.side_rows] = jnp.zeros((p.side_rows - row, LANES), F32)
            block = slice(r * p.n_col, (r + 1) * p.n_col)
            side_ref[block] = send[block].astype(BF16)
            leave(r).start()

    def leave(r):
        block = pl.ds(r * p.n_col, p.n_col)
        return pltpu.make_async_copy(side_ref.at[block], side_hbm.at[block], sems.at[r])

    second = lax.rem(col_ref[0], p.split) == 1

    @pl.when(jnp.logical_not(second))
    def _():
        fill(range(p.ek), range(p.hk))

    @pl.when(second)
    def _():
        fill(range(p.hk), range(p.hk - p.ek, p.hk))

    for r in range(p.n_row):
        leave(r).wait()


def home_kernel(p, col_ref, *refs):
    part_refs = refs[:p.n_col]
    out_ref, hold = refs[p.n_col:]
    me = col_ref[0]
    for shift in range(p.n_col):
        hold[lax.rem(me + (p.n_col - shift), p.n_col)] = part_refs[shift][...].astype(F32)
    both = 2 * p.half - p.rows
    tail = p.per * p.i_main
    for g in range(p.n_group):
        for s in range(p.own):
            rows = []
            for u in range(p.per):
                for skip, half in ((0, hold[g * p.split, s]), (both, hold[g * p.split + 1, s])):
                    rows.append(half[u * p.i_main + min(skip, p.i_main):(u + 1) * p.i_main])
                    rows.append(half[tail + u * p.i_rem + max(skip - p.i_main, 0):tail + (u + 1) * p.i_rem])
            rows = [value for value in rows if value.shape[0]]
            out_ref[g * p.own + s] = jnp.concatenate(rows, axis=0).astype(BF16)


def outer_kernel(p, recv_ref, pair_ref, w_ref, wv_ref, wg_ref, wo_ref, mid_ref, edge_ref, gate_ref,
                 flat, rt, lhs, mid):
    flat[...] = recv_ref[...].reshape(p.n * p.side_rows, LANES).astype(F32)

    def chunk(h, k):
        return jnp.concatenate(
            [flat[pl.ds(h * p.side_rows + k * p.own + s, p.n // p.split, stride=p.split * p.side_rows), :]
             for s in range(p.own)], axis=0)

    hk, ek = p.hk, p.ek
    for u in range(p.per):
        for k in range(p.lk):
            value = chunk(0, ek + u * hk + k) if k < hk else chunk(1, hk + u * ek + k - hk)
            row = (u * p.lk + k) * LANES
            rt[row:row + LANES, :] = jnp.transpose(value)
    right = []
    for first in range(0, p.outer, p.pack):
        right.append(jnp.concatenate(
            [rt[pl.ds(first + d, p.cols, stride=p.outer), :] for d in range(p.pack)], axis=1))
    right = jnp.concatenate(right, axis=0).astype(BF16)
    at = over(lane_iota(p.seq_total), p.outer)
    left = []
    for g in range(p.lk):
        base = chunk(0, g) if g < ek else chunk(1, g - ek)
        turned = [base] + [pltpu.roll(base, t * p.outer, axis=1) for t in range(1, p.pack)]
        for a in range(p.pack):
            left.append(jnp.concatenate(
                [jnp.where(at == d, turned[(d - a) % p.pack], 0.0) for d in range(p.pack)], axis=0).astype(BF16))
    products = dot(right, jnp.concatenate(left, axis=1)) * (1.0 / p.seq_total)
    for i in range(p.rows):
        for g in range(p.outer // p.pack):
            lhs[i * p.cpad:i * p.cpad + p.cols, g * LANES:(g + 1) * LANES] = products[
                g * p.cols:(g + 1) * p.cols, i * LANES:(i + 1) * LANES].astype(BF16)
        if p.cpad > p.cols:
            lhs[i * p.cpad + p.cols:(i + 1) * p.cpad, :] = jnp.zeros((p.cpad - p.cols, lhs.shape[1]), BF16)
    update = dot(lhs[...], w_ref[...])
    for i in range(p.rows):
        fresh = (pair_ref[i].astype(F32) + update[i * p.cpad:i * p.cpad + p.cols]).astype(BF16)
        mid_ref[i] = fresh
        mid[i * p.cols:(i + 1) * p.cols, :] = fresh.astype(F32)
    tail = mid.shape[0] - p.rows * p.cols
    mid[p.rows * p.cols:, :] = jnp.zeros((tail, LANES), F32)
    step = p.q * p.cols
    for k in range(p.ig):
        normed = standardize_features(mid[k * step:k * step + LANES, :]).astype(BF16)
        value = dot_nt(wv_ref[...], normed)
        gate = jax.nn.sigmoid(dot_nt(wg_ref[...], normed))
        edge_ref[:, k * SUBLANES:(k + 1) * SUBLANES, :] = (gate * value).reshape(
            p.n, SUBLANES, LANES).astype(BF16)
        many = min(step, p.rows * p.cols - k * step)
        gate_ref[k * step:k * step + many, :] = jax.nn.sigmoid(dot(normed, wo_ref[...]))[:many]


def triangle_kernel(p, recv_ref, out_ref, flat, ls, rs, os, sb):
    for r in range(p.n_row):
        for c in range(p.n_col):
            flat[c, r * p.edge_rows:(r + 1) * p.edge_rows, :] = recv_ref[r * p.n_col + c].astype(F32)
    lane = lane_iota(p.m)
    part_of = jnp.broadcast_to(lane_iota(1) // p.jslot, (p.m, LANES))
    blocks = p.per * p.ig
    for ch in range(p.ch):
        for c in range(p.n_col):
            for first in range(0, p.n_col, p.q):
                many = min(p.q, p.n_col - first) * blocks * p.q
                start, end = p.j_base(first) + many // SUBLANES * SUBLANES, p.j_base(first) + LANES
                if start < end:
                    rs[ch, c, start:end, :] = jnp.zeros((end - start, LANES), F32)
    for ch in range(p.ch):
        for c in range(p.n_col):
            left = flat[c, pl.ds(ch, p.m, stride=SUBLANES), :]
            right = flat[c, pl.ds(p.ch + ch, p.m, stride=SUBLANES), :]
            both = jnp.concatenate([left, right], axis=0).astype(BF16)
            for a in range(p.q):
                turn = (-a * p.cols) % LANES
                turned = pltpu.roll(both, turn, axis=1).astype(F32) if turn else None
                lt = turned[:p.m] if turn else left
                rt = turned[p.m:] if turn else right
                ls[ch, c, pl.ds(a, p.m, stride=p.q), :] = jnp.where(lane < p.cols, lt, 0.0)
                for first in range(0, p.n_col, p.q):
                    many = min(p.q, p.n_col - first) * blocks
                    rs[ch, c, pl.ds(p.j_base(first) + a, many, stride=p.q), :] = rt[
                        first * blocks:first * blocks + many]
    for ch in range(p.ch):
        lfull = jnp.concatenate([ls[ch, c] for c in range(p.n_col)], axis=1).astype(BF16)
        rfull = jnp.concatenate([rs[ch, c] for c in range(p.n_col)], axis=1).astype(BF16)
        summed = dot_nt(lfull, rfull)
        for b in range(summed.shape[1] // LANES):
            os[ch, b] = summed[:, b * LANES:(b + 1) * LANES]
        rows = [[os[ch, b, pl.ds(a, p.m, stride=p.q), :] for a in range(p.q)]
                for b in range(summed.shape[1] // LANES)]
        for c in range(p.n_col):
            b, part = c // p.q, c % p.q
            packed = None
            for a in range(p.q):
                turn = ((a - part) * p.jslot) % LANES
                piece = pltpu.roll(rows[b][a].astype(BF16), turn, axis=1).astype(F32) if turn else rows[b][a]
                packed = piece if packed is None else jnp.where(part_of == a, piece, packed)
            sb[c, pl.ds(ch, p.m, stride=p.ch), :] = packed
    for r in range(p.n_row):
        for c in range(p.n_col):
            for k in range(p.ig):
                row = (r * p.ig + k) * p.ch
                out_ref[r * p.n_col + c, k] = sb[c, row:row + p.ch, :].astype(BF16)


def final_kernel(p, recv_ref, mid_ref, gate_ref, w_ref, out_hbm, flat, hold, update, out_ref, sems):
    copies = []
    for k in range(p.ig):
        for d in range(p.n):
            flat[k, d * p.ch:(d + 1) * p.ch, :] = recv_ref[d, k].astype(F32)
    for k in range(p.ig):
        normed = jnp.transpose(standardize_features(flat[k], axis=0)).astype(BF16)
        hold[k] = dot(normed, w_ref[...])
        first, last = k * p.q, min((k + 1) * p.q, p.rows)
        for i in range(first, last):
            for u in range(p.per):
                row = (i - first) * p.jslot + u * p.ipad
                update[i * p.cols + u * p.rows:i * p.cols + (u + 1) * p.rows, :] = hold[k, row:row + p.rows, :]
        span = slice(first * p.cols, last * p.cols)
        fresh = mid_ref[first:last].astype(F32) + (gate_ref[span] * update[span]).reshape(
            last - first, p.cols, p.width)
        out_ref[first:last] = fresh.astype(BF16)
        rows = pl.ds(first, last - first)
        copies.append(pltpu.make_async_copy(out_ref.at[rows], out_hbm.at[rows], sems.at[k]))
        copies[-1].start()
    for copy in copies:
        copy.wait()


def fast(p, x, pair, w_in, w_out, w_bias, w_side, w_outer, w_tri, w_last):
    col = lax.axis_index("col")
    n, ch, width = p.n, p.ch, p.width
    sds = jax.ShapeDtypeStruct

    side_w = jnp.concatenate([w_side[:, :p.outer]] * p.pack + [w_side[:, p.outer:]] * p.pack, axis=1)
    by_d = jnp.transpose(w_outer.reshape(p.outer, p.outer, width), (1, 0, 2)).reshape(w_outer.shape)
    blocks = jnp.transpose(w_tri.reshape(width, 5, width), (1, 2, 0)).reshape(5, n, ch, width)
    value_w = jnp.concatenate([blocks[0], blocks[2]], axis=1).reshape(n * 2 * ch, width)
    gate_w = jnp.concatenate([blocks[1], blocks[3]], axis=1).reshape(n * 2 * ch, width)
    own_gate_w = w_tri[:, 4 * width:]

    at = col.reshape(1)
    chunks = (p.own, p.res, p.feat)
    piece, *parts = call(
        functools.partial(bias_kernel, p), (sds((n, p.bias_rows, LANES), BF16),) + (sds(chunks, BF16),) * p.n_col,
        [pltpu.VMEM(pair.shape, BF16), pltpu.VMEM((p.heads, width), BF16), pltpu.VMEM((p.n_group,) + chunks, BF16),
         pltpu.VMEM((p.n_col, p.bias_rows, LANES), BF16), pltpu.SemaphoreType.DMA((3,)),
         pltpu.SemaphoreType.DMA((p.n_row,)), pltpu.SemaphoreType.DMA((p.n_col,))],
        [SMEM] + [HBM] * 3, "bias", limit=64, out_spec=HBM)(at, pair, w_bias.T, x.reshape((p.n_group,) + chunks))
    bias = lax.all_to_all(piece, ALL, 0, 0, tiled=True)

    def ring(parts):
        return [parts[0]] + [
            lax.ppermute(parts[shift], "col", [(c, (c + shift) % p.n_col) for c in range(p.n_col)])
            for shift in range(1, p.n_col)]

    parts = ring(parts)
    mine, every = (p.own, p.queries, p.feat), (p.own, p.total, p.feat)
    q, k, v, gate, rest = call(
        functools.partial(project_kernel, p),
        (sds(mine, BF16), sds(every, BF16), sds(every, BF16), sds(mine, F32), sds(mine, BF16)),
        [pltpu.VMEM((p.n_col, p.own, p.res, p.feat), F32)],
        [SMEM] + [VMEM] * (p.n_col + 1), "project")(at, *parts, w_in)
    emb, sides = call(
        functools.partial(attend_kernel, p),
        (sds((p.n_col, p.own, p.per * p.half, p.feat), BF16), sds((n, p.side_rows, LANES), BF16)),
        [pltpu.VMEM((p.total, p.queries * p.heads), F32), pltpu.VMEM((2, p.own * p.queries, LANES), F32)]
        + [pltpu.VMEM((p.queries // p.pack * p.own, LANES), F32)] * 2
        + [pltpu.VMEM((n, p.side_rows, LANES), F32), pltpu.VMEM((n, p.side_rows, LANES), BF16),
           pltpu.SemaphoreType.DMA((p.n_row,))],
        [SMEM] + [VMEM] * 8, "attend", out_spec=(VMEM, HBM))(at, q, k, v, gate, rest, bias, w_out, side_w)

    sides = lax.all_to_all(sides, ALL, 0, 0, tiled=True)

    parts = ring([lax.dynamic_index_in_dim(emb, lax.rem(col + shift, p.n_col), 0, keepdims=False)
                  for shift in range(p.n_col)])
    home = call(functools.partial(home_kernel, p), sds(x.shape, BF16),
                [pltpu.VMEM((p.n_col, p.own, p.per * p.half, p.feat), F32)],
                [SMEM] + [VMEM] * p.n_col, "home")(at, *parts)

    mid, edges, out_gate = call(
        functools.partial(outer_kernel, p),
        (sds((p.rows, p.cols, width), BF16), sds((n, p.edge_rows, LANES), BF16),
         sds((p.rows * p.cols, width), F32)),
        [pltpu.VMEM((n * p.side_rows, LANES), F32),
         pltpu.VMEM((p.rk * LANES, p.seq_total), F32),
         pltpu.VMEM((p.rows * p.cpad, p.outer * p.outer), BF16),
         pltpu.VMEM(((p.ig - 1) * p.q * p.cols + LANES, LANES), F32)],
        [VMEM] * 6, "outer")(sides, pair, by_d, value_w, gate_w, own_gate_w)

    edges, home = lax.optimization_barrier((edges, home))
    edges = lax.all_to_all(edges, ALL, 0, 0, tiled=True)
    n_lane = p.j_base(p.n_col - 1) // LANES + 1
    back = call(
        functools.partial(triangle_kernel, p), sds((n, p.ig, ch, LANES), BF16),
        [pltpu.VMEM((p.n_col, p.n_row * p.edge_rows, LANES), F32),
         pltpu.VMEM((ch, p.n_col, p.m * p.q, LANES), F32),
         pltpu.VMEM((ch, p.n_col, n_lane * LANES, LANES), F32),
         pltpu.VMEM((ch, n_lane, p.m * p.q, LANES), F32),
         pltpu.VMEM((p.n_col, p.m * ch, LANES), F32)],
        [VMEM], "triangle")(edges)

    back = lax.all_to_all(back, ALL, 0, 0, tiled=True)
    state = call(
        functools.partial(final_kernel, p), sds((p.rows, p.cols, width), BF16),
        [pltpu.VMEM((p.ig, width, LANES), F32), pltpu.VMEM((p.ig, LANES, LANES), F32),
         pltpu.VMEM((p.rows * p.cols, LANES), F32), pltpu.VMEM((p.rows, p.cols, width), BF16),
         pltpu.SemaphoreType.DMA((p.ig,))],
        [VMEM] * 4, "final", out_spec=HBM)(back, mid, out_gate, w_last)
    return home, state


def general(
    stack_embedding,
    pair_representation,
    mixing_entry_coefficients,
    mixing_final_coefficients,
    pair_bias_matrix,
    tensor_side_coefficients,
    outer_output_weight,
    triangle_projection_weight,
    triangle_output_weight,
):
    sequences_per_device, residues_per_device, alignment_channels = stack_embedding.shape
    rows_dev = pair_representation.shape[0]
    pair_width = pair_representation.shape[2]
    number_heads = pair_bias_matrix.shape[1]
    head_channels = alignment_channels // number_heads
    outer_width = tensor_side_coefficients.shape[1] // 2
    row_count = lax.axis_size("row")
    seq_total = sequences_per_device * row_count
    row_index = lax.axis_index("row")
    normalized_input = (
        standardize_features(stack_embedding).astype(jnp.bfloat16).reshape(-1, alignment_channels)
    )
    mapped_lines = jnp.dot(
        normalized_input, mixing_entry_coefficients, preferred_element_type=jnp.float32
    )
    stack_probe_vectors = (
        (mapped_lines[:, :alignment_channels] * head_channels ** (-0.5))
        .astype(jnp.bfloat16)
        .reshape(sequences_per_device, residues_per_device, number_heads, head_channels)
    )
    stack_lookup_vectors = (
        mapped_lines[:, alignment_channels : 2 * alignment_channels]
        .astype(jnp.bfloat16)
        .reshape(sequences_per_device, residues_per_device, alignment_channels)
    )
    stack_content_vectors = (
        mapped_lines[:, 2 * alignment_channels : 3 * alignment_channels]
        .astype(jnp.bfloat16)
        .reshape(sequences_per_device, residues_per_device, alignment_channels)
    )
    sigmoid_factors = jax.nn.sigmoid(mapped_lines[:, 3 * alignment_channels :]).reshape(
        sequences_per_device, residues_per_device, alignment_channels
    )
    pair_normed = standardize_features(pair_representation).astype(jnp.bfloat16)
    bias_local = jnp.einsum(
        "ijc,ch->hij", pair_normed, pair_bias_matrix, preferred_element_type=jnp.float32
    ).astype(jnp.bfloat16)
    bias_all = lax.all_gather(bias_local, "row", axis=1, tiled=True)
    bias_query = lax.all_to_all(bias_all, "col", split_axis=1, concat_axis=2, tiled=True)
    best_score = jnp.full(
        (sequences_per_device, number_heads, residues_per_device), -1e30, jnp.float32
    )
    received_keys = lax.all_gather(stack_lookup_vectors, "col", axis=1, tiled=True)
    received_values = lax.all_gather(stack_content_vectors, "col", axis=1, tiled=True)
    key_count = received_keys.shape[1]
    received_keys = received_keys.reshape(
        sequences_per_device, key_count, number_heads, head_channels
    )
    received_values = received_values.reshape(
        sequences_per_device, key_count, number_heads, head_channels
    )
    bias_piece = bias_query.astype(jnp.float32)
    scores = (
        jnp.einsum(
            "yeca,yica->ycei",
            stack_probe_vectors,
            received_keys,
            preferred_element_type=jnp.float32,
        )
        + bias_piece[None]
    )
    next_best = jnp.maximum(best_score, jnp.max(scores, axis=-1))
    weights = jnp.exp(scores - next_best[..., None])
    next_sum = jnp.sum(weights, axis=-1)
    update = jnp.einsum(
        "shqk,skhd->sqhd",
        weights.astype(jnp.bfloat16),
        received_values,
        preferred_element_type=jnp.float32,
    )
    weighted_mixture = (update / jnp.transpose(next_sum, (0, 2, 1))[..., None]).reshape(
        sequences_per_device, residues_per_device, alignment_channels
    )
    scaled_mixture = (sigmoid_factors * weighted_mixture).astype(jnp.bfloat16)
    stack_increment = jnp.dot(
        scaled_mixture.reshape(-1, alignment_channels),
        mixing_final_coefficients,
        preferred_element_type=jnp.float32,
    ).reshape(sequences_per_device, residues_per_device, alignment_channels)
    stack_embedding_updated = (stack_embedding.astype(jnp.float32) + stack_increment).astype(
        jnp.bfloat16
    )
    tensor_standardized = (
        standardize_features(stack_embedding_updated)
        .astype(jnp.bfloat16)
        .reshape(-1, alignment_channels)
    )
    sides = jnp.dot(
        tensor_standardized, tensor_side_coefficients, preferred_element_type=jnp.float32
    ).astype(jnp.bfloat16)
    sides = sides.reshape(sequences_per_device, residues_per_device, 2 * outer_width)
    left_side = sides[..., :outer_width]
    right_side = sides[..., outer_width:]
    left_wide = lax.all_gather(left_side, "col", axis=1, tiled=True)
    left_every, right_all = (
        lax.all_gather(left_wide, "row", axis=0, tiled=True),
        lax.all_gather(right_side, "row", axis=0, tiled=True),
    )
    left_all = lax.dynamic_slice_in_dim(left_every, row_index * rows_dev, rows_dev, 1)
    products = jnp.einsum("sic,sjd->ijcd", left_all, right_all, preferred_element_type=jnp.float32)
    averaged = (products * (1.0 / seq_total)).astype(jnp.bfloat16)
    outer_update = jnp.dot(
        averaged.reshape(-1, outer_width * outer_width),
        outer_output_weight,
        preferred_element_type=jnp.float32,
    )
    pair_mid = (
        pair_representation.astype(jnp.float32)
        + outer_update.reshape(rows_dev, residues_per_device, pair_width)
    ).astype(jnp.bfloat16)
    tri_normed = standardize_features(pair_mid).astype(jnp.bfloat16).reshape(-1, pair_width)
    tri_parts = jnp.dot(
        tri_normed, triangle_projection_weight, preferred_element_type=jnp.float32
    ).reshape(rows_dev, residues_per_device, 5 * pair_width)
    left_edge = (
        jax.nn.sigmoid(tri_parts[..., pair_width : 2 * pair_width]) * tri_parts[..., :pair_width]
    ).astype(jnp.bfloat16)
    right_edge = (
        jax.nn.sigmoid(tri_parts[..., 3 * pair_width : 4 * pair_width])
        * tri_parts[..., 2 * pair_width : 3 * pair_width]
    ).astype(jnp.bfloat16)
    out_gate = jax.nn.sigmoid(tri_parts[..., 4 * pair_width :])
    right_rows = lax.all_gather(right_edge, "row", axis=0, tiled=True)
    right_query = lax.all_to_all(right_rows, "col", split_axis=0, concat_axis=1, tiled=True)
    arrived = lax.all_gather(left_edge, "col", axis=1, tiled=True)
    summed = jnp.einsum("ikc,jkc->ijc", arrived, right_query, preferred_element_type=jnp.float32)
    tri_ln = standardize_features(summed).astype(jnp.bfloat16)
    tri_update = jnp.dot(
        tri_ln.reshape(-1, pair_width), triangle_output_weight, preferred_element_type=jnp.float32
    ).reshape(rows_dev, residues_per_device, pair_width)
    pair_state_next = (pair_mid.astype(jnp.float32) + out_gate * tri_update).astype(jnp.bfloat16)
    return (stack_embedding_updated, pair_state_next)


def shards(x, pair, w_in, w_out, w_bias, w_side, w_outer, w_tri, w_last):
    p = Plan(lax.axis_size("row"), lax.axis_size("col"), x.shape, pair.shape, w_bias.shape[1],
             w_side.shape[1] // 2, w_last.shape[1])
    path = functools.partial(fast, p) if p.ok else general
    return path(x, pair, w_in, w_out, w_bias, w_side, w_outer, w_tri, w_last)


def solution(mesh):
    return jax.shard_map(
        shards,
        mesh=mesh,
        in_specs=(P("row", "col", None), P("row", "col", None), P(), P(), P(), P(), P(), P(), P()),
        out_specs=(P("row", "col", None), P("row", "col", None)),
        check_vma=False,
    )
```
